32 devices in a mesh: shard: 4 (over y, x), seq: 8 (over z, core).
Axes of the slice: x: 2, y: 2, z: 4, core: 2. Of those that a mesh axis runs over, the one named last changes fastest.
Arguments:
- block_in: bfloat16 [4, 1024, 1024], P('shard', 'seq'), may hold values from -6 to 6
- doc_lengths: int32 [4, 5], P('shard'), may hold values from 1 to 512, 1024 in all within a row
- qkv_weight: bfloat16 [1024, 3072], P('shard'), may hold values from -1 to 1
- out_weight: bfloat16 [1024, 1024], P('shard'), may hold values from -1.5 to 1.5
- in_weight: bfloat16 [1024, 5248], P('shard'), may hold values from -0.1875 to 0.1875
- down_weight: bfloat16 [2624, 1024], P('shard'), may hold values from -0.125 to 0.125
- attn_gain: bfloat16 [1024], P('shard'), may hold values from 0.099609375 to 1.8984375
- mlp_gain: bfloat16 [1024], P('shard'), may hold values from 0.099609375 to 1.8984375
- out_grad: bfloat16 [4, 1024, 1024], P('shard', 'seq'), may hold values from -6 to 6
Outputs:
- block_out: bfloat16 [4, 1024, 1024], P('shard', 'seq')
- block_in_grad: float32 [4, 1024, 1024], P('shard', 'seq')
- qkv_grad: float32 [1024, 3072], P('shard')
- out_weight_grad: float32 [1024, 1024], P('shard')
- in_weight_grad: float32 [1024, 5248], P('shard')
- down_grad: float32 [2624, 1024], P('shard')
- attn_gain_grad: float32 [1024], P('shard')
- mlp_gain_grad: float32 [1024], P('shard')
The draws below stay inside these ranges and needn't reach their ends.
All inputs are finite; a program needn't handle non-finite values.
Results may differ from the reference program's by a relative error of at most 0.014.
Values may be sent and summed in bfloat16 or wider, within the bound.
No kernel may reach another device: no remote copies, remote signals or barrier semaphores. Data moves between devices by JAX's collectives and lax.ppermute only.
A program may use at most 256 MiB of HBM per device.

```python
import math
import jax
import jax.numpy as jnp
import numpy as np
from jax import lax

D = 1024
HEAD = 64
FF = 2624
WINDOW = 64
DOCS = 5
SEQ = 1024
BATCH = 4


def draw_qkv_weight(key, part):
    query_part = jnp.clip(jax.random.normal(jax.random.fold_in(key, 11), (D, D), jnp.float32), -6.0, 6.0)
    key_part = jnp.clip(jax.random.normal(jax.random.fold_in(key, 12), (D, D), jnp.float32), -6.0, 6.0)
    value_part = jnp.clip(jax.random.normal(jax.random.fold_in(key, 13), (D, D), jnp.float32), -6.0, 6.0)
    whole = jnp.concatenate([query_part, key_part, value_part], axis=1) * D ** (-0.5)
    return jnp.clip(whole, -1.0, 1.0).astype(jnp.bfloat16)


def shard_levels(stream_key, shape, pieces, low, largest):
    def one(dim, parts):
        steps = jax.random.uniform(jax.random.fold_in(jax.random.fold_in(stream_key, 6), dim), (parts,), jnp.float32, low / len(pieces), largest / len(pieces))
        return jnp.repeat(jnp.exp(steps), shape[dim] // parts).reshape((-1,) + (1,) * (len(shape) - dim - 1))

    factor_of = one(*pieces[0])
    for cut in pieces[1:]:
        factor_of = factor_of * one(*cut)
    return factor_of


def split_up(number_of, total, most, lean):
    loads = [(1 << 20) // math.isqrt(standing ** lean) + 1 for standing in range(2, number_of + 1)]
    rest, counts = total - most - (number_of - 1), [1] * (number_of - 1)
    while rest > 0:
        free = [i for i in range(number_of - 1) if counts[i] < most]
        pool, budget = sum([loads[i] for i in free]), rest
        for i in free:
            more = min(most - counts[i], max(1, budget * loads[i] // pool), rest)
            counts[i] = counts[i] + more
            rest = rest - more
    return np.array([most] + counts)


def ragged(key, count, total, limit, lean):
    if count == 2:
        one = jax.random.randint(key, (), max(1, total - limit), min(limit, total - 1) + 1)
        return jnp.stack([one, total - one])
    sizes = jnp.asarray(split_up(count, total, limit, lean), jnp.int32)
    couples = (count - 1) // 2
    donor, sink = sizes[1:1 + 2 * couples:2], sizes[2:2 + 2 * couples:2]
    margin = jnp.minimum(donor - 1, limit - sink)
    passed = jax.random.randint(jax.random.fold_in(key, 1), (couples,), 0, 1 << 20) % (margin + 1)
    sizes = sizes.at[1:1 + 2 * couples:2].set(donor - passed).at[2:2 + 2 * couples:2].set(sink + passed)
    return sizes[jax.random.permutation(jax.random.fold_in(key, 2), count)]


def normal_values(key, shape, spread, most, split=(), kind=jnp.bfloat16):
    array = jax.random.normal(key, shape, jnp.float32) * spread
    if len(split) > 0:
        array = shard_levels(key, shape, split, -0.22, 0.18) * array
    return jnp.clip(array, min=-most, max=most).astype(kind)


def setup_inputs(seed: int = 0) -> dict:
    seeds = jax.random.split(jax.random.key(seed), 10)
    block_in = normal_values(seeds[0], (BATCH, SEQ, D), 1.0, 6.0, ((0, 4), (1, 8)))
    doc_lengths = jax.vmap(lambda own: ragged(own, DOCS, SEQ, SEQ // 2, 2))(jax.random.split(seeds[1], BATCH)).reshape((BATCH, DOCS)).astype(jnp.int32)
    qkv_weight = draw_qkv_weight(jax.random.fold_in(seeds[9], 71), 0)
    out_weight = normal_values(seeds[3], (D, D), (D // 64) ** -0.5, 1.5, ((0, 4),))
    in_weight = normal_values(seeds[4], (D, 2 * FF), D ** -0.5, 0.1875, ((0, 4),))
    down_weight = normal_values(seeds[5], (FF, D), FF ** -0.5, 0.125, ((0, 4),))
    attn_gain = jnp.clip(1.0 + 0.18 * jax.random.normal(seeds[6], (D,), jnp.float32), 0.099609375, 1.8984375).astype(jnp.bfloat16)
    mlp_gain = jnp.clip(1.0 + 0.18 * jax.random.normal(seeds[7], (D,), jnp.float32), 0.099609375, 1.8984375).astype(jnp.bfloat16)
    out_grad = normal_values(seeds[8], (BATCH, SEQ, D), 1.0, 6.0, ((0, 4), (1, 8)))
    return dict(block_in=block_in, doc_lengths=doc_lengths, qkv_weight=qkv_weight, out_weight=out_weight, in_weight=in_weight, down_weight=down_weight, attn_gain=attn_gain, mlp_gain=mlp_gain, out_grad=out_grad)


EPSILON = 1e-05
NEGATIVE = -1e+30

def layer_norm(values, gain):
    row_mean = lax.optimization_barrier(jnp.mean(values, axis=-1, keepdims=True))
    centered = values - row_mean
    variance = lax.optimization_barrier(jnp.mean(centered * centered, axis=-1, keepdims=True))
    inv_std = lax.rsqrt(variance + EPSILON)
    normed = centered * inv_std
    return (normed, inv_std, normed * gain)

def norm_back(grad_h, normed, inv_std, gain):
    scaled = grad_h * gain
    gain_grad = lax.optimization_barrier(jnp.sum(grad_h * normed, axis=0))
    back = inv_std * (scaled - lax.optimization_barrier(jnp.mean(scaled, axis=-1, keepdims=True)) - normed * lax.optimization_barrier(jnp.mean(scaled * normed, axis=-1, keepdims=True)))
    return (back, gain_grad)

def doc_info(lengths, spots):
    ends = jnp.cumsum(lengths).astype(jnp.int32)
    before = ends[None, :] <= spots[:, None]
    segment = lax.optimization_barrier(jnp.sum(before.astype(jnp.int32), axis=1)).astype(jnp.int32)
    start = lax.optimization_barrier(jnp.sum(jnp.where(before, lengths[None, :], 0), axis=1)).astype(jnp.int32)
    return (segment, (spots - start).astype(jnp.int32))

def rope_tables(position):
    half = HEAD // 2
    freq = jnp.power(10000.0, -(jnp.arange(half).astype(jnp.float32) * (2.0 / HEAD)))
    angle = position.astype(jnp.float32)[:, None] * freq[None, :]
    return (jnp.cos(angle)[:, None, :], jnp.sin(angle)[:, None, :])

def rotate(values, cos_h, sin_h):
    half = values.shape[-1] // 2
    first = values[..., :half]
    second = values[..., half:]
    return jnp.concatenate([first * cos_h - second * sin_h, second * cos_h + first * sin_h], axis=-1)

def unrotate(values, cos_h, sin_h):
    half = values.shape[-1] // 2
    first = values[..., :half]
    second = values[..., half:]
    return jnp.concatenate([first * cos_h + second * sin_h, second * cos_h - first * sin_h], axis=-1)

def gelu_parts(values):
    cdf = 0.5 * (1.0 + jax.scipy.special.erf(values * 2.0 ** (-0.5)))
    pdf = jnp.exp(-0.5 * values * values) * (2.0 * math.pi) ** (-0.5)
    return (values * cdf, cdf + values * pdf)

def block_scores(q_blk, k_blk, allowed):
    scores = jnp.einsum('qhe,khe->hqk', q_blk.astype(jnp.float32), k_blk.astype(jnp.float32)) * HEAD ** (-0.5)
    return jnp.where(allowed[None], scores, NEGATIVE)

def attend(q_blk, k_blk, v_blk, allowed):
    scores = block_scores(q_blk, k_blk, allowed)
    top = lax.optimization_barrier(jnp.max(scores, axis=-1, keepdims=True))
    log_total = top + jnp.log(lax.optimization_barrier(jnp.sum(jnp.exp(scores - top), axis=-1, keepdims=True)))
    prob_b = jnp.exp(scores - log_total).astype(jnp.bfloat16)
    mixed = jnp.einsum('hqk,khe->qhe', prob_b.astype(jnp.float32), v_blk.astype(jnp.float32))
    return (mixed.astype(jnp.bfloat16), log_total)

def attend_back(q_blk, k_blk, v_blk, allowed, log_total, d_mix):
    scores = block_scores(q_blk, k_blk, allowed)
    prob_f = jnp.exp(scores - log_total)
    prob_b = prob_f.astype(jnp.bfloat16)
    d_val = jnp.einsum('hqk,qhe->khe', prob_b.astype(jnp.float32), d_mix.astype(jnp.float32))
    d_prob = jnp.einsum('qhe,khe->hqk', d_mix.astype(jnp.float32), v_blk.astype(jnp.float32))
    delta = lax.optimization_barrier(jnp.sum(prob_f * d_prob, axis=-1, keepdims=True))
    d_score = (prob_f * (d_prob - delta)).astype(jnp.bfloat16).astype(jnp.float32)
    d_query = jnp.einsum('hqk,khe->qhe', d_score, k_blk.astype(jnp.float32)) * HEAD ** (-0.5)
    d_key = jnp.einsum('hqk,qhe->khe', d_score, q_blk.astype(jnp.float32)) * HEAD ** (-0.5)
    return (d_query, d_key, d_val)

def one_row(weights, row_in, lengths, row_grad):
    qkv_w, out_w, in_w, down_w, gain_a, gain_m = weights
    seq_len, width = row_in.shape
    heads = width // HEAD
    ff_units = down_w.shape[0]
    reach = WINDOW
    block_rows = min(seq_len, 512)
    block_count = seq_len // block_rows
    spots = jnp.arange(seq_len, dtype=jnp.int32)
    segment, position = doc_info(lengths, spots)
    key_spots = (jnp.arange(seq_len + 2 * reach, dtype=jnp.int32) - reach).astype(jnp.int32)
    key_segment = doc_info(lengths, key_spots)[0]
    key_valid = (key_spots >= 0) & (key_spots < seq_len)
    feats = row_in.astype(jnp.float32)
    normed_a, inv_a, scaled_a = layer_norm(feats, gain_a.astype(jnp.float32))
    h_attn = scaled_a.astype(jnp.bfloat16)
    qkv_act = jnp.dot(h_attn, qkv_w, preferred_element_type=jnp.float32)
    cos_h, sin_h = rope_tables(position)
    query = rotate(qkv_act[:, :width].reshape(seq_len, heads, HEAD), cos_h, sin_h).astype(jnp.bfloat16)
    key_rows = rotate(qkv_act[:, width:2 * width].reshape(seq_len, heads, HEAD), cos_h, sin_h).astype(jnp.bfloat16)
    value_rows = qkv_act[:, 2 * width:].reshape(seq_len, heads, HEAD).astype(jnp.bfloat16)
    pad_spec = ((reach, reach), (0, 0), (0, 0))
    ext_keys = jnp.pad(key_rows, pad_spec)
    ext_vals = jnp.pad(value_rows, pad_spec)

    def block_mask(index):
        start = (index * block_rows).astype(jnp.int32)
        q_spots = lax.dynamic_slice_in_dim(spots, start, block_rows)
        q_seg = lax.dynamic_slice_in_dim(segment, start, block_rows)
        k_spots = lax.dynamic_slice_in_dim(key_spots, start, block_rows + 2 * reach)
        k_seg = lax.dynamic_slice_in_dim(key_segment, start, block_rows + 2 * reach)
        k_ok = lax.dynamic_slice_in_dim(key_valid, start, block_rows + 2 * reach)
        near = jnp.abs(q_spots[:, None] - k_spots[None, :]) <= reach
        return k_ok[None, :] & (q_seg[:, None] == k_seg[None, :]) & near

    def block_inputs(index):
        start = (index * block_rows).astype(jnp.int32)
        q_blk = lax.dynamic_slice_in_dim(query, start, block_rows)
        k_blk = lax.dynamic_slice_in_dim(ext_keys, start, block_rows + 2 * reach)
        v_blk = lax.dynamic_slice_in_dim(ext_vals, start, block_rows + 2 * reach)
        return (start, q_blk, k_blk, v_blk)

    def forward_block(index):
        start, q_blk, k_blk, v_blk = block_inputs(index)
        return attend(q_blk, k_blk, v_blk, block_mask(index))
    mixed, log_total = lax.map(forward_block, jnp.arange(block_count, dtype=jnp.int32))
    attn_out = mixed.reshape(seq_len, width)
    resid = feats + jnp.dot(attn_out, out_w, preferred_element_type=jnp.float32)
    normed_m, inv_m, scaled_m = layer_norm(resid, gain_m.astype(jnp.float32))
    h_mlp = scaled_m.astype(jnp.bfloat16)
    up_act = jnp.dot(h_mlp, in_w, preferred_element_type=jnp.float32)
    gate_in = up_act[:, :ff_units]
    lin = up_act[:, ff_units:]
    gelu_val, gelu_slope = gelu_parts(gate_in)
    act = (gelu_val * lin).astype(jnp.bfloat16)
    row_out = (resid + jnp.dot(act, down_w, preferred_element_type=jnp.float32)).astype(jnp.bfloat16)
    grad_f = row_grad.astype(jnp.float32)
    down_g = jnp.dot(act.T, row_grad, preferred_element_type=jnp.float32)
    d_act = jnp.dot(row_grad, down_w.T, preferred_element_type=jnp.float32)
    d_up = jnp.concatenate([d_act * lin * gelu_slope, d_act * gelu_val], axis=1).astype(jnp.bfloat16)
    in_g = jnp.dot(h_mlp.T, d_up, preferred_element_type=jnp.float32)
    d_hmlp = jnp.dot(d_up, in_w.T, preferred_element_type=jnp.float32)
    d_back_m, gain_m_g = norm_back(d_hmlp, normed_m, inv_m, gain_m.astype(jnp.float32))
    d_resid = grad_f + d_back_m
    d_resid_b = d_resid.astype(jnp.bfloat16)
    out_g = jnp.dot(attn_out.T, d_resid_b, preferred_element_type=jnp.float32)
    d_attn = jnp.dot(d_resid_b, out_w.T, preferred_element_type=jnp.float32).astype(jnp.bfloat16)
    d_attn3 = d_attn.reshape(seq_len, heads, HEAD)

    def backward_block(carry, index):
        start, q_blk, k_blk, v_blk = block_inputs(index)
        d_blk = lax.dynamic_slice_in_dim(d_attn3, start, block_rows)
        d_query, d_key, d_val = attend_back(q_blk, k_blk, v_blk, block_mask(index), log_total[index], d_blk)
        key_part = block_rows + 2 * reach
        fresh = jnp.concatenate([d_key.reshape(key_part, width), d_val.reshape(key_part, width)], axis=1)
        old = lax.dynamic_slice_in_dim(carry, start, key_part)
        return (lax.dynamic_update_slice_in_dim(carry, old + fresh, start, 0), d_query)
    ext_grad, d_q_blocks = lax.scan(backward_block, jnp.zeros((seq_len + 2 * reach, 2 * width), jnp.float32), jnp.arange(block_count, dtype=jnp.int32))
    kv_grad = ext_grad[reach:reach + seq_len]
    d_query = unrotate(d_q_blocks.reshape(seq_len, heads, HEAD), cos_h, sin_h).reshape(seq_len, width)
    d_keys = unrotate(kv_grad[:, :width].reshape(seq_len, heads, HEAD), cos_h, sin_h).reshape(seq_len, width)
    d_qkv = jnp.concatenate([d_query, d_keys, kv_grad[:, width:]], axis=1).astype(jnp.bfloat16)
    qkv_g = jnp.dot(h_attn.T, d_qkv, preferred_element_type=jnp.float32)
    d_hattn = jnp.dot(d_qkv, qkv_w.T, preferred_element_type=jnp.float32)
    d_back_a, gain_a_g = norm_back(d_hattn, normed_a, inv_a, gain_a.astype(jnp.float32))
    row_in_grad = d_resid + d_back_a
    return (row_out, row_in_grad, (qkv_g, out_g, in_g, down_g, gain_a_g, gain_m_g))

def reference(block_in, doc_lengths, qkv_weight, out_weight, in_weight, down_weight, attn_gain, mlp_gain, out_grad):
    weights = (qkv_weight, out_weight, in_weight, down_weight, attn_gain, mlp_gain)
    initial = tuple((jnp.zeros(weight.shape, jnp.float32) for weight in weights))

    def row_step(totals, row_data):
        row_out, row_in_grad, grads = one_row(weights, row_data[0], row_data[1], row_data[2])
        return (tuple((total + extra for total, extra in zip(totals, grads))), (row_out, row_in_grad))
    totals, (outputs, in_grads) = lax.scan(row_step, initial, (block_in, doc_lengths, out_grad))
    return (outputs, in_grads, totals[0], totals[1], totals[2], totals[3], totals[4], totals[5])
```

```python
import functools
import math

import jax
import jax.numpy as jnp
from jax import lax
from jax.experimental import pallas as pl
from jax.experimental.pallas import tpu as pltpu
from jax.sharding import PartitionSpec as P

HEAD = 64
WINDOW = 64
EPSILON = 1e-05
NEGATIVE = -1e30
BF = jnp.bfloat16
F32 = jnp.float32
TAIL = 16


def mm(a, b, dims=((1,), (0,))):
    return lax.dot_general(a, b, (dims, ((), ())), preferred_element_type=F32)


def call(kernel, out_shape, *args, scalars=None, scratch=()):
    vmem = pl.BlockSpec(memory_space=pltpu.VMEM)
    specs = [vmem] * len(args)
    if scalars is not None:
        specs = [pl.BlockSpec(memory_space=pltpu.SMEM)] + specs
        args = (scalars,) + tuple(args)
    return pl.pallas_call(
        kernel,
        out_shape=out_shape,
        in_specs=specs,
        out_specs=jax.tree.map(lambda _: vmem, out_shape),
        scratch_shapes=list(scratch),
        compiler_params=pltpu.CompilerParams(vmem_limit_bytes=58 << 20),
    )(*args)


def sds(shape, dtype):
    return jax.ShapeDtypeStruct(shape, dtype)


def norm(values):
    centered = values - jnp.mean(values, axis=-1, keepdims=True)
    variance = jnp.mean(centered * centered, axis=-1, keepdims=True)
    inv_std = lax.rsqrt(variance + EPSILON)
    return centered * inv_std, inv_std


def norm_back(scaled, normed, inv_std):
    return inv_std * (
        scaled
        - jnp.mean(scaled, axis=-1, keepdims=True)
        - normed * jnp.mean(scaled * normed, axis=-1, keepdims=True)
    )


def swap_halves(x):
    width = x.shape[-1]
    half = HEAD // 2
    lane = lax.broadcasted_iota(jnp.int32, x.shape, 1)
    return jnp.where(
        lane % HEAD < half,
        pltpu.roll(x, width - half, 1),
        pltpu.roll(x, half, 1),
    )


def weights_kernel(S, hb, sc, mine, other, out):
    s, c = sc[0], sc[1]
    for m in range(S):
        base = (s ^ m) * (2 * hb)
        out[pl.ds(pl.multiple_of(base + c * hb, hb), hb), :] = mine[m]
        out[pl.ds(pl.multiple_of(base + (1 - c) * hb, hb), hb), :] = other[m]


def late_weights_kernel(S, hb, sc, im, io, om, oo, gate, lin, outw):
    s, c = sc[0], sc[1]
    for m in range(S):
        base = (s ^ m) * (2 * hb)
        a = pl.ds(pl.multiple_of(base + c * hb, hb), hb)
        b = pl.ds(pl.multiple_of(base + (1 - c) * hb, hb), hb)
        gate[a, :] = im[m, 0]
        gate[b, :] = io[m, 0]
        lin[a, :] = im[m, 1]
        lin[b, :] = io[m, 1]
        base = m * (2 * hb)
        a = pl.ds(pl.multiple_of(base + c * hb, hb), hb)
        b = pl.ds(pl.multiple_of(base + (1 - c) * hb, hb), hb)
        outw[a, :] = om[m]
        outw[b, :] = oo[m]


def qkv_kernel(S, T, hb, sc, *refs):
    x = refs[:S]
    wm, wo, gain, cos, sin = refs[S : S + 5]
    h, rq, kv, lead, last, wnat = refs[S + 5 :]
    weights_kernel(S, hb, sc, wm, wo, wnat)
    cw = rq.shape[1]
    for m in range(S):
        normed, _ = norm(x[m][...].astype(F32))
        rows = pl.ds(m * T, T)
        h[rows, :] = (normed * gain[...]).astype(BF)
        act = mm(h[rows, :], wnat[...])
        cm, sm = cos[rows, :], sin[rows, :]
        q, k = act[:, :cw], act[:, cw : 2 * cw]
        rq[rows, :] = (q * cm + swap_halves(q) * sm).astype(BF)
        kb = (k * cm + swap_halves(k) * sm).astype(BF)
        vb = act[:, 2 * cw :].astype(BF)
        kv[rows, :cw] = kb
        kv[rows, cw:] = vb
        lead[m, :, :cw] = kb[:WINDOW]
        lead[m, :, cw:] = vb[:WINDOW]
        last[m, :, :cw] = kb[T - WINDOW :]
        last[m, :, cw:] = vb[T - WINDOW :]


def attend_kernel(S, T, heads, rq, kv, before, after, mask, out, total, ext):
    cw = heads * HEAD
    for m in range(S):
        rows = pl.ds(m * T, T)
        ext[:WINDOW, :] = before[m]
        ext[WINDOW : WINDOW + T, :] = kv[rows, :]
        ext[WINDOW + T :, :] = after[m]
        ok = mask[rows, :] > 0.0
        for h in range(heads):
            q = rq[rows, h * HEAD : (h + 1) * HEAD]
            k = ext[:, h * HEAD : (h + 1) * HEAD]
            v = ext[:, cw + h * HEAD : cw + (h + 1) * HEAD]
            scores = mm(q, k, ((1,), (1,))) * HEAD ** (-0.5)
            scores = jnp.where(ok, scores, NEGATIVE)
            top = jnp.max(scores, axis=-1, keepdims=True)
            log_total = top + jnp.log(jnp.sum(jnp.exp(scores - top), axis=-1, keepdims=True))
            prob = jnp.exp(scores - log_total).astype(BF)
            out[rows, h * HEAD : (h + 1) * HEAD] = mm(prob, v).astype(BF)
            total[rows, h : h + 1] = log_total


def attend_back_kernel(S, T, heads, *refs):
    rq, kv, before, after, mask, total, cos, sin = refs[:8]
    d_mix = refs[8 : 8 + S]
    dq, dkv, to_left, to_right, ext = refs[8 + S :]
    cw = heads * HEAD
    for m in range(S):
        rows = pl.ds(m * T, T)
        ext[:WINDOW, :] = before[m]
        ext[WINDOW : WINDOW + T, :] = kv[rows, :]
        ext[WINDOW + T :, :] = after[m]
        ok = mask[rows, :] > 0.0
        dqs = []
        for h in range(heads):
            ks = slice(h * HEAD, (h + 1) * HEAD)
            vs = slice(cw + h * HEAD, cw + (h + 1) * HEAD)
            q = rq[rows, ks]
            k = ext[:, ks]
            v = ext[:, vs]
            d = d_mix[m][:, ks]
            scores = mm(q, k, ((1,), (1,))) * HEAD ** (-0.5)
            scores = jnp.where(ok, scores, NEGATIVE)
            prob = jnp.exp(scores - total[rows, h : h + 1])
            d_val = mm(prob.astype(BF), d, ((0,), (0,)))
            d_prob = mm(d, v, ((1,), (1,)))
            delta = jnp.sum(prob * d_prob, axis=-1, keepdims=True)
            d_score = (prob * (d_prob - delta)).astype(BF)
            dqs.append(mm(d_score, k) * HEAD ** (-0.5))
            d_key = mm(d_score, q, ((0,), (0,))) * HEAD ** (-0.5)
            for sl, g in ((ks, d_key), (vs, d_val)):
                to_left[m, :, sl] = g[:WINDOW].astype(BF)
                dkv[rows, sl] = g[WINDOW : WINDOW + T]
                to_right[m, :, sl] = g[WINDOW + T :].astype(BF)
        g = jnp.concatenate(dqs, axis=1)
        dq[rows, :] = (g * cos[rows, :] - swap_halves(g) * sin[rows, :]).astype(BF)


def middle_kernel(S, T, *refs):
    x = refs[:S]
    att = refs[S : 2 * S]
    outw, gain, gate_w, lin_w, d_act = refs[2 * S : 2 * S + 5]
    resid_own, h, act, d_gate, d_lin = refs[2 * S + 5 : 2 * S + 10]
    pieces = refs[2 * S + 10 :]
    cw = att[0].shape[1]
    for m in range(S):
        rows = pl.ds(m * T, T)
        resid = x[m][...].astype(F32)
        for j in range(S):
            resid = resid + mm(
                att[j][pl.ds((m ^ j) * T, T), :], outw[j * cw : (j + 1) * cw, :]
            )
        if m == 0:
            resid_own[...] = resid
        normed, _ = norm(resid)
        hb = (normed * gain[...]).astype(BF)
        h[rows, :] = hb
        gate_in = mm(hb, gate_w[...])
        lin = mm(hb, lin_w[...])
        cdf = 0.5 * (1.0 + lax.erf(gate_in * 2.0 ** (-0.5)))
        pdf = jnp.exp(-0.5 * gate_in * gate_in) * (2.0 * math.pi) ** (-0.5)
        gelu = gate_in * cdf
        act[rows, :] = (gelu * lin).astype(BF)
        da = d_act[rows, :]
        dg = (da * lin * (cdf + gate_in * pdf)).astype(BF)
        dl = (da * gelu).astype(BF)
        d_gate[rows, :] = dg
        d_lin[rows, :] = dl
        part = mm(dg, gate_w[...], ((1,), (1,))) + mm(dl, lin_w[...], ((1,), (1,)))
        pieces[m][...] = part.astype(BF)


def resid_back_kernel(S, *refs):
    parts = refs[:S]
    resid, gain, grad, outw = refs[S : S + 4]
    d_resid, d_resid_b, gain_g = refs[S + 4 : S + 7]
    pieces = refs[S + 7 :]
    d_h = parts[0][...].astype(F32)
    for m in range(1, S):
        d_h = d_h + parts[m][...].astype(F32)
    normed, inv_std = norm(resid[...])
    gain_g[...] = jnp.sum(d_h * normed, axis=0, keepdims=True)
    dr = grad[...].astype(F32) + norm_back(d_h * gain[...], normed, inv_std)
    d_resid[...] = dr
    db = dr.astype(BF)
    d_resid_b[...] = db
    cw = pieces[0].shape[1]
    for m in range(S):
        pieces[m][...] = mm(db, outw[m * cw : (m + 1) * cw, :], ((1,), (1,))).astype(BF)


def qkv_back_kernel(S, T, hb, sc, *refs):
    x = refs[:S]
    dq, dkv, from_left, from_right, cos, sin, h, wnat, gain_m_g = refs[S : S + 9]
    send = refs[S + 9]
    keep = refs[S + 10 : 2 * S + 10]
    pieces = refs[2 * S + 10 : 3 * S + 10]
    d_qkv, grad, gain_row = refs[3 * S + 10 :]
    s, c = sc[0], sc[1]
    cw = dq.shape[1]
    total = None
    for m in range(S):
        rows = pl.ds(m * T, T)
        g = dkv[rows, :]
        pad = jnp.zeros((T - WINDOW, 2 * cw), F32)
        g = g + jnp.concatenate([from_left[m].astype(F32), pad], axis=0)
        g = g + jnp.concatenate([pad, from_right[m].astype(F32)], axis=0)
        dk = g[:, :cw]
        dk = dk * cos[rows, :] - swap_halves(dk) * sin[rows, :]
        d_qkv[rows, :cw] = dq[rows, :]
        d_qkv[rows, cw : 2 * cw] = dk.astype(BF)
        d_qkv[rows, 2 * cw :] = g[:, cw:].astype(BF)
    grad[...] = mm(h[...], d_qkv[...], ((0,), (0,)))
    for m in range(S):
        d_h = mm(d_qkv[pl.ds(m * T, T), :], wnat[...], ((1,), (1,)))
        normed, _ = norm(x[m][...].astype(F32))
        part = jnp.sum(d_h * normed, axis=0, keepdims=True)
        total = part if total is None else total + part
        pieces[m][...] = d_h.astype(BF)
    gain_row[0:1, :] = total
    gain_row[1:2, :] = gain_m_g[...]
    row = lax.broadcasted_iota(jnp.int32, (TAIL, 2 * hb), 0)
    for m in range(S):
        base = (s ^ m) * (2 * hb)
        for ref, half in ((send.at[m], 1 - c), (keep[m], c)):
            rows = pl.ds(pl.multiple_of(base + half * hb, hb), hb)
            ref[:hb, :] = grad[rows, :].astype(BF)
            ref[hb:, :] = jnp.zeros((TAIL, ref.shape[1]), BF)
            cols = pl.ds(pl.multiple_of(base, 2 * hb), 2 * hb)
            for i in range(2):
                both = jnp.broadcast_to(gain_row[i : i + 1, cols], row.shape)
                ref[hb:, i * 2 * hb : (i + 1) * 2 * hb] = jnp.where(row == 0, both, 0.0).astype(BF)


def in_grad_kernel(S, hb, sc, h, d_gate, d_lin, *refs):
    send = refs[0]
    keep = refs[1 : S + 1]
    grad = refs[S + 1]
    s, c = sc[0], sc[1]
    for i, d in enumerate((d_gate, d_lin)):
        grad[...] = mm(h[...], d[...], ((0,), (0,)))
        for m in range(S):
            base = (s ^ m) * (2 * hb)
            for ref, half in ((send.at[m], 1 - c), (keep[m], c)):
                rows = pl.ds(pl.multiple_of(base + half * hb, hb), hb)
                ref[i] = grad[rows, :].astype(BF)


def in_back_kernel(S, *refs):
    parts = refs[:S]
    x, gain, d_resid, out = refs[S:]
    d_h = parts[0][...].astype(F32)
    for m in range(1, S):
        d_h = d_h + parts[m][...].astype(F32)
    normed, inv_std = norm(x[...].astype(F32))
    out[...] = d_resid[...] + norm_back(d_h * gain[...], normed, inv_std)


def qkv_final_kernel(S, hb, sc, *refs):
    mine = refs[:S]
    other = refs[S]
    grad, gain_a, gain_m = refs[S + 1 :]
    s, c = sc[0], sc[1]
    cw = mine[0].shape[1] // 3
    d = cw * S
    total = None
    for m in range(S):
        for ref, half in ((mine[m], c), (other.at[m], 1 - c)):
            rows = pl.ds(pl.multiple_of(half * hb, hb), hb)
            for i in range(3):
                cols = pl.ds(pl.multiple_of(i * d + (s ^ m) * cw, cw), cw)
                grad[rows, cols] = ref[:hb, i * cw : (i + 1) * cw].astype(F32)
        part = mine[m][hb:, :].astype(F32)
        total = part if total is None else total + part
    row = jnp.sum(total, axis=0, keepdims=True)
    gain_a[...] = row[:, : 2 * hb]
    gain_m[...] = row[:, 2 * hb : 4 * hb]


def after(values, *others):
    flat, tree = jax.tree.flatten(values)
    out = lax.optimization_barrier(tuple(flat) + tuple(others))
    return jax.tree.unflatten(tree, out[: len(flat)])


def shards(
    block_in,
    doc_lengths,
    qkv_weight,
    out_weight,
    in_weight,
    down_weight,
    attn_gain,
    mlp_gain,
    out_grad,
):
    S, Q = lax.axis_size("shard"), lax.axis_size("seq")
    Z = Q // 2
    s, q = lax.axis_index("shard"), lax.axis_index("seq")
    c, z = q % 2, q // 2
    sc = jnp.stack([s, c]).astype(jnp.int32)
    T, D = block_in.shape[1:]
    cw = D // S
    heads = cw // HEAD
    hb = D // S // 2
    ff = in_weight.shape[1] // 2
    fs = ff // S

    def peer(x, m):
        return lax.ppermute(x, "shard", [(i, i ^ m) for i in range(S)])

    def core_swap(x):
        return lax.ppermute(x, "seq", [(i, i ^ 1) for i in range(Q)])

    def along(x, pairs):
        return lax.ppermute(x, "seq", [(2 * a + e, 2 * b + e) for a, b in pairs for e in (0, 1)])

    def shift(x, step):
        return lax.ppermute(x, "seq", [(i, i + step) for i in range(Q) if 0 <= i + step < Q])

    def gather(x):
        return [x] + [peer(x, m) for m in range(1, S)]

    def swap_out(pieces):
        return [pieces[0]] + [peer(pieces[m], m) for m in range(1, S)]

    def z_sum(x):
        half = Z // 2
        for k in range(half - 1):
            x = x + along(x, [(k, k + 1), (Z - 1 - k, Z - 2 - k)])
        if Z > 1:
            x = x + along(x, [(half - 1, half), (half, half - 1)])
        for k in range(half - 1, 0, -1):
            got = along(x, [(k, k - 1), (Z - 1 - k, Z - k)])
            x = jnp.where((z == k - 1) | (z == Z - k), got, x)
        return x

    def cols(w, start, size):
        return lax.dynamic_slice_in_dim(w, start, size, axis=1)

    x_own = block_in[0]
    misc = jnp.zeros((8, max(2 * hb, 128)), F32)
    misc = misc.at[0, : 2 * hb].set(attn_gain.astype(F32))
    misc = misc.at[1, : 2 * hb].set(mlp_gain.astype(F32))
    misc = misc.at[2, : doc_lengths.shape[1]].set(doc_lengths[0].astype(F32))
    miscs = gather(misc)
    x = gather(x_own)

    qkv_half = lax.dynamic_slice_in_dim(qkv_weight, c * hb, hb, axis=0)
    qkv_pieces = [
        jnp.concatenate([cols(qkv_half, i * D + (s ^ m) * cw, cw) for i in range(3)], axis=1)
        for m in range(S)
    ]
    wm = jnp.stack(swap_out(qkv_pieces))
    wo = core_swap(wm)

    in_half = lax.dynamic_slice_in_dim(in_weight, c * hb, hb, axis=0)
    out_half = lax.dynamic_slice_in_dim(out_weight, c * hb, hb, axis=0)
    in_pieces = [
        jnp.stack([cols(in_half, (s ^ m) * fs, fs), cols(in_half, ff + (s ^ m) * fs, fs)])
        for m in range(S)
    ]
    in_pieces, out_half, g_own = after((in_pieces, out_half, out_grad[0]), wm)
    im = jnp.stack(swap_out(in_pieces))
    om = jnp.stack(gather(out_half))
    io, oo = core_swap(im), core_swap(om)
    grads = gather(g_own)
    og = jnp.concatenate(grads, axis=0)

    stack = jnp.stack(miscs)
    gains = [
        jnp.concatenate(
            [lax.dynamic_index_in_dim(stack[:, i, : 2 * hb], s ^ j, 0, True) for j in range(S)],
            axis=1,
        )
        for i in range(2)
    ]
    gain_a, gain_m = gains
    lengths = stack[:, 2, : doc_lengths.shape[1]].astype(jnp.int32)
    first_spot = q * T
    ends = jnp.cumsum(lengths, axis=1)
    key_spots = first_spot - WINDOW + jnp.arange(T + 2 * WINDOW, dtype=jnp.int32)
    passed = ends[:, :, None] <= key_spots[None, None, :]
    key_segment = jnp.sum(passed.astype(jnp.int32), axis=1)
    start = jnp.sum(jnp.where(passed, lengths[:, :, None], 0), axis=1)
    position = (key_spots[None] - start)[:, WINDOW : WINDOW + T]
    segment = key_segment[:, WINDOW : WINDOW + T]
    spots = key_spots[WINDOW : WINDOW + T]
    near = jnp.abs(spots[:, None] - key_spots[None, :]) <= WINDOW
    valid = (key_spots >= 0) & (key_spots < Q * T)
    mask = (segment[:, :, None] == key_segment[:, None, :]) & (near & valid[None, :])[None]
    mask = mask.astype(F32).reshape(S * T, T + 2 * WINDOW)
    half = HEAD // 2
    freq = jnp.power(10000.0, -(jnp.arange(half).astype(F32) * (2.0 / HEAD)))
    angle = position.reshape(S * T, 1).astype(F32) * freq[None, :]
    cos_h, sin_h = jnp.cos(angle), jnp.sin(angle)
    cos = jnp.concatenate([cos_h, cos_h] * heads, axis=1)
    sin = jnp.concatenate([-sin_h, sin_h] * heads, axis=1)

    h_attn, rq, kv, lead, last, wnat = call(
        functools.partial(qkv_kernel, S, T, hb),
        (
            sds((S * T, D), BF),
            sds((S * T, cw), BF),
            sds((S * T, 2 * cw), BF),
            sds((S, WINDOW, 2 * cw), BF),
            sds((S, WINDOW, 2 * cw), BF),
            sds((D, 3 * cw), BF),
        ),
        *x,
        wm,
        wo,
        gain_a,
        cos,
        sin,
        scalars=sc,
    )
    before_kv, after_kv = shift(last, 1), shift(lead, -1)
    ext = pltpu.VMEM((T + 2 * WINDOW, 2 * cw), BF)
    att_own, total = call(
        functools.partial(attend_kernel, S, T, heads),
        (sds((S * T, cw), BF), sds((S * T, heads), F32)),
        rq,
        kv,
        before_kv,
        after_kv,
        mask,
        scratch=[ext],
    )
    att = gather(att_own)

    gate_w, lin_w, outw = call(
        functools.partial(late_weights_kernel, S, hb),
        (sds((D, fs), BF), sds((D, fs), BF), sds((D, D), BF)),
        im,
        io,
        om,
        oo,
        scalars=sc,
    )
    d_act = mm(og, down_weight, ((1,), (1,)))
    mid = call(
        functools.partial(middle_kernel, S, T),
        (
            sds((T, D), F32),
            sds((S * T, D), BF),
            sds((S * T, fs), BF),
            sds((S * T, fs), BF),
            sds((S * T, fs), BF),
        )
        + (sds((T, D), BF),) * S,
        *x,
        *att,
        outw,
        gain_m,
        gate_w,
        lin_w,
        d_act,
    )
    resid_own, h_mlp, act, d_gate, d_lin = mid[:5]
    d_hmlp = swap_out(mid[5:])

    back = call(
        functools.partial(resid_back_kernel, S),
        (sds((T, D), F32), sds((T, D), BF), sds((1, D), F32)) + (sds((T, cw), BF),) * S,
        *d_hmlp,
        resid_own,
        gain_m,
        g_own,
        outw,
    )
    d_resid, d_resid_b, gain_m_g = back[:3]
    d_mix = swap_out(back[3:])

    dq, dkv, to_left, to_right = call(
        functools.partial(attend_back_kernel, S, T, heads),
        (
            sds((S * T, cw), BF),
            sds((S * T, 2 * cw), F32),
            sds((S, WINDOW, 2 * cw), BF),
            sds((S, WINDOW, 2 * cw), BF),
        ),
        rq,
        kv,
        before_kv,
        after_kv,
        mask,
        total,
        cos,
        sin,
        *d_mix,
        scratch=[ext],
    )
    from_right, from_left = shift(to_left, -1), shift(to_right, 1)
    res = call(
        functools.partial(qkv_back_kernel, S, T, hb),
        (sds((S, hb + TAIL, 3 * cw), BF),)
        + (sds((hb + TAIL, 3 * cw), BF),) * S
        + (sds((T, D), BF),) * S,
        *x,
        dq,
        dkv,
        from_left,
        from_right,
        cos,
        sin,
        h_attn,
        wnat,
        gain_m_g,
        scalars=sc,
        scratch=[
            pltpu.VMEM((S * T, 3 * cw), BF),
            pltpu.VMEM((D, 3 * cw), F32),
            pltpu.VMEM((2, D), F32),
        ],
    )
    got = core_swap(res[0])
    qkv_g = [res[1 + m] + got[m] for m in range(S)]
    d_hattn = swap_out(res[1 + S :])
    qkv_g = [z_sum(p) for p in swap_out(qkv_g)]
    qkv_other = core_swap(jnp.stack(qkv_g))

    other_half = cols(og, (1 - c) * (D // 2), D // 2)
    own_half = cols(og, c * (D // 2), D // 2)
    down_send = mm(act, other_half, ((0,), (0,))).astype(BF)
    down_keep = mm(act, own_half, ((0,), (0,)))
    down_sum = (down_keep + core_swap(down_send).astype(F32)).astype(BF)
    down_mine = z_sum(down_sum)
    down_other = core_swap(down_mine)

    ig = call(
        functools.partial(in_grad_kernel, S, hb),
        (sds((S, 2, hb, fs), BF),) + (sds((2, hb, fs), BF),) * S,
        h_mlp,
        d_gate,
        d_lin,
        scalars=sc,
        scratch=[pltpu.VMEM((D, fs), F32)],
    )
    got = core_swap(ig[0])
    in_g = [ig[1 + m] + got[m] for m in range(S)]
    in_g = [z_sum(p) for p in swap_out(in_g)]
    in_mine = jnp.stack(in_g)
    in_other = core_swap(in_mine)

    out_parts = mm(act, down_weight).astype(BF)
    out_parts = swap_out([out_parts[m * T : (m + 1) * T] for m in range(S)])
    final = resid_own
    for p in out_parts:
        final = final + p.astype(F32)
    final = final.astype(BF)

    drb = jnp.concatenate(gather(d_resid_b), axis=0)
    out_send = mm(att_own, cols(drb, (1 - c) * (D // 2), D // 2), ((0,), (0,))).astype(BF)
    out_keep = mm(att_own, cols(drb, c * (D // 2), D // 2), ((0,), (0,)))
    out_sum = (out_keep + core_swap(out_send).astype(F32)).astype(BF)
    out_mine = z_sum(out_sum)
    out_other = core_swap(out_mine)

    in_rows = call(
        functools.partial(in_back_kernel, S),
        sds((T, D), F32),
        *d_hattn,
        x_own,
        gain_a,
        d_resid,
    )

    qkv_grad, gain_a_grad, gain_m_grad = call(
        functools.partial(qkv_final_kernel, S, hb),
        (sds((2 * hb, 3 * D), F32), sds((1, 2 * hb), F32), sds((1, 2 * hb), F32)),
        *qkv_g,
        qkv_other,
        scalars=sc,
    )

    def by_core(mine, other, axis):
        return jnp.where(
            c == 0,
            jnp.concatenate([mine, other], axis=axis),
            jnp.concatenate([other, mine], axis=axis),
        )

    down_grad = by_core(down_mine, down_other, 1).astype(F32)
    out_wgrad = by_core(out_mine, out_other, 1).astype(F32)
    in_all = by_core(in_mine, in_other, 2)
    in_nat = [lax.dynamic_index_in_dim(in_all, s ^ j, 0, False) for j in range(S)]
    in_wgrad = jnp.concatenate([p[i] for i in range(2) for p in in_nat], axis=1).astype(F32)
    return (
        final[None],
        in_rows[None],
        qkv_grad,
        out_wgrad,
        in_wgrad,
        down_grad,
        gain_a_grad[0],
        gain_m_grad[0],
    )


def solution(mesh):
    rows = P("shard", "seq", None)
    mat = P("shard", None)
    vec = P("shard")
    return jax.shard_map(
        shards,
        mesh=mesh,
        in_specs=(rows, mat, mat, mat, mat, mat, vec, vec, rows),
        out_specs=(rows, rows, mat, mat, mat, mat, vec, vec),
        check_vma=False,
    )
```

```python
import functools
import math

import jax
import jax.numpy as jnp
from jax import lax
from jax.experimental import pallas as pl
from jax.experimental.pallas import tpu as pltpu
from jax.sharding import PartitionSpec as P


HEAD = 64
WINDOW = 64
EPSILON = 1e-05
NEGATIVE = -1e30
BF = jnp.bfloat16
F32 = jnp.float32
TAIL = 16
NT = ((1,), (1,))
TN = ((0,), (0,))


def mm(a, b, dims=((1,), (0,))):
    return lax.dot_general(a, b, (dims, ((), ())), preferred_element_type=F32)


def call(kernel, out_shape, *args, scalars=None, scratch=()):
    vmem = pl.BlockSpec(memory_space=pltpu.VMEM)
    specs = [vmem] * len(args)
    if scalars is not None:
        specs = [pl.BlockSpec(memory_space=pltpu.SMEM)] + specs
        args = (scalars,) + tuple(args)
    return pl.pallas_call(
        kernel,
        out_shape=out_shape,
        in_specs=specs,
        out_specs=jax.tree.map(lambda _: vmem, out_shape),
        scratch_shapes=list(scratch),
        compiler_params=pltpu.CompilerParams(vmem_limit_bytes=58 << 20),
    )(*args)


def sds(shape, dtype):
    return jax.ShapeDtypeStruct(shape, dtype)


def norm(values):
    centered = values - jnp.mean(values, axis=-1, keepdims=True)
    variance = jnp.mean(centered * centered, axis=-1, keepdims=True)
    inv_std = lax.rsqrt(variance + EPSILON)
    return centered * inv_std, inv_std


def norm_back(scaled, normed, inv_std):
    return inv_std * (
        scaled
        - jnp.mean(scaled, axis=-1, keepdims=True)
        - normed * jnp.mean(scaled * normed, axis=-1, keepdims=True)
    )


def swap_halves(x):
    half = HEAD // 2
    lane = lax.broadcasted_iota(jnp.int32, x.shape, 1)
    return jnp.where(lane % HEAD < half, pltpu.roll(x, 128 - half, 1), pltpu.roll(x, half, 1))


def turned(x, cos, sin):
    blocks = [x[:, i : i + 128] for i in range(0, x.shape[1], 128)]
    return jnp.concatenate([b * cos + swap_halves(b) * sin for b in blocks], axis=1)


def at(start, size):
    return pl.ds(pl.multiple_of(start, size), size)


def pick(ref, index, size):
    if size % 128 == 0:
        return ref[:, at(index * size, size)]
    two = ref[:, at(index // 2 * (2 * size), 2 * size)]
    return jnp.where(index % 2 == 0, two[:, :size], two[:, size:])


def in_order(S, hb, sc, relative, mine, other, out):
    s, c = sc[0], sc[1]
    for m in range(S):
        base = (m if relative else (s ^ m)) * (2 * hb)
        out[at(base + c * hb, hb), :] = mine[m][...]
        out[at(base + (1 - c) * hb, hb), :] = other[m][...]


def qkv_kernel(S, T, hb, sc, *refs):
    x, wm, wo = refs[:S], refs[S : 2 * S], refs[2 * S : 3 * S]
    cos, sin = refs[3 * S : 3 * S + 2]
    h, rq, kv, lead, last, wnat, gain_a, gain_m = refs[3 * S + 2 :]
    in_order(S, hb, sc, False, wm, wo, wnat)
    cw = rq.shape[1]
    for m in range(S):
        rows = x[m][T:, :].astype(F32)
        cols = at((sc[0] ^ m) * (2 * hb), 2 * hb)
        gain_a[:, cols] = rows[0:1, : 2 * hb]
        gain_m[:, cols] = rows[0:1, 2 * hb : 4 * hb]
    for m in range(S):
        normed, _ = norm(x[m][:T, :].astype(F32))
        h[m * T : (m + 1) * T, :] = (normed * gain_a[...]).astype(BF)
    act = mm(h[...], wnat[...])
    rq[...] = turned(act[:, :cw], cos[...], sin[...]).astype(BF)
    kv[:, :cw] = turned(act[:, cw : 2 * cw], cos[...], sin[...]).astype(BF)
    kv[:, cw:] = act[:, 2 * cw :].astype(BF)
    for m in range(S):
        lead[m] = kv[m * T : m * T + WINDOW, :]
        last[m] = kv[(m + 1) * T - WINDOW : (m + 1) * T, :]


def two_heads(x):
    lane = lax.broadcasted_iota(jnp.int32, x.shape, 1)
    first = jnp.where(lane < HEAD, 1.0, 0.0).astype(x.dtype)
    return jnp.concatenate([x * first, x * (1 - first).astype(x.dtype)], axis=0)


def one_pair(x, T):
    lane = lax.broadcasted_iota(jnp.int32, (T, 128), 1)
    return jnp.where(lane < HEAD, x[:T], x[T:])


def extend(m, T, kv, before, after, ext):
    ext[:WINDOW, :] = before[m]
    ext[WINDOW : WINDOW + T, :] = kv[m * T : (m + 1) * T, :]
    ext[WINDOW + T :, :] = after[m]


def attend_kernel(S, T, rq, kv, before, after, mask, out, total, ext):
    cw = rq.shape[1]
    for m in range(S):
        rows = slice(m * T, (m + 1) * T)
        extend(m, T, kv, before, after, ext)
        ok = mask[rows, :] > 0.0
        ok = jnp.concatenate([ok, ok], axis=0)
        for p in range(cw // 128):
            lanes = slice(p * 128, (p + 1) * 128)
            q = two_heads(rq[rows, lanes])
            k, v = ext[:, lanes], ext[:, cw + p * 128 : cw + (p + 1) * 128]
            scores = jnp.where(ok, mm(q, k, NT) * HEAD ** (-0.5), NEGATIVE)
            top = jnp.max(scores, axis=-1, keepdims=True)
            log_total = top + jnp.log(jnp.sum(jnp.exp(scores - top), axis=-1, keepdims=True))
            prob = jnp.exp(scores - log_total).astype(BF)
            out[rows, lanes] = one_pair(mm(prob, v), T).astype(BF)
            total[rows, 2 * p : 2 * p + 1] = log_total[:T]
            total[rows, 2 * p + 1 : 2 * p + 2] = log_total[T:]


def attend_back_kernel(S, T, *refs):
    rq, kv, before, after, mask, total, cos, sin = refs[:8]
    d_mix = refs[8 : 8 + S]
    dq, dkv, to_left, to_right, ext = refs[8 + S :]
    cw = rq.shape[1]
    for m in range(S):
        rows = slice(m * T, (m + 1) * T)
        extend(m, T, kv, before, after, ext)
        ok = mask[rows, :] > 0.0
        ok = jnp.concatenate([ok, ok], axis=0)
        for p in range(cw // 128):
            ks = slice(p * 128, (p + 1) * 128)
            vs = slice(cw + p * 128, cw + (p + 1) * 128)
            q, d = two_heads(rq[rows, ks]), two_heads(d_mix[m][:, ks])
            k, v = ext[:, ks], ext[:, vs]
            log_total = jnp.concatenate(
                [total[rows, 2 * p : 2 * p + 1], total[rows, 2 * p + 1 : 2 * p + 2]], axis=0
            )
            scores = jnp.where(ok, mm(q, k, NT) * HEAD ** (-0.5), NEGATIVE)
            prob = jnp.exp(scores - log_total)
            d_prob = mm(d, v, NT)
            delta = jnp.sum(prob * d_prob, axis=-1, keepdims=True)
            d_score = (prob * (d_prob - delta)).astype(BF)
            d_val = mm(prob.astype(BF), d, TN)
            d_key = mm(d_score, q, TN) * HEAD ** (-0.5)
            g = one_pair(mm(d_score, k), T) * HEAD ** (-0.5)
            dq[rows, ks] = turned(g, cos[rows, :], -sin[rows, :]).astype(BF)
            for sl, g in ((ks, d_key), (vs, d_val)):
                to_left[m, :, sl] = g[:WINDOW].astype(BF)
                dkv[rows, sl] = g[WINDOW : WINDOW + T]
                to_right[m, :, sl] = g[WINDOW + T :].astype(BF)


def late_weights_kernel(S, hb, sc, *refs):
    im, io, om, oo = (refs[i * S : (i + 1) * S] for i in range(4))
    gate, lin, outw = refs[4 * S :]
    in_order(S, hb, sc, False, [r.at[:hb] for r in im], [r.at[:hb] for r in io], gate)
    in_order(S, hb, sc, False, [r.at[hb:] for r in im], [r.at[hb:] for r in io], lin)
    in_order(S, hb, sc, True, om, oo, outw)


def up_kernel(S, T, *refs):
    x = refs[:S]
    att = refs[S : 2 * S]
    outw, gain, gate_w, lin_w = refs[2 * S : 2 * S + 4]
    resid_own, h, gate_in, lin, mixed = refs[2 * S + 4 :]
    cw = att[0].shape[1]
    for m in range(S):
        for j in range(S):
            part = att[j][(m ^ j) * T : ((m ^ j) + 1) * T, :]
            mixed[m * T : (m + 1) * T, j * cw : (j + 1) * cw] = part
    summed = mm(mixed[...], outw[...])
    for m in range(S):
        resid = x[m][:T, :].astype(F32) + summed[m * T : (m + 1) * T]
        if m == 0:
            resid_own[...] = resid
        normed, _ = norm(resid)
        h[m * T : (m + 1) * T, :] = (normed * gain[...]).astype(BF)
    gate_in[...] = mm(h[...], gate_w[...])
    lin[...] = mm(h[...], lin_w[...])


def up_back_kernel(S, T, *refs):
    og = refs[:S]
    gate_in, lin, down, gate_w, lin_w = refs[S : S + 5]
    act, d_gate, d_lin = refs[S + 5 : S + 8]
    pieces = refs[S + 8 : 2 * S + 8]
    both = refs[2 * S + 8]
    for m in range(S):
        both[m * T : (m + 1) * T, :] = og[m][...]
    d_act = mm(both[...], down[...], NT)
    gate, ln = gate_in[...], lin[...]
    cdf = 0.5 * (1.0 + lax.erf(gate * 2.0 ** (-0.5)))
    pdf = jnp.exp(-0.5 * gate * gate) * (2.0 * math.pi) ** (-0.5)
    gelu = gate * cdf
    act[...] = (gelu * ln).astype(BF)
    d_gate[...] = (d_act * ln * (cdf + gate * pdf)).astype(BF)
    d_lin[...] = (d_act * gelu).astype(BF)
    part = mm(d_gate[...], gate_w[...], NT) + mm(d_lin[...], lin_w[...], NT)
    for m in range(S):
        pieces[m][...] = part[m * T : (m + 1) * T].astype(BF)


def resid_back_kernel(S, *refs):
    parts = refs[:S]
    resid, gain, grad, outw = refs[S : S + 4]
    d_resid, d_resid_b, gain_g = refs[S + 4 : S + 7]
    pieces = refs[S + 7 :]
    d_h = parts[0][...].astype(F32)
    for m in range(1, S):
        d_h = d_h + parts[m][...].astype(F32)
    normed, inv_std = norm(resid[...])
    gain_g[...] = jnp.sum(d_h * normed, axis=0, keepdims=True)
    dr = grad[...].astype(F32) + norm_back(d_h * gain[...], normed, inv_std)
    d_resid[...] = dr
    db = dr.astype(BF)
    d_resid_b[...] = db
    cw = pieces[0].shape[1]
    d_att = mm(db, outw[...], NT)
    for m in range(S):
        pieces[m][...] = d_att[:, m * cw : (m + 1) * cw].astype(BF)


def down_grad_kernel(S, T, sc, act, *refs):
    og, (send, keep, both) = refs[:S], refs[S:]
    half = send.shape[1]
    for m in range(S):
        both[m * T : (m + 1) * T, :] = og[m][...]
    for ref, part in ((send, 1 - sc[1]), (keep, sc[1])):
        ref[...] = mm(act[...], both[:, at(part * half, half)], TN).astype(BF)


def in_grad_kernel(S, hb, sc, h, d_gate, d_lin, send, keep, grad):
    fs = d_gate.shape[1]
    for i, d in enumerate((d_gate, d_lin)):
        grad[...] = mm(d[...], h[...], TN)
        for m in range(S):
            for ref, half in ((send, 1 - sc[1]), (keep, sc[1])):
                block = pick(grad, (sc[0] ^ m) * 2 + half, hb)
                ref[i * fs : (i + 1) * fs, m * hb : (m + 1) * hb] = block.astype(BF)


def out_grad_kernel(S, T, sc, att, *refs):
    drb, (send, keep, both, grad) = refs[:S], refs[S:]
    hb = send.shape[1]
    for m in range(S):
        both[m * T : (m + 1) * T, :] = drb[m][...]
    grad[...] = mm(both[...], att[...], TN)
    send[...] = pick(grad, 1 - sc[1], hb).astype(BF)
    keep[...] = pick(grad, sc[1], hb).astype(BF)


def out_parts_kernel(S, T, act, down, *pieces):
    out = mm(act[...], down[...])
    for m in range(S):
        pieces[m][...] = out[m * T : (m + 1) * T].astype(BF)


def qkv_back_kernel(S, T, hb, sc, *refs):
    x = refs[:S]
    dq, dkv, from_left, from_right, cos, sin, h, wnat, gain_m_g = refs[S : S + 9]
    send, keep = refs[S + 9 : S + 11]
    pieces = refs[S + 11 : 2 * S + 11]
    d_qkv, grad, gain_row = refs[2 * S + 11 :]
    cw = dq.shape[1]
    d_qkv[:, :cw] = dq[...]
    for m in range(S):
        for start, edge in ((m * T, from_left), ((m + 1) * T - WINDOW, from_right)):
            rows = slice(start, start + WINDOW)
            dkv[rows, :] = dkv[rows, :] + edge[m].astype(F32)
    d_qkv[:, cw : 2 * cw] = turned(dkv[:, :cw], cos[...], -sin[...]).astype(BF)
    d_qkv[:, 2 * cw :] = dkv[:, cw:].astype(BF)
    grad[...] = mm(d_qkv[...], h[...], TN)
    d_h = mm(d_qkv[...], wnat[...], NT)
    total = None
    for m in range(S):
        part = d_h[m * T : (m + 1) * T]
        pieces[m][...] = part.astype(BF)
        normed, _ = norm(x[m][:T, :].astype(F32))
        part = jnp.sum(part * normed, axis=0, keepdims=True)
        total = part if total is None else total + part
    gain_row[0:1, :] = total
    gain_row[1:2, :] = gain_m_g[...]
    row = lax.broadcasted_iota(jnp.int32, (TAIL, hb), 0)
    for m in range(S):
        lanes = slice(m * hb, (m + 1) * hb)
        base = (sc[0] ^ m) * 2
        tail = jnp.zeros((TAIL, hb), F32)
        for i in range(4):
            line = pick(gain_row, base + i % 2, hb)[i // 2 : i // 2 + 1]
            tail = jnp.where(row == i, jnp.broadcast_to(line, tail.shape), tail)
        for ref, half in ((send, 1 - sc[1]), (keep, sc[1])):
            ref[: 3 * cw, lanes] = pick(grad, base + half, hb).astype(BF)
            ref[3 * cw :, lanes] = tail.astype(BF)


def pair_sum_kernel(S, hb, keep, got, *pieces):
    for m in range(S):
        lanes = slice(m * hb, (m + 1) * hb)
        pieces[m][...] = keep[:, lanes] + got[:, lanes]


def down_halves_kernel(sc, keep, got, send_z, keep_z):
    half = send_z.shape[1]
    for ref, part in ((send_z, 1 - sc[2]), (keep_z, sc[2])):
        cols = at(part * half, half)
        ref[...] = keep[:, cols] + got[:, cols]


def slot_halves_kernel(S, sc, *refs):
    slots, extra, (send_z, keep_z) = refs[:S], refs[S:-2], refs[-2:]
    rows, hb = slots[0].shape
    half = S // 2
    low = (sc[2] == 0).astype(F32).astype(BF)
    high = (sc[2] == 1).astype(F32).astype(BF)
    for k in range(half):
        a, b = slots[k][...], slots[half + k][...]
        lanes = slice(k * hb, (k + 1) * hb)
        keep_z[:rows, lanes] = a * low + b * high
        send_z[:rows, lanes] = a * high + b * low
    if extra:
        size = extra[0].shape[0] // S
        for k in range(half):
            a, b = (
                extra[0][i * size : (i + 1) * size, :] + extra[1][i * size : (i + 1) * size, :]
                for i in (k, half + k)
            )
            lanes = slice(k * hb, (k + 1) * hb)
            keep_z[rows:, lanes] = a * low + b * high
            send_z[rows:, lanes] = a * high + b * low


def in_back_kernel(S, *refs):
    parts = refs[:S]
    x, gain, d_resid, out = refs[S:]
    d_h = parts[0][...].astype(F32)
    for m in range(1, S):
        d_h = d_h + parts[m][...].astype(F32)
    normed, inv_std = norm(x[...].astype(F32))
    out[...] = d_resid[...] + norm_back(d_h * gain[...], normed, inv_std)


def down_final_kernel(sc, own, far, own_o, far_o, out):
    half = own.shape[1]
    for part, a, b in ((sc[1], own, far), (1 - sc[1], own_o, far_o)):
        out[:, at((2 * part + sc[2]) * half, half)] = a[...].astype(F32)
        out[:, at((2 * part + 1 - sc[2]) * half, half)] = b[...].astype(F32)


def unit(n):
    rows = lax.broadcasted_iota(jnp.int32, (n, n), 0)
    return jnp.where(rows == lax.broadcasted_iota(jnp.int32, (n, n), 1), 1.0, 0.0).astype(BF)


def in_final_kernel(S, hb, sc, own, far, own_o, far_o, out):
    half = S // 2
    fs = own.shape[0] // 2
    eye = unit(hb)
    for j in range(S):
        m = sc[0] ^ j
        here = (m // half == sc[2]).astype(F32).astype(BF)
        there = (m // half != sc[2]).astype(F32).astype(BF)
        for part, a, b in ((sc[1], own, far), (1 - sc[1], own_o, far_o)):
            block = mm(eye, pick(a, m % half, hb) * here + pick(b, m % half, hb) * there, NT)
            for i in range(2):
                start = (i * S + j) * fs
                out[at(part * hb, hb), start : start + fs] = block[:, i * fs : (i + 1) * fs]


def qkv_final_kernel(S, hb, sc, own, far, own_o, far_o, out, wout, gain_a, gain_m):
    half = S // 2
    D = wout.shape[1]
    cw = D // S
    eye = unit(hb)
    low = (sc[2] == 0).astype(F32).astype(BF)
    high = (sc[2] == 1).astype(F32).astype(BF)
    rows = 3 * cw + TAIL
    total = None
    for part, a, b in ((sc[1], own, far), (1 - sc[1], own_o, far_o)):
        for m in range(S):
            lanes = slice((m % half) * hb, (m % half + 1) * hb)
            p, q = (low, high) if m < half else (high, low)
            block = a[:, lanes] * p + b[:, lanes] * q
            grad = mm(eye, block[: 3 * cw], NT)
            for i in range(3):
                cols = at(i * D + (sc[0] ^ m) * cw, cw)
                out[at(part * hb, hb), cols] = grad[:, i * cw : (i + 1) * cw]
            wout[at(part * hb, hb), m * cw : (m + 1) * cw] = mm(eye, block[rows:], NT)
            if a is own:
                tail = block[3 * cw : rows].astype(F32)
                total = tail if total is None else total + tail
    gain_a[:, :hb], gain_a[:, hb:] = total[0:1], total[1:2]
    gain_m[:, :hb], gain_m[:, hb:] = total[2:3], total[3:4]


def after(values, *others):
    flat, tree = jax.tree.flatten(values)
    rest = jax.tree.leaves(others)
    out = lax.optimization_barrier(tuple(flat) + tuple(rest))
    return jax.tree.unflatten(tree, out[: len(flat)])


def shards(
    block_in,
    doc_lengths,
    qkv_weight,
    out_weight,
    in_weight,
    down_weight,
    attn_gain,
    mlp_gain,
    out_grad,
):
    S, Q = lax.axis_size("shard"), lax.axis_size("seq")
    Z = Q // 2
    s, q = lax.axis_index("shard"), lax.axis_index("seq")
    c, z = q % 2, q // 2
    kz = ((z + 1) // 2) % 2 if Z == 4 else 0 * z
    sc = jnp.stack([s, c, kz]).astype(jnp.int32)
    T, D = block_in.shape[1:]
    cw = D // S
    hb = D // S // 2
    ff = in_weight.shape[1] // 2
    fs = ff // S

    def peer(x, m):
        return lax.ppermute(x, "shard", [(i, i ^ m) for i in range(S)])

    def core_swap(x):
        return lax.ppermute(x, "seq", [(i, i ^ 1) for i in range(Q)])

    def along(x, pairs):
        both = [(2 * a + e, 2 * b + e) for a, b in pairs for e in (0, 1)]
        return lax.ppermute(x, "seq", both)

    def shift(x, step):
        pairs = [(i, i + step) for i in range(Q) if 0 <= i + step < Q]
        return lax.ppermute(x, "seq", pairs)

    def gather(x):
        return [x] + [peer(x, m) for m in range(1, S)]

    def swap_out(pieces):
        return [pieces[0]] + [peer(pieces[m], m) for m in range(1, S)]

    def line_sum(x):
        half = Z // 2
        for k in range(half - 1):
            x = x + along(x, [(k, k + 1), (Z - 1 - k, Z - 2 - k)])
        if Z > 1:
            x = x + along(x, [(half - 1, half), (half, half - 1)])
        for k in range(half - 1, 0, -1):
            got = along(x, [(k, k - 1), (Z - 1 - k, Z - k)])
            x = jnp.where((z == k - 1) | (z == Z - k), got, x)
        return x

    def z_sum(send, keep):
        if Z == 4:
            near = [(i, i ^ 1) for i in range(Z)]
            part = keep + along(send, near)
            own = part + along(part, [(i, Z - 1 - i) for i in range(Z)])
            far = along(own, near)
        else:
            own, far = line_sum(keep), line_sum(send)
        return own, far, core_swap(own), core_swap(far)

    def cols(w, start, size):
        return lax.dynamic_slice_in_dim(w, start, size, axis=1)

    x_own = block_in[0]
    row = jnp.concatenate(
        [attn_gain, mlp_gain, (doc_lengths[0] // 64).astype(BF), (doc_lengths[0] % 64).astype(BF)]
    )
    docs = doc_lengths.shape[1]
    rows = jnp.pad(row[None], ((0, TAIL - 1), (0, D - row.shape[0])))
    x = gather(jnp.concatenate([x_own, rows], axis=0))

    qkv_half = lax.dynamic_slice_in_dim(qkv_weight, c * hb, hb, axis=0)
    qkv_pieces = [
        jnp.concatenate([cols(qkv_half, i * D + (s ^ m) * cw, cw) for i in range(3)], axis=1)
        for m in range(S)
    ]
    wm = swap_out(qkv_pieces)
    wo = [core_swap(w) for w in wm]

    in_half = lax.dynamic_slice_in_dim(in_weight, c * hb, hb, axis=0)
    out_half = lax.dynamic_slice_in_dim(out_weight, c * hb, hb, axis=0)
    in_pieces = [
        jnp.concatenate([cols(in_half, i * ff + (s ^ m) * fs, fs) for i in range(2)], axis=0)
        for m in range(S)
    ]
    in_pieces, out_half = after((in_pieces, out_half), wm)
    im = swap_out(in_pieces)
    om = gather(out_half)
    io = [core_swap(w) for w in im]
    oo = [core_swap(w) for w in om]

    tails = jnp.stack([p[T, 4 * hb : 4 * hb + 2 * docs] for p in x]).astype(jnp.int32)
    lengths = tails[:, :docs] * 64 + tails[:, docs:]
    ends = jnp.cumsum(lengths, axis=1)
    key_spots = q * T - WINDOW + jnp.arange(T + 2 * WINDOW, dtype=jnp.int32)
    passed = ends[:, :, None] <= key_spots[None, None, :]
    key_segment = jnp.sum(passed.astype(jnp.int32), axis=1)
    start = jnp.sum(jnp.where(passed, lengths[:, :, None], 0), axis=1)
    position = (key_spots[None] - start)[:, WINDOW : WINDOW + T]
    segment = key_segment[:, WINDOW : WINDOW + T]
    spots = key_spots[WINDOW : WINDOW + T]
    near = jnp.abs(spots[:, None] - key_spots[None, :]) <= WINDOW
    valid = (key_spots >= 0) & (key_spots < Q * T)
    mask = (segment[:, :, None] == key_segment[:, None, :]) & (near & valid[None, :])[None]
    mask = mask.astype(F32).reshape(S * T, T + 2 * WINDOW)
    half = HEAD // 2
    freq = jnp.power(10000.0, -(jnp.arange(half).astype(F32) * (2.0 / HEAD)))
    angle = position.reshape(S * T, 1).astype(F32) * freq[None, :]
    cos_h, sin_h = jnp.cos(angle), jnp.sin(angle)
    cos = jnp.concatenate([cos_h] * 4, axis=1)
    sin = jnp.concatenate([-sin_h, sin_h] * 2, axis=1)

    h_attn, rq, kv, lead, last, wnat, gain_a, gain_m = call(
        functools.partial(qkv_kernel, S, T, hb),
        (
            sds((S * T, D), BF),
            sds((S * T, cw), BF),
            sds((S * T, 2 * cw), BF),
            sds((S, WINDOW, 2 * cw), BF),
            sds((S, WINDOW, 2 * cw), BF),
            sds((D, 3 * cw), BF),
            sds((1, D), F32),
            sds((1, D), F32),
        ),
        *x,
        *wm,
        *wo,
        cos,
        sin,
        scalars=sc,
    )
    before_kv, after_kv = shift(last, 1), shift(lead, -1)
    ext = pltpu.VMEM((T + 2 * WINDOW, 2 * cw), BF)
    att_own, total = call(
        functools.partial(attend_kernel, S, T),
        (sds((S * T, cw), BF), sds((S * T, cw // HEAD), F32)),
        rq,
        kv,
        before_kv,
        after_kv,
        mask,
        scratch=[ext],
    )
    att = gather(att_own)

    g_own = after(out_grad[0], att_own)
    og = gather(g_own)
    gate_w, lin_w, outw = call(
        functools.partial(late_weights_kernel, S, hb),
        (sds((D, fs), BF), sds((D, fs), BF), sds((D, D), BF)),
        *im,
        *io,
        *om,
        *oo,
        scalars=sc,
    )
    resid_own, h_mlp, gate_in, lin = call(
        functools.partial(up_kernel, S, T),
        (sds((T, D), F32), sds((S * T, D), BF), sds((S * T, fs), F32), sds((S * T, fs), F32)),
        *x,
        *att,
        outw,
        gain_m,
        gate_w,
        lin_w,
        scratch=[pltpu.VMEM((S * T, D), BF)],
    )
    wide = pltpu.VMEM((S * T, D), BF)
    mid = call(
        functools.partial(up_back_kernel, S, T),
        (sds((S * T, fs), BF),) * 3 + (sds((T, D), BF),) * S,
        *og,
        gate_in,
        lin,
        down_weight,
        gate_w,
        lin_w,
        scratch=[wide],
    )
    act, d_gate, d_lin = mid[:3]
    d_hmlp = swap_out(mid[3:])

    down_send, down_keep = call(
        functools.partial(down_grad_kernel, S, T),
        (sds((fs, D // 2), BF),) * 2,
        act,
        *og,
        scalars=sc,
        scratch=[wide],
    )
    down_z = call(
        down_halves_kernel,
        (sds((fs, D // 4), BF),) * 2,
        down_keep,
        core_swap(down_send),
        scalars=sc,
    )
    down_sums = z_sum(*down_z)

    in_send, in_keep = call(
        functools.partial(in_grad_kernel, S, hb),
        (sds((2 * fs, D // 2), BF),) * 2,
        h_mlp,
        d_gate,
        d_lin,
        scalars=sc,
        scratch=[pltpu.VMEM((fs, D), F32)],
    )
    in_g = call(
        functools.partial(pair_sum_kernel, S, hb),
        (sds((2 * fs, hb), BF),) * S,
        in_keep,
        core_swap(in_send),
    )
    in_z = call(
        functools.partial(slot_halves_kernel, S),
        (sds((2 * fs, D // 4), BF),) * 2,
        *swap_out(in_g),
        scalars=sc,
    )
    in_sums = z_sum(*in_z)

    back = call(
        functools.partial(resid_back_kernel, S),
        (sds((T, D), F32), sds((T, D), BF), sds((1, D), F32)) + (sds((T, cw), BF),) * S,
        *d_hmlp,
        resid_own,
        gain_m,
        g_own,
        outw,
    )
    d_resid, d_resid_b, gain_m_g = back[:3]
    d_mix = swap_out(back[3:])

    out_parts = call(
        functools.partial(out_parts_kernel, S, T), (sds((T, D), BF),) * S, act, down_weight
    )
    out_parts = swap_out(out_parts)
    final = resid_own
    for p in out_parts:
        final = final + p.astype(F32)
    final = final.astype(BF)

    dq, dkv, to_left, to_right = call(
        functools.partial(attend_back_kernel, S, T),
        (
            sds((S * T, cw), BF),
            sds((S * T, 2 * cw), F32),
            sds((S, WINDOW, 2 * cw), BF),
            sds((S, WINDOW, 2 * cw), BF),
        ),
        rq,
        kv,
        before_kv,
        after_kv,
        mask,
        total,
        cos,
        sin,
        *d_mix,
        scratch=[ext],
    )
    from_right, from_left = shift(to_left, -1), shift(to_right, 1)

    drb = gather(d_resid_b)
    out_send, out_keep = call(
        functools.partial(out_grad_kernel, S, T),
        (sds((D, hb), BF),) * 2,
        att_own,
        *drb,
        scalars=sc,
        scratch=[wide, pltpu.VMEM((D, cw), F32)],
    )
    out_got = core_swap(out_send)

    res = call(
        functools.partial(qkv_back_kernel, S, T, hb),
        (sds((3 * cw + TAIL, D // 2), BF),) * 2 + (sds((T, D), BF),) * S,
        *x,
        dq,
        dkv,
        from_left,
        from_right,
        cos,
        sin,
        h_attn,
        wnat,
        gain_m_g,
        scalars=sc,
        scratch=[
            pltpu.VMEM((S * T, 3 * cw), BF),
            pltpu.VMEM((3 * cw, D), F32),
            pltpu.VMEM((2, D), F32),
        ],
    )
    qkv_g = call(
        functools.partial(pair_sum_kernel, S, hb),
        (sds((3 * cw + TAIL, hb), BF),) * S,
        res[1],
        core_swap(res[0]),
    )
    qkv_z = call(
        functools.partial(slot_halves_kernel, S),
        (sds((3 * cw + TAIL + D // S, D // 4), BF),) * 2,
        *swap_out(qkv_g),
        out_keep,
        out_got,
        scalars=sc,
    )
    qkv_sums = z_sum(*qkv_z)
    d_hattn = swap_out(res[2:])

    in_rows = call(
        functools.partial(in_back_kernel, S), sds((T, D), F32), *d_hattn, x_own, gain_a, d_resid
    )

    down_grad = call(down_final_kernel, sds((fs, D), F32), *down_sums, scalars=sc)
    in_grad = call(
        functools.partial(in_final_kernel, S, hb), sds((2 * hb, 2 * ff), F32), *in_sums, scalars=sc
    )
    qkv_grad, out_wgrad, gain_a_grad, gain_m_grad = call(
        functools.partial(qkv_final_kernel, S, hb),
        (
            sds((2 * hb, 3 * D), F32),
            sds((2 * hb, D), F32),
            sds((1, 2 * hb), F32),
            sds((1, 2 * hb), F32),
        ),
        *qkv_sums,
        scalars=sc,
    )
    return (
        final[None],
        in_rows[None],
        qkv_grad,
        out_wgrad,
        in_grad,
        down_grad,
        gain_a_grad[0],
        gain_m_grad[0],
    )


def solution(mesh):
    rows = P("shard", "seq", None)
    mat = P("shard", None)
    vec = P("shard")

    return jax.shard_map(
        shards,
        mesh=mesh,
        in_specs=(rows, mat, mat, mat, mat, mat, vec, vec, rows),
        out_specs=(rows, rows, mat, mat, mat, mat, vec, vec),
        check_vma=False,
    )
```

```python
import functools
import math

import jax
import jax.numpy as jnp
from jax import lax
from jax.experimental import pallas as pl
from jax.experimental.pallas import tpu as pltpu
from jax.sharding import PartitionSpec as P


HEAD = 64
WINDOW = 64
EPSILON = 1e-05
NEGATIVE = -1e30
BF = jnp.bfloat16
F32 = jnp.float32
TAIL = 16
NT = ((1,), (1,))
TN = ((0,), (0,))


def mm(a, b, dims=((1,), (0,))):
    return lax.dot_general(a, b, (dims, ((), ())), preferred_element_type=F32)


def call(kernel, out_shape, *args, scalars=None, scratch=()):
    vmem = pl.BlockSpec(memory_space=pltpu.VMEM)
    specs = [vmem] * len(args)
    if scalars is not None:
        specs = [pl.BlockSpec(memory_space=pltpu.SMEM)] + specs
        args = (scalars,) + tuple(args)
    return pl.pallas_call(
        kernel,
        out_shape=out_shape,
        in_specs=specs,
        out_specs=jax.tree.map(lambda _: vmem, out_shape),
        scratch_shapes=list(scratch),
        compiler_params=pltpu.CompilerParams(vmem_limit_bytes=58 << 20),
    )(*args)


def sds(shape, dtype):
    return jax.ShapeDtypeStruct(shape, dtype)


def norm(values):
    centered = values - jnp.mean(values, axis=-1, keepdims=True)
    variance = jnp.mean(centered * centered, axis=-1, keepdims=True)
    inv_std = lax.rsqrt(variance + EPSILON)
    return centered * inv_std, inv_std


def norm_back(scaled, normed, inv_std):
    return inv_std * (
        scaled
        - jnp.mean(scaled, axis=-1, keepdims=True)
        - normed * jnp.mean(scaled * normed, axis=-1, keepdims=True)
    )


def swap_halves(x):
    half = HEAD // 2
    lane = lax.broadcasted_iota(jnp.int32, x.shape, 1)
    return jnp.where(lane % HEAD < half, pltpu.roll(x, 128 - half, 1), pltpu.roll(x, half, 1))


def turned(x, cos, sin):
    blocks = [x[:, i : i + 128] for i in range(0, x.shape[1], 128)]
    return jnp.concatenate([b * cos + swap_halves(b) * sin for b in blocks], axis=1)


def at(start, size):
    return pl.ds(pl.multiple_of(start, size), size)


def pick(ref, index, size):
    if size % 128 == 0:
        return ref[:, at(index * size, size)]
    two = ref[:, at(index // 2 * (2 * size), 2 * size)]
    return jnp.where(index % 2 == 0, two[:, :size], two[:, size:])


def in_order(S, hb, sc, relative, mine, other, out):
    s, c = sc[0], sc[1]
    for m in range(S):
        base = (m if relative else (s ^ m)) * (2 * hb)
        out[at(base + c * hb, hb), :] = mine[m][...]
        out[at(base + (1 - c) * hb, hb), :] = other[m][...]


def qkv_kernel(S, T, hb, sc, *refs):
    x, wm, wo, misc = (refs[i * S : (i + 1) * S] for i in range(4))
    cos, sin = refs[4 * S : 4 * S + 2]
    h, rq, kv, lead, last, wnat, gain_a, gain_m = refs[4 * S + 2 :]
    in_order(S, hb, sc, False, wm, wo, wnat)
    cw = rq.shape[1]
    for m in range(S):
        rows = misc[m][...].astype(F32)
        cols = at((sc[0] ^ m) * (2 * hb), 2 * hb)
        gain_a[:, cols] = rows[0:1, : 2 * hb]
        gain_m[:, cols] = rows[0:1, 2 * hb : 4 * hb]
    for m in range(S):
        normed, _ = norm(x[m][...].astype(F32))
        h[m * T : (m + 1) * T, :] = (normed * gain_a[...]).astype(BF)
    act = mm(h[...], wnat[...])
    rq[...] = turned(act[:, :cw], cos[...], sin[...]).astype(BF)
    kv[:, :cw] = turned(act[:, cw : 2 * cw], cos[...], sin[...]).astype(BF)
    kv[:, cw:] = act[:, 2 * cw :].astype(BF)
    for m in range(S):
        lead[m] = kv[m * T : m * T + WINDOW, :]
        last[m] = kv[(m + 1) * T - WINDOW : (m + 1) * T, :]


def two_heads(x):
    lane = lax.broadcasted_iota(jnp.int32, x.shape, 1)
    first = jnp.where(lane < HEAD, 1.0, 0.0).astype(x.dtype)
    return jnp.concatenate([x * first, x * (1 - first).astype(x.dtype)], axis=0)


def one_pair(x, T):
    lane = lax.broadcasted_iota(jnp.int32, (T, 128), 1)
    return jnp.where(lane < HEAD, x[:T], x[T:])


def extend(m, T, kv, before, after, ext):
    ext[:WINDOW, :] = before[m]
    ext[WINDOW : WINDOW + T, :] = kv[m * T : (m + 1) * T, :]
    ext[WINDOW + T :, :] = after[m]


def attend_kernel(S, T, rq, kv, before, after, mask, out, total, ext):
    cw = rq.shape[1]
    for m in range(S):
        rows = slice(m * T, (m + 1) * T)
        extend(m, T, kv, before, after, ext)
        ok = mask[rows, :] > 0.0
        ok = jnp.concatenate([ok, ok], axis=0)
        for p in range(cw // 128):
            lanes = slice(p * 128, (p + 1) * 128)
            q = two_heads(rq[rows, lanes])
            k, v = ext[:, lanes], ext[:, cw + p * 128 : cw + (p + 1) * 128]
            scores = jnp.where(ok, mm(q, k, NT) * HEAD ** (-0.5), NEGATIVE)
            top = jnp.max(scores, axis=-1, keepdims=True)
            log_total = top + jnp.log(jnp.sum(jnp.exp(scores - top), axis=-1, keepdims=True))
            prob = jnp.exp(scores - log_total).astype(BF)
            out[rows, lanes] = one_pair(mm(prob, v), T).astype(BF)
            total[rows, 2 * p : 2 * p + 1] = log_total[:T]
            total[rows, 2 * p + 1 : 2 * p + 2] = log_total[T:]


def attend_back_kernel(S, T, *refs):
    rq, kv, before, after, mask, total, cos, sin = refs[:8]
    d_mix = refs[8 : 8 + S]
    dq, dkv, to_left, to_right, ext = refs[8 + S :]
    cw = rq.shape[1]
    for m in range(S):
        rows = slice(m * T, (m + 1) * T)
        extend(m, T, kv, before, after, ext)
        ok = mask[rows, :] > 0.0
        ok = jnp.concatenate([ok, ok], axis=0)
        for p in range(cw // 128):
            ks = slice(p * 128, (p + 1) * 128)
            vs = slice(cw + p * 128, cw + (p + 1) * 128)
            q, d = two_heads(rq[rows, ks]), two_heads(d_mix[m][:, ks])
            k, v = ext[:, ks], ext[:, vs]
            log_total = jnp.concatenate(
                [total[rows, 2 * p : 2 * p + 1], total[rows, 2 * p + 1 : 2 * p + 2]], axis=0
            )
            scores = jnp.where(ok, mm(q, k, NT) * HEAD ** (-0.5), NEGATIVE)
            prob = jnp.exp(scores - log_total)
            d_prob = mm(d, v, NT)
            delta = jnp.sum(prob * d_prob, axis=-1, keepdims=True)
            d_score = (prob * (d_prob - delta)).astype(BF)
            d_val = mm(prob.astype(BF), d, TN)
            d_key = mm(d_score, q, TN) * HEAD ** (-0.5)
            g = one_pair(mm(d_score, k), T) * HEAD ** (-0.5)
            dq[rows, ks] = turned(g, cos[rows, :], -sin[rows, :]).astype(BF)
            for sl, g in ((ks, d_key), (vs, d_val)):
                to_left[m, :, sl] = g[:WINDOW].astype(BF)
                dkv[rows, sl] = g[WINDOW : WINDOW + T]
                to_right[m, :, sl] = g[WINDOW + T :].astype(BF)


def late_weights_kernel(S, hb, sc, *refs):
    im, io, om, oo = (refs[i * S : (i + 1) * S] for i in range(4))
    gate, lin, outw = refs[4 * S :]
    in_order(S, hb, sc, False, [r.at[:hb] for r in im], [r.at[:hb] for r in io], gate)
    in_order(S, hb, sc, False, [r.at[hb:] for r in im], [r.at[hb:] for r in io], lin)
    in_order(S, hb, sc, True, om, oo, outw)


def up_kernel(S, T, *refs):
    x = refs[:S]
    att = refs[S : 2 * S]
    outw, gain, gate_w, lin_w = refs[2 * S : 2 * S + 4]
    resid_own, h, gate_in, lin, mixed = refs[2 * S + 4 :]
    cw = att[0].shape[1]
    for m in range(S):
        for j in range(S):
            part = att[j][(m ^ j) * T : ((m ^ j) + 1) * T, :]
            mixed[m * T : (m + 1) * T, j * cw : (j + 1) * cw] = part
    summed = mm(mixed[...], outw[...])
    for m in range(S):
        resid = x[m][...].astype(F32) + summed[m * T : (m + 1) * T]
        if m == 0:
            resid_own[...] = resid
        normed, _ = norm(resid)
        h[m * T : (m + 1) * T, :] = (normed * gain[...]).astype(BF)
    gate_in[...] = mm(h[...], gate_w[...])
    lin[...] = mm(h[...], lin_w[...])


def up_back_kernel(S, T, *refs):
    og = refs[:S]
    gate_in, lin, down, gate_w, lin_w = refs[S : S + 5]
    act, d_gate, d_lin = refs[S + 5 : S + 8]
    pieces = refs[S + 8 : 2 * S + 8]
    both = refs[2 * S + 8]
    for m in range(S):
        both[m * T : (m + 1) * T, :] = og[m][...]
    d_act = mm(both[...], down[...], NT)
    gate, ln = gate_in[...], lin[...]
    cdf = 0.5 * (1.0 + lax.erf(gate * 2.0 ** (-0.5)))
    pdf = jnp.exp(-0.5 * gate * gate) * (2.0 * math.pi) ** (-0.5)
    gelu = gate * cdf
    act[...] = (gelu * ln).astype(BF)
    d_gate[...] = (d_act * ln * (cdf + gate * pdf)).astype(BF)
    d_lin[...] = (d_act * gelu).astype(BF)
    part = mm(d_gate[...], gate_w[...], NT) + mm(d_lin[...], lin_w[...], NT)
    for m in range(S):
        pieces[m][...] = part[m * T : (m + 1) * T].astype(BF)


def resid_back_kernel(S, *refs):
    parts = refs[:S]
    resid, gain, grad, outw = refs[S : S + 4]
    d_resid, d_resid_b, gain_g = refs[S + 4 : S + 7]
    pieces = refs[S + 7 :]
    d_h = parts[0][...].astype(F32)
    for m in range(1, S):
        d_h = d_h + parts[m][...].astype(F32)
    normed, inv_std = norm(resid[...])
    gain_g[...] = jnp.sum(d_h * normed, axis=0, keepdims=True)
    dr = grad[...].astype(F32) + norm_back(d_h * gain[...], normed, inv_std)
    d_resid[...] = dr
    db = dr.astype(BF)
    d_resid_b[...] = db
    cw = pieces[0].shape[1]
    d_att = mm(db, outw[...], NT)
    for m in range(S):
        pieces[m][...] = d_att[:, m * cw : (m + 1) * cw].astype(BF)


def down_grad_kernel(S, T, sc, act, *refs):
    og, (send, keep, both) = refs[:S], refs[S:]
    half = send.shape[1]
    for m in range(S):
        both[m * T : (m + 1) * T, :] = og[m][...]
    for ref, part in ((send, 1 - sc[1]), (keep, sc[1])):
        ref[...] = mm(act[...], both[:, at(part * half, half)], TN).astype(BF)


def in_grad_kernel(S, hb, sc, h, d_gate, d_lin, send, keep, grad):
    fs = d_gate.shape[1]
    for i, d in enumerate((d_gate, d_lin)):
        grad[...] = mm(d[...], h[...], TN)
        for m in range(S):
            for ref, half in ((send, 1 - sc[1]), (keep, sc[1])):
                block = pick(grad, (sc[0] ^ m) * 2 + half, hb)
                ref[i * fs : (i + 1) * fs, m * hb : (m + 1) * hb] = block.astype(BF)


def out_grad_kernel(S, T, sc, att, *refs):
    drb, (send, keep, both, grad) = refs[:S], refs[S:]
    hb = send.shape[1]
    for m in range(S):
        both[m * T : (m + 1) * T, :] = drb[m][...]
    grad[...] = mm(both[...], att[...], TN)
    send[...] = pick(grad, 1 - sc[1], hb).astype(BF)
    keep[...] = pick(grad, sc[1], hb).astype(BF)


def out_parts_kernel(S, T, act, down, *pieces):
    out = mm(act[...], down[...])
    for m in range(S):
        pieces[m][...] = out[m * T : (m + 1) * T].astype(BF)


def qkv_back_kernel(S, T, hb, sc, *refs):
    x = refs[:S]
    dq, dkv, from_left, from_right, cos, sin, h, wnat, gain_m_g = refs[S : S + 9]
    send, keep = refs[S + 9 : S + 11]
    pieces = refs[S + 11 : 2 * S + 11]
    d_qkv, grad, gain_row = refs[2 * S + 11 :]
    cw = dq.shape[1]
    d_qkv[:, :cw] = dq[...]
    for m in range(S):
        for start, edge in ((m * T, from_left), ((m + 1) * T - WINDOW, from_right)):
            rows = slice(start, start + WINDOW)
            dkv[rows, :] = dkv[rows, :] + edge[m].astype(F32)
    d_qkv[:, cw : 2 * cw] = turned(dkv[:, :cw], cos[...], -sin[...]).astype(BF)
    d_qkv[:, 2 * cw :] = dkv[:, cw:].astype(BF)
    grad[...] = mm(d_qkv[...], h[...], TN)
    d_h = mm(d_qkv[...], wnat[...], NT)
    total = None
    for m in range(S):
        part = d_h[m * T : (m + 1) * T]
        pieces[m][...] = part.astype(BF)
        normed, _ = norm(x[m][...].astype(F32))
        part = jnp.sum(part * normed, axis=0, keepdims=True)
        total = part if total is None else total + part
    gain_row[0:1, :] = total
    gain_row[1:2, :] = gain_m_g[...]
    row = lax.broadcasted_iota(jnp.int32, (TAIL, hb), 0)
    for m in range(S):
        lanes = slice(m * hb, (m + 1) * hb)
        base = (sc[0] ^ m) * 2
        tail = jnp.zeros((TAIL, hb), F32)
        for i in range(4):
            line = pick(gain_row, base + i % 2, hb)[i // 2 : i // 2 + 1]
            tail = jnp.where(row == i, jnp.broadcast_to(line, tail.shape), tail)
        for ref, half in ((send, 1 - sc[1]), (keep, sc[1])):
            ref[: 3 * cw, lanes] = pick(grad, base + half, hb).astype(BF)
            ref[3 * cw :, lanes] = tail.astype(BF)


def pair_sum_kernel(S, hb, keep, got, *pieces):
    for m in range(S):
        lanes = slice(m * hb, (m + 1) * hb)
        pieces[m][...] = keep[:, lanes] + got[:, lanes]


def lane_halves_kernel(sc, keep, got, send_z, keep_z):
    half = send_z.shape[1]
    for ref, part in ((send_z, 1 - sc[2]), (keep_z, sc[2])):
        cols = at(part * half, half)
        ref[...] = keep[:, cols] + got[:, cols]


def row_halves_kernel(sc, keep, got, send_z, keep_z):
    half = send_z.shape[0]
    for ref, part in ((send_z, 1 - sc[2]), (keep_z, sc[2])):
        rows = at(part * half, half)
        ref[...] = keep[rows, :] + got[rows, :]


def slot_halves_kernel(S, sc, *refs):
    slots, chunks = refs[:S], refs[S:]
    hb = slots[0].shape[1]
    half = S // 2
    low = (sc[2] == 0).astype(F32).astype(BF)
    high = (sc[2] == 1).astype(F32).astype(BF)
    start = 0
    for send_z, keep_z in (chunks[:2], chunks[2:]):
        stop = start + send_z.shape[0]
        for k in range(half):
            a, b = slots[k][start:stop, :], slots[half + k][start:stop, :]
            lanes = slice(k * hb, (k + 1) * hb)
            keep_z[:, lanes] = a * low + b * high
            send_z[:, lanes] = a * high + b * low
        start = stop


def in_back_kernel(S, *refs):
    parts = refs[:S]
    x, gain, d_resid, out = refs[S:]
    d_h = parts[0][...].astype(F32)
    for m in range(1, S):
        d_h = d_h + parts[m][...].astype(F32)
    normed, inv_std = norm(x[...].astype(F32))
    out[...] = d_resid[...] + norm_back(d_h * gain[...], normed, inv_std)


def down_final_kernel(sc, own, far, own_o, far_o, out):
    half = own.shape[1]
    for part, a, b in ((sc[1], own, far), (1 - sc[1], own_o, far_o)):
        out[:, at((2 * part + sc[2]) * half, half)] = a[...].astype(F32)
        out[:, at((2 * part + 1 - sc[2]) * half, half)] = b[...].astype(F32)


def unit(n):
    rows = lax.broadcasted_iota(jnp.int32, (n, n), 0)
    return jnp.where(rows == lax.broadcasted_iota(jnp.int32, (n, n), 1), 1.0, 0.0).astype(BF)


def in_final_kernel(S, hb, sc, *refs):
    out = refs[-1]
    half = S // 2
    fs = refs[0].shape[0] // 2
    eye = unit(hb)
    for j in range(S):
        m = sc[0] ^ j
        place = jnp.where(m // half == sc[2], 0, half) + m % half
        for part, parts in ((sc[1], refs[:S]), (1 - sc[1], refs[S : 2 * S])):
            block = parts[0][...] * (place == 0).astype(F32).astype(BF)
            for i in range(1, S):
                block = block + parts[i][...] * (place == i).astype(F32).astype(BF)
            block = mm(eye, block, NT)
            for i in range(2):
                start = (i * S + j) * fs
                out[at(part * hb, hb), start : start + fs] = block[:, i * fs : (i + 1) * fs]


def qkv_final_kernel(S, hb, sc, *refs):
    first, second, (out, gain_a, gain_m) = refs[:4], refs[4:8], refs[8:]
    half = S // 2
    D = out.shape[1] // 3
    cw = D // S
    eye = unit(hb)
    low = (sc[2] == 0).astype(F32).astype(BF)
    high = (sc[2] == 1).astype(F32).astype(BF)
    total = None
    for i, part in ((0, sc[1]), (2, 1 - sc[1])):
        for m in range(S):
            lanes = slice((m % half) * hb, (m % half + 1) * hb)
            p, q = (low, high) if m < half else (high, low)
            blocks = [r[i][:, lanes] * p + r[i + 1][:, lanes] * q for r in (first, second)]
            block = jnp.concatenate(blocks, axis=0)
            grad = mm(eye, block[: 3 * cw], NT)
            for k in range(3):
                cols = at(k * D + (sc[0] ^ m) * cw, cw)
                out[at(part * hb, hb), cols] = grad[:, k * cw : (k + 1) * cw]
            if i == 0:
                tail = block[3 * cw :].astype(F32)
                total = tail if total is None else total + tail
    gain_a[:, :hb], gain_a[:, hb:] = total[0:1], total[1:2]
    gain_m[:, :hb], gain_m[:, hb:] = total[2:3], total[3:4]


def out_final_kernel(hb, sc, own, far, own_o, far_o, out):
    half = own.shape[0]
    eye = unit(hb)
    for part, a, b in ((sc[1], own, far), (1 - sc[1], own_o, far_o)):
        out[at(part * hb, hb), at(sc[2] * half, half)] = mm(eye, a[...], NT)
        out[at(part * hb, hb), at((1 - sc[2]) * half, half)] = mm(eye, b[...], NT)


def after(values, *others):
    flat, tree = jax.tree.flatten(values)
    rest = jax.tree.leaves(others)
    out = lax.optimization_barrier(tuple(flat) + tuple(rest))
    return jax.tree.unflatten(tree, out[: len(flat)])


def shards(
    block_in,
    doc_lengths,
    qkv_weight,
    out_weight,
    in_weight,
    down_weight,
    attn_gain,
    mlp_gain,
    out_grad,
):
    S, Q = lax.axis_size("shard"), lax.axis_size("seq")
    Z = Q // 2
    s, q = lax.axis_index("shard"), lax.axis_index("seq")
    c, z = q % 2, q // 2
    kz = ((z + 1) // 2) % 2 if Z == 4 else 0 * z
    sc = jnp.stack([s, c, kz]).astype(jnp.int32)
    T, D = block_in.shape[1:]
    cw = D // S
    hb = D // S // 2
    ff = in_weight.shape[1] // 2
    fs = ff // S

    def permute(x, axis, pairs):
        return lax.ppermute(x, axis, pairs)

    def peer(x, m):
        return permute(x, "shard", [(i, i ^ m) for i in range(S)])

    def core_swap(x):
        return permute(x, "seq", [(i, i ^ 1) for i in range(Q)])

    def along(x, pairs):
        both = [(2 * a + e, 2 * b + e) for a, b in pairs for e in (0, 1)]
        return permute(x, "seq", both)

    def shift(x, step):
        pairs = [(i, i + step) for i in range(Q) if 0 <= i + step < Q]
        return permute(x, "seq", pairs)

    def gather(x):
        return [x] + [peer(x, m) for m in range(1, S)]

    def swap_out(pieces):
        return [pieces[0]] + [peer(pieces[m], m) for m in range(1, S)]

    def line_sum(x):
        half = Z // 2
        for k in range(half - 1):
            x = x + along(x, [(k, k + 1), (Z - 1 - k, Z - 2 - k)])
        if Z > 1:
            x = x + along(x, [(half - 1, half), (half, half - 1)])
        for k in range(half - 1, 0, -1):
            got = along(x, [(k, k - 1), (Z - 1 - k, Z - k)])
            x = jnp.where((z == k - 1) | (z == Z - k), got, x)
        return x

    def z_sum(send, keep):
        if Z == 4:
            near = [(i, i ^ 1) for i in range(Z)]
            part = keep + along(send, near)
            own = part + along(part, [(i, Z - 1 - i) for i in range(Z)])
            far = along(own, near)
        else:
            own, far = line_sum(keep), line_sum(send)
        return own, far

    def both_cores(parts):
        return [*parts, core_swap(parts[0]), core_swap(parts[1])]

    def slots_out(x, other):
        out = []
        for k in range(S // 2):
            pairs = []
            for i in range(S):
                for j in range(Q):
                    half = ((j // 2 + 1) // 2) % 2 if Z == 4 else 0
                    m = (half ^ other) * (S // 2) + k
                    pairs.append((i * Q + j, (i ^ m) * Q + j))
            out.append(permute(x[:, k * hb : (k + 1) * hb], ("shard", "seq"), pairs))
        return out

    def cols(w, start, size):
        return lax.dynamic_slice_in_dim(w, start, size, axis=1)

    x_own = block_in[0]
    row = jnp.concatenate(
        [attn_gain, mlp_gain, (doc_lengths[0] // 64).astype(BF), (doc_lengths[0] % 64).astype(BF)]
    )
    docs = doc_lengths.shape[1]
    rows = jnp.pad(row[None], ((0, TAIL - 1), (0, 640 - row.shape[0])))
    x = gather(x_own)
    misc = gather(rows)

    qkv_half = lax.dynamic_slice_in_dim(qkv_weight, c * hb, hb, axis=0)
    qkv_pieces = [
        jnp.concatenate([cols(qkv_half, i * D + (s ^ m) * cw, cw) for i in range(3)], axis=1)
        for m in range(S)
    ]
    wm = swap_out(qkv_pieces)
    wo = [core_swap(w) for w in wm]

    in_half = lax.dynamic_slice_in_dim(in_weight, c * hb, hb, axis=0)
    out_half = lax.dynamic_slice_in_dim(out_weight, c * hb, hb, axis=0)
    in_pieces = [
        jnp.concatenate([cols(in_half, i * ff + (s ^ m) * fs, fs) for i in range(2)], axis=0)
        for m in range(S)
    ]
    im = swap_out(in_pieces)
    om = gather(out_half)
    io = [core_swap(w) for w in im]
    oo = [core_swap(w) for w in om]

    tails = jnp.stack([p[0, 4 * hb : 4 * hb + 2 * docs] for p in misc]).astype(jnp.int32)
    lengths = tails[:, :docs] * 64 + tails[:, docs:]
    ends = jnp.cumsum(lengths, axis=1)
    key_spots = q * T - WINDOW + jnp.arange(T + 2 * WINDOW, dtype=jnp.int32)
    passed = ends[:, :, None] <= key_spots[None, None, :]
    key_segment = jnp.sum(passed.astype(jnp.int32), axis=1)
    start = jnp.sum(jnp.where(passed, lengths[:, :, None], 0), axis=1)
    position = (key_spots[None] - start)[:, WINDOW : WINDOW + T]
    segment = key_segment[:, WINDOW : WINDOW + T]
    spots = key_spots[WINDOW : WINDOW + T]
    near = jnp.abs(spots[:, None] - key_spots[None, :]) <= WINDOW
    valid = (key_spots >= 0) & (key_spots < Q * T)
    mask = (segment[:, :, None] == key_segment[:, None, :]) & (near & valid[None, :])[None]
    mask = mask.astype(F32).reshape(S * T, T + 2 * WINDOW)
    half = HEAD // 2
    freq = jnp.power(10000.0, -(jnp.arange(half).astype(F32) * (2.0 / HEAD)))
    angle = position.reshape(S * T, 1).astype(F32) * freq[None, :]
    cos_h, sin_h = jnp.cos(angle), jnp.sin(angle)
    cos = jnp.concatenate([cos_h] * 4, axis=1)
    sin = jnp.concatenate([-sin_h, sin_h] * 2, axis=1)

    h_attn, rq, kv, lead, last, wnat, gain_a, gain_m = call(
        functools.partial(qkv_kernel, S, T, hb),
        (
            sds((S * T, D), BF),
            sds((S * T, cw), BF),
            sds((S * T, 2 * cw), BF),
            sds((S, WINDOW, 2 * cw), BF),
            sds((S, WINDOW, 2 * cw), BF),
            sds((D, 3 * cw), BF),
            sds((1, D), F32),
            sds((1, D), F32),
        ),
        *x,
        *wm,
        *wo,
        *misc,
        cos,
        sin,
        scalars=sc,
    )
    before_kv, after_kv = shift(last, 1), shift(lead, -1)
    ext = pltpu.VMEM((T + 2 * WINDOW, 2 * cw), BF)
    att_own, total = call(
        functools.partial(attend_kernel, S, T),
        (sds((S * T, cw), BF), sds((S * T, cw // HEAD), F32)),
        rq,
        kv,
        before_kv,
        after_kv,
        mask,
        scratch=[ext],
    )
    att = gather(att_own)

    g_own = after(out_grad[0], att_own)
    og = gather(g_own)
    gate_w, lin_w, outw = call(
        functools.partial(late_weights_kernel, S, hb),
        (sds((D, fs), BF), sds((D, fs), BF), sds((D, D), BF)),
        *im,
        *io,
        *om,
        *oo,
        scalars=sc,
    )
    resid_own, h_mlp, gate_in, lin = call(
        functools.partial(up_kernel, S, T),
        (sds((T, D), F32), sds((S * T, D), BF), sds((S * T, fs), F32), sds((S * T, fs), F32)),
        *x,
        *att,
        outw,
        gain_m,
        gate_w,
        lin_w,
        scratch=[pltpu.VMEM((S * T, D), BF)],
    )
    wide = pltpu.VMEM((S * T, D), BF)
    mid = call(
        functools.partial(up_back_kernel, S, T),
        (sds((S * T, fs), BF),) * 3 + (sds((T, D), BF),) * S,
        *og,
        gate_in,
        lin,
        down_weight,
        gate_w,
        lin_w,
        scratch=[wide],
    )
    act, d_gate, d_lin = mid[:3]
    d_hmlp = swap_out(mid[3:])

    down_send, down_keep = call(
        functools.partial(down_grad_kernel, S, T),
        (sds((fs, D // 2), BF),) * 2,
        act,
        *og,
        scalars=sc,
        scratch=[wide],
    )
    down_z = call(
        lane_halves_kernel,
        (sds((fs, D // 4), BF),) * 2,
        down_keep,
        core_swap(down_send),
        scalars=sc,
    )
    down_sums = both_cores(z_sum(*down_z))

    in_send, in_keep = call(
        functools.partial(in_grad_kernel, S, hb),
        (sds((2 * fs, D // 2), BF),) * 2,
        h_mlp,
        d_gate,
        d_lin,
        scalars=sc,
        scratch=[pltpu.VMEM((fs, D), F32)],
    )
    in_z = call(
        lane_halves_kernel,
        (sds((2 * fs, D // 4), BF),) * 2,
        in_keep,
        core_swap(in_send),
        scalars=sc,
    )
    in_sums = []
    for k, part in enumerate(z_sum(*in_z)):
        in_sums += slots_out(part, k)
    in_sums += [core_swap(p) for p in in_sums]

    back = call(
        functools.partial(resid_back_kernel, S),
        (sds((T, D), F32), sds((T, D), BF), sds((1, D), F32)) + (sds((T, cw), BF),) * S,
        *d_hmlp,
        resid_own,
        gain_m,
        g_own,
        outw,
    )
    d_resid, d_resid_b, gain_m_g = back[:3]
    d_mix = swap_out(back[3:])

    out_parts = call(
        functools.partial(out_parts_kernel, S, T), (sds((T, D), BF),) * S, act, down_weight
    )
    out_parts = swap_out(out_parts)
    final = resid_own
    for p in out_parts:
        final = final + p.astype(F32)
    final = final.astype(BF)

    dq, dkv, to_left, to_right = call(
        functools.partial(attend_back_kernel, S, T),
        (
            sds((S * T, cw), BF),
            sds((S * T, 2 * cw), F32),
            sds((S, WINDOW, 2 * cw), BF),
            sds((S, WINDOW, 2 * cw), BF),
        ),
        rq,
        kv,
        before_kv,
        after_kv,
        mask,
        total,
        cos,
        sin,
        *d_mix,
        scratch=[ext],
    )
    from_right, from_left = shift(to_left, -1), shift(to_right, 1)

    drb = gather(d_resid_b)
    out_send, out_keep = call(
        functools.partial(out_grad_kernel, S, T),
        (sds((D, hb), BF),) * 2,
        att_own,
        *drb,
        scalars=sc,
        scratch=[wide, pltpu.VMEM((D, cw), F32)],
    )
    out_z = call(
        row_halves_kernel, (sds((D // 2, hb), BF),) * 2, out_keep, core_swap(out_send), scalars=sc
    )
    out_sums = both_cores(z_sum(*out_z))

    res = call(
        functools.partial(qkv_back_kernel, S, T, hb),
        (sds((3 * cw + TAIL, D // 2), BF),) * 2 + (sds((T, D), BF),) * S,
        *x,
        dq,
        dkv,
        from_left,
        from_right,
        cos,
        sin,
        h_attn,
        wnat,
        gain_m_g,
        scalars=sc,
        scratch=[
            pltpu.VMEM((S * T, 3 * cw), BF),
            pltpu.VMEM((3 * cw, D), F32),
            pltpu.VMEM((2, D), F32),
        ],
    )
    qkv_g = call(
        functools.partial(pair_sum_kernel, S, hb),
        (sds((3 * cw + TAIL, hb), BF),) * S,
        res[1],
        core_swap(res[0]),
    )
    cut = 3 * cw // 2
    qkv_z = call(
        functools.partial(slot_halves_kernel, S),
        (sds((cut, D // 4), BF),) * 2 + (sds((cut + TAIL, D // 4), BF),) * 2,
        *swap_out(qkv_g),
        scalars=sc,
    )
    qkv_sums = both_cores(z_sum(*qkv_z[:2]))
    qkv_sums += both_cores(z_sum(*qkv_z[2:]))
    d_hattn = swap_out(res[2:])

    in_rows = call(
        functools.partial(in_back_kernel, S), sds((T, D), F32), *d_hattn, x_own, gain_a, d_resid
    )

    down_grad = call(down_final_kernel, sds((fs, D), F32), *down_sums, scalars=sc)
    in_grad = call(
        functools.partial(in_final_kernel, S, hb), sds((2 * hb, 2 * ff), F32), *in_sums, scalars=sc
    )
    out_wgrad = call(
        functools.partial(out_final_kernel, hb), sds((2 * hb, D), F32), *out_sums, scalars=sc
    )
    qkv_grad, gain_a_grad, gain_m_grad = call(
        functools.partial(qkv_final_kernel, S, hb),
        (
            sds((2 * hb, 3 * D), F32),
            sds((1, 2 * hb), F32),
            sds((1, 2 * hb), F32),
        ),
        *qkv_sums,
        scalars=sc,
    )
    return (
        final[None],
        in_rows[None],
        qkv_grad,
        out_wgrad,
        in_grad,
        down_grad,
        gain_a_grad[0],
        gain_m_grad[0],
    )


def solution(mesh):
    rows = P("shard", "seq", None)
    mat = P("shard", None)
    vec = P("shard")

    return jax.shard_map(
        shards,
        mesh=mesh,
        in_specs=(rows, mat, mat, mat, mat, mat, vec, vec, rows),
        out_specs=(rows, rows, mat, mat, mat, mat, vec, vec),
        check_vma=False,
    )
```

```python
import functools
import math

import jax
import jax.numpy as jnp
from jax import lax
from jax.experimental import pallas as pl
from jax.experimental.pallas import tpu as pltpu
from jax.sharding import PartitionSpec as P


HEAD = 64
WINDOW = 64
EPSILON = 1e-05
NEGATIVE = -1e30
BF = jnp.bfloat16
F32 = jnp.float32
TAIL = 16
NT = ((1,), (1,))
TN = ((0,), (0,))


def mm(a, b, dims=((1,), (0,))):
    return lax.dot_general(a, b, (dims, ((), ())), preferred_element_type=F32)


def call(kernel, out_shape, *args, scalars=None, scratch=()):
    vmem = pl.BlockSpec(memory_space=pltpu.VMEM)
    specs = [vmem] * len(args)
    if scalars is not None:
        specs = [pl.BlockSpec(memory_space=pltpu.SMEM)] + specs
        args = (scalars,) + tuple(args)
    return pl.pallas_call(
        kernel,
        out_shape=out_shape,
        in_specs=specs,
        out_specs=jax.tree.map(lambda _: vmem, out_shape),
        scratch_shapes=list(scratch),
        compiler_params=pltpu.CompilerParams(vmem_limit_bytes=58 << 20),
    )(*args)


def sds(shape, dtype):
    return jax.ShapeDtypeStruct(shape, dtype)


def norm(values):
    centered = values - jnp.mean(values, axis=-1, keepdims=True)
    variance = jnp.mean(centered * centered, axis=-1, keepdims=True)
    inv_std = lax.rsqrt(variance + EPSILON)
    return centered * inv_std, inv_std


def norm_back(scaled, normed, inv_std):
    return inv_std * (
        scaled
        - jnp.mean(scaled, axis=-1, keepdims=True)
        - normed * jnp.mean(scaled * normed, axis=-1, keepdims=True)
    )


def swap_halves(x):
    half = HEAD // 2
    lane = lax.broadcasted_iota(jnp.int32, x.shape, 1)
    return jnp.where(lane % HEAD < half, pltpu.roll(x, 128 - half, 1), pltpu.roll(x, half, 1))


def turned(x, cos, sin):
    blocks = [x[:, i : i + 128] for i in range(0, x.shape[1], 128)]
    return jnp.concatenate([b * cos + swap_halves(b) * sin for b in blocks], axis=1)


def at(start, size):
    return pl.ds(pl.multiple_of(start, size), size)


def pick(ref, index, size):
    if size % 128 == 0:
        return ref[:, at(index * size, size)]
    two = ref[:, at(index // 2 * (2 * size), 2 * size)]
    return jnp.where(index % 2 == 0, two[:, :size], two[:, size:])


def in_order(S, hb, sc, relative, mine, other, out):
    s, c = sc[0], sc[1]
    for m in range(S):
        base = (m if relative else (s ^ m)) * (2 * hb)
        out[at(base + c * hb, hb), :] = mine[m][...]
        out[at(base + (1 - c) * hb, hb), :] = other[m][...]


def qkv_kernel(S, T, hb, sc, *refs):
    x, wm, wo, misc = (refs[i * S : (i + 1) * S] for i in range(4))
    cos, sin = refs[4 * S : 4 * S + 2]
    h, rq, kv, lead, last, wnat, gain_a, gain_m = refs[4 * S + 2 :]
    in_order(S, hb, sc, False, wm, wo, wnat)
    cw = rq.shape[1]
    for m in range(S):
        rows = misc[m][...].astype(F32)
        cols = at((sc[0] ^ m) * (2 * hb), 2 * hb)
        gain_a[:, cols] = rows[0:1, : 2 * hb]
        gain_m[:, cols] = rows[0:1, 2 * hb : 4 * hb]
    for m in range(S):
        normed, _ = norm(x[m][...].astype(F32))
        h[m * T : (m + 1) * T, :] = (normed * gain_a[...]).astype(BF)
    act = mm(h[...], wnat[...])
    rq[...] = turned(act[:, :cw], cos[...], sin[...]).astype(BF)
    kv[:, :cw] = turned(act[:, cw : 2 * cw], cos[...], sin[...]).astype(BF)
    kv[:, cw:] = act[:, 2 * cw :].astype(BF)
    for m in range(S):
        lead[m] = kv[m * T : m * T + WINDOW, :]
        last[m] = kv[(m + 1) * T - WINDOW : (m + 1) * T, :]


def two_heads(x):
    lane = lax.broadcasted_iota(jnp.int32, x.shape, 1)
    first = jnp.where(lane < HEAD, 1.0, 0.0).astype(x.dtype)
    return jnp.concatenate([x * first, x * (1 - first).astype(x.dtype)], axis=0)


def one_pair(x, T):
    lane = lax.broadcasted_iota(jnp.int32, (T, 128), 1)
    return jnp.where(lane < HEAD, x[:T], x[T:])


def extend(m, rows, T, kv, before, after, ext):
    ext[:WINDOW, :] = before[m]
    ext[WINDOW : WINDOW + T, :] = kv[rows, :]
    ext[WINDOW + T :, :] = after[m]


def attend_kernel(S, T, rq, kv, before, after, mask, out, total, ext):
    cw = rq.shape[1]

    def row(m, carry):
        rows = at(m * T, T)
        extend(m, rows, T, kv, before, after, ext)
        ok = mask[rows, :] > 0.0
        ok = jnp.concatenate([ok, ok], axis=0)
        for p in range(cw // 128):
            lanes = slice(p * 128, (p + 1) * 128)
            q = two_heads(rq[rows, lanes])
            k, v = ext[:, lanes], ext[:, cw + p * 128 : cw + (p + 1) * 128]
            scores = jnp.where(ok, mm(q, k, NT) * HEAD ** (-0.5), NEGATIVE)
            top = jnp.max(scores, axis=-1, keepdims=True)
            log_total = top + jnp.log(jnp.sum(jnp.exp(scores - top), axis=-1, keepdims=True))
            prob = jnp.exp(scores - log_total).astype(BF)
            out[rows, lanes] = one_pair(mm(prob, v), T).astype(BF)
            total[rows, 2 * p : 2 * p + 1] = log_total[:T]
            total[rows, 2 * p + 1 : 2 * p + 2] = log_total[T:]
        return carry

    lax.fori_loop(0, S, row, 0)


def attend_back_kernel(S, T, *refs):
    rq, kv, before, after, mask, total, cos, sin = refs[:8]
    d_mix = refs[8 : 8 + S]
    dq, dkv, to_left, to_right, ext, d_all = refs[8 + S :]
    cw = rq.shape[1]
    for m in range(S):
        d_all[m * T : (m + 1) * T, :] = d_mix[m][...]

    def row(m, carry):
        rows = at(m * T, T)
        extend(m, rows, T, kv, before, after, ext)
        ok = mask[rows, :] > 0.0
        ok = jnp.concatenate([ok, ok], axis=0)
        for p in range(cw // 128):
            ks = slice(p * 128, (p + 1) * 128)
            vs = slice(cw + p * 128, cw + (p + 1) * 128)
            q, d = two_heads(rq[rows, ks]), two_heads(d_all[rows, ks])
            k, v = ext[:, ks], ext[:, vs]
            log_total = jnp.concatenate(
                [total[rows, 2 * p : 2 * p + 1], total[rows, 2 * p + 1 : 2 * p + 2]], axis=0
            )
            scores = jnp.where(ok, mm(q, k, NT) * HEAD ** (-0.5), NEGATIVE)
            prob = jnp.exp(scores - log_total)
            d_prob = mm(d, v, NT)
            delta = jnp.sum(prob * d_prob, axis=-1, keepdims=True)
            d_score = (prob * (d_prob - delta)).astype(BF)
            d_val = mm(prob.astype(BF), d, TN)
            d_key = mm(d_score, q, TN) * HEAD ** (-0.5)
            g = one_pair(mm(d_score, k), T) * HEAD ** (-0.5)
            dq[rows, ks] = turned(g, cos[rows, :], -sin[rows, :]).astype(BF)
            for sl, g in ((ks, d_key), (vs, d_val)):
                to_left[m, :, sl] = g[:WINDOW].astype(BF)
                dkv[rows, sl] = g[WINDOW : WINDOW + T]
                to_right[m, :, sl] = g[WINDOW + T :].astype(BF)
        return carry

    lax.fori_loop(0, S, row, 0)


def late_weights_kernel(S, hb, sc, *refs):
    im, io, om, oo = (refs[i * S : (i + 1) * S] for i in range(4))
    gate, lin, outw = refs[4 * S :]
    in_order(S, hb, sc, False, [r.at[:hb] for r in im], [r.at[:hb] for r in io], gate)
    in_order(S, hb, sc, False, [r.at[hb:] for r in im], [r.at[hb:] for r in io], lin)
    in_order(S, hb, sc, True, om, oo, outw)


def up_kernel(S, T, *refs):
    x = refs[:S]
    att = refs[S : 2 * S]
    outw, gain, gate_w, lin_w = refs[2 * S : 2 * S + 4]
    resid_own, h, gate_in, lin, mixed = refs[2 * S + 4 :]
    cw = att[0].shape[1]
    for m in range(S):
        for j in range(S):
            part = att[j][(m ^ j) * T : ((m ^ j) + 1) * T, :]
            mixed[m * T : (m + 1) * T, j * cw : (j + 1) * cw] = part
    summed = mm(mixed[...], outw[...])
    for m in range(S):
        resid = x[m][...].astype(F32) + summed[m * T : (m + 1) * T]
        if m == 0:
            resid_own[...] = resid
        normed, _ = norm(resid)
        h[m * T : (m + 1) * T, :] = (normed * gain[...]).astype(BF)
    gate_in[...] = mm(h[...], gate_w[...])
    lin[...] = mm(h[...], lin_w[...])


def up_back_kernel(S, T, *refs):
    og = refs[:S]
    gate_in, lin, down, gate_w, lin_w = refs[S : S + 5]
    act, d_gate, d_lin = refs[S + 5 : S + 8]
    pieces = refs[S + 8 : 2 * S + 8]
    both = refs[2 * S + 8]
    for m in range(S):
        both[m * T : (m + 1) * T, :] = og[m][...]
    d_act = mm(both[...], down[...], NT)
    gate, ln = gate_in[...], lin[...]
    cdf = 0.5 * (1.0 + lax.erf(gate * 2.0 ** (-0.5)))
    pdf = jnp.exp(-0.5 * gate * gate) * (2.0 * math.pi) ** (-0.5)
    gelu = gate * cdf
    act[...] = (gelu * ln).astype(BF)
    d_gate[...] = (d_act * ln * (cdf + gate * pdf)).astype(BF)
    d_lin[...] = (d_act * gelu).astype(BF)
    part = mm(d_gate[...], gate_w[...], NT) + mm(d_lin[...], lin_w[...], NT)
    for m in range(S):
        pieces[m][...] = part[m * T : (m + 1) * T].astype(BF)


def resid_back_kernel(S, *refs):
    parts = refs[:S]
    resid, gain, grad, outw = refs[S : S + 4]
    d_resid, d_resid_b, gain_g = refs[S + 4 : S + 7]
    pieces = refs[S + 7 :]
    d_h = parts[0][...].astype(F32)
    for m in range(1, S):
        d_h = d_h + parts[m][...].astype(F32)
    normed, inv_std = norm(resid[...])
    gain_g[...] = jnp.sum(d_h * normed, axis=0, keepdims=True)
    dr = grad[...].astype(F32) + norm_back(d_h * gain[...], normed, inv_std)
    d_resid[...] = dr
    db = dr.astype(BF)
    d_resid_b[...] = db
    cw = pieces[0].shape[1]
    d_att = mm(db, outw[...], NT)
    for m in range(S):
        pieces[m][...] = d_att[:, m * cw : (m + 1) * cw].astype(BF)


def down_grad_kernel(S, T, sc, act, *refs):
    og, (send, keep, both) = refs[:S], refs[S:]
    half = send.shape[1]
    for m in range(S):
        both[m * T : (m + 1) * T, :] = og[m][...]
    for ref, part in ((send, 1 - sc[1]), (keep, sc[1])):
        ref[...] = mm(act[...], both[:, at(part * half, half)], TN).astype(BF)


def in_grad_kernel(S, hb, sc, h, d_gate, d_lin, send, keep, grad):
    fs = d_gate.shape[1]
    for i, d in enumerate((d_gate, d_lin)):
        grad[...] = mm(d[...], h[...], TN)
        for m in range(S):
            for ref, half in ((send, 1 - sc[1]), (keep, sc[1])):
                block = pick(grad, (sc[0] ^ m) * 2 + half, hb)
                ref[i * fs : (i + 1) * fs, m * hb : (m + 1) * hb] = block.astype(BF)


def out_grad_kernel(S, T, sc, att, *refs):
    drb, (send, keep, both, grad) = refs[:S], refs[S:]
    hb = send.shape[1]
    for m in range(S):
        both[m * T : (m + 1) * T, :] = drb[m][...]
    grad[...] = mm(both[...], att[...], TN)
    send[...] = pick(grad, 1 - sc[1], hb).astype(BF)
    keep[...] = pick(grad, sc[1], hb).astype(BF)


def out_parts_kernel(S, T, act, down, *pieces):
    out = mm(act[...], down[...])
    for m in range(S):
        pieces[m][...] = out[m * T : (m + 1) * T].astype(BF)


def qkv_back_kernel(S, T, hb, sc, *refs):
    x = refs[:S]
    dq, dkv, from_left, from_right, cos, sin, h, wnat, gain_m_g = refs[S : S + 9]
    send, keep = refs[S + 9 : S + 11]
    pieces = refs[S + 11 : 2 * S + 11]
    d_qkv, grad, gain_row = refs[2 * S + 11 :]
    cw = dq.shape[1]
    d_qkv[:, :cw] = dq[...]
    for m in range(S):
        for start, edge in ((m * T, from_left), ((m + 1) * T - WINDOW, from_right)):
            rows = slice(start, start + WINDOW)
            dkv[rows, :] = dkv[rows, :] + edge[m].astype(F32)
    d_qkv[:, cw : 2 * cw] = turned(dkv[:, :cw], cos[...], -sin[...]).astype(BF)
    d_qkv[:, 2 * cw :] = dkv[:, cw:].astype(BF)
    grad[...] = mm(d_qkv[...], h[...], TN)
    d_h = mm(d_qkv[...], wnat[...], NT)
    total = None
    for m in range(S):
        part = d_h[m * T : (m + 1) * T]
        pieces[m][...] = part.astype(BF)
        normed, _ = norm(x[m][...].astype(F32))
        part = jnp.sum(part * normed, axis=0, keepdims=True)
        total = part if total is None else total + part
    gain_row[0:1, :] = total
    gain_row[1:2, :] = gain_m_g[...]
    row = lax.broadcasted_iota(jnp.int32, (TAIL, hb), 0)
    for m in range(S):
        lanes = slice(m * hb, (m + 1) * hb)
        base = (sc[0] ^ m) * 2
        tail = jnp.zeros((TAIL, hb), F32)
        for i in range(4):
            line = pick(gain_row, base + i % 2, hb)[i // 2 : i // 2 + 1]
            tail = jnp.where(row == i, jnp.broadcast_to(line, tail.shape), tail)
        for ref, half in ((send, 1 - sc[1]), (keep, sc[1])):
            ref[: 3 * cw, lanes] = pick(grad, base + half, hb).astype(BF)
            ref[3 * cw :, lanes] = tail.astype(BF)


def pair_sum_kernel(S, hb, keep, got, *pieces):
    for m in range(S):
        lanes = slice(m * hb, (m + 1) * hb)
        pieces[m][...] = keep[:, lanes] + got[:, lanes]


def lane_halves_kernel(sc, keep, got, send_z, keep_z):
    half = send_z.shape[1]
    for ref, part in ((send_z, 1 - sc[2]), (keep_z, sc[2])):
        cols = at(part * half, half)
        ref[...] = keep[:, cols] + got[:, cols]


def row_halves_kernel(sc, keep, got, send_z, keep_z):
    half = send_z.shape[0]
    for ref, part in ((send_z, 1 - sc[2]), (keep_z, sc[2])):
        rows = at(part * half, half)
        ref[...] = keep[rows, :] + got[rows, :]


def slot_halves_kernel(S, sc, *refs):
    slots, chunks = refs[:S], refs[S:]
    hb = slots[0].shape[1]
    half = S // 2
    low = (sc[2] == 0).astype(F32).astype(BF)
    high = (sc[2] == 1).astype(F32).astype(BF)
    start = 0
    for send_z, keep_z in (chunks[:2], chunks[2:]):
        stop = start + send_z.shape[0]
        for k in range(half):
            a, b = slots[k][start:stop, :], slots[half + k][start:stop, :]
            lanes = slice(k * hb, (k + 1) * hb)
            keep_z[:, lanes] = a * low + b * high
            send_z[:, lanes] = a * high + b * low
        start = stop


def in_back_kernel(S, *refs):
    parts = refs[:S]
    x, gain, d_resid, out = refs[S:]
    d_h = parts[0][...].astype(F32)
    for m in range(1, S):
        d_h = d_h + parts[m][...].astype(F32)
    normed, inv_std = norm(x[...].astype(F32))
    out[...] = d_resid[...] + norm_back(d_h * gain[...], normed, inv_std)


def down_final_kernel(sc, own, far, own_o, far_o, out):
    half = own.shape[1]
    for part, a, b in ((sc[1], own, far), (1 - sc[1], own_o, far_o)):
        out[:, at((2 * part + sc[2]) * half, half)] = a[...].astype(F32)
        out[:, at((2 * part + 1 - sc[2]) * half, half)] = b[...].astype(F32)


def unit(n):
    rows = lax.broadcasted_iota(jnp.int32, (n, n), 0)
    return jnp.where(rows == lax.broadcasted_iota(jnp.int32, (n, n), 1), 1.0, 0.0).astype(BF)


def in_final_kernel(S, hb, sc, *refs):
    out = refs[-1]
    half = S // 2
    fs = refs[0].shape[0] // 2
    eye = unit(hb)
    for j in range(S):
        m = sc[0] ^ j
        place = jnp.where(m // half == sc[2], 0, half) + m % half
        for part, parts in ((sc[1], refs[:S]), (1 - sc[1], refs[S : 2 * S])):
            block = parts[0][...] * (place == 0).astype(F32).astype(BF)
            for i in range(1, S):
                block = block + parts[i][...] * (place == i).astype(F32).astype(BF)
            block = mm(eye, block, NT)
            for i in range(2):
                start = (i * S + j) * fs
                out[at(part * hb, hb), start : start + fs] = block[:, i * fs : (i + 1) * fs]


def qkv_final_kernel(S, hb, sc, *refs):
    first, second, (out, gain_a, gain_m) = refs[:4], refs[4:8], refs[8:]
    half = S // 2
    D = out.shape[1] // 3
    cw = D // S
    eye = unit(hb)
    low = (sc[2] == 0).astype(F32).astype(BF)
    high = (sc[2] == 1).astype(F32).astype(BF)
    total = None
    for i, part in ((0, sc[1]), (2, 1 - sc[1])):
        for m in range(S):
            lanes = slice((m % half) * hb, (m % half + 1) * hb)
            p, q = (low, high) if m < half else (high, low)
            blocks = [r[i][:, lanes] * p + r[i + 1][:, lanes] * q for r in (first, second)]
            block = jnp.concatenate(blocks, axis=0)
            grad = mm(eye, block[: 3 * cw], NT)
            for k in range(3):
                cols = at(k * D + (sc[0] ^ m) * cw, cw)
                out[at(part * hb, hb), cols] = grad[:, k * cw : (k + 1) * cw]
            if i == 0:
                tail = block[3 * cw :].astype(F32)
                total = tail if total is None else total + tail
    gain_a[:, :hb], gain_a[:, hb:] = total[0:1], total[1:2]
    gain_m[:, :hb], gain_m[:, hb:] = total[2:3], total[3:4]


def out_final_kernel(hb, sc, own, far, own_o, far_o, out):
    half = own.shape[0]
    eye = unit(hb)
    for part, a, b in ((sc[1], own, far), (1 - sc[1], own_o, far_o)):
        out[at(part * hb, hb), at(sc[2] * half, half)] = mm(eye, a[...], NT)
        out[at(part * hb, hb), at((1 - sc[2]) * half, half)] = mm(eye, b[...], NT)


def after(values, *others):
    flat, tree = jax.tree.flatten(values)
    rest = jax.tree.leaves(others)
    out = lax.optimization_barrier(tuple(flat) + tuple(rest))
    return jax.tree.unflatten(tree, out[: len(flat)])


def shards(
    block_in,
    doc_lengths,
    qkv_weight,
    out_weight,
    in_weight,
    down_weight,
    attn_gain,
    mlp_gain,
    out_grad,
):
    S, Q = lax.axis_size("shard"), lax.axis_size("seq")
    Z = Q // 2
    s, q = lax.axis_index("shard"), lax.axis_index("seq")
    c, z = q % 2, q // 2
    kz = ((z + 1) // 2) % 2 if Z == 4 else 0 * z
    sc = jnp.stack([s, c, kz]).astype(jnp.int32)
    T, D = block_in.shape[1:]
    cw = D // S
    hb = D // S // 2
    ff = in_weight.shape[1] // 2
    fs = ff // S

    def permute(x, axis, pairs):
        return lax.ppermute(x, axis, pairs)

    def peer(x, m):
        return permute(x, "shard", [(i, i ^ m) for i in range(S)])

    def core_swap(x):
        return permute(x, "seq", [(i, i ^ 1) for i in range(Q)])

    def along(x, pairs):
        both = [(2 * a + e, 2 * b + e) for a, b in pairs for e in (0, 1)]
        return permute(x, "seq", both)

    def shift(x, step):
        pairs = [(i, i + step) for i in range(Q) if 0 <= i + step < Q]
        return permute(x, "seq", pairs)

    def gather(x):
        return [x] + [peer(x, m) for m in range(1, S)]

    def swap_out(pieces):
        return [pieces[0]] + [peer(pieces[m], m) for m in range(1, S)]

    def line_sum(x):
        half = Z // 2
        for k in range(half - 1):
            x = x + along(x, [(k, k + 1), (Z - 1 - k, Z - 2 - k)])
        if Z > 1:
            x = x + along(x, [(half - 1, half), (half, half - 1)])
        for k in range(half - 1, 0, -1):
            got = along(x, [(k, k - 1), (Z - 1 - k, Z - k)])
            x = jnp.where((z == k - 1) | (z == Z - k), got, x)
        return x

    def z_sum(send, keep):
        if Z == 4:
            near = [(i, i ^ 1) for i in range(Z)]
            part = keep + along(send, near)
            own = part + along(part, [(i, Z - 1 - i) for i in range(Z)])
            far = along(own, near)
        else:
            own, far = line_sum(keep), line_sum(send)
        return own, far

    def both_cores(parts):
        return [*parts, core_swap(parts[0]), core_swap(parts[1])]

    def slots_out(x, other):
        out = []
        for k in range(S // 2):
            pairs = []
            for i in range(S):
                for j in range(Q):
                    half = ((j // 2 + 1) // 2) % 2 if Z == 4 else 0
                    m = (half ^ other) * (S // 2) + k
                    pairs.append((i * Q + j, (i ^ m) * Q + j))
            out.append(permute(x[:, k * hb : (k + 1) * hb], ("shard", "seq"), pairs))
        return out

    def cols(w, start, size):
        return lax.dynamic_slice_in_dim(w, start, size, axis=1)

    x_own = block_in[0]
    row = jnp.concatenate(
        [attn_gain, mlp_gain, (doc_lengths[0] // 64).astype(BF), (doc_lengths[0] % 64).astype(BF)]
    )
    docs = doc_lengths.shape[1]
    rows = jnp.pad(row[None], ((0, TAIL - 1), (0, 640 - row.shape[0])))
    x = gather(x_own)
    misc = gather(rows)

    qkv_half = lax.dynamic_slice_in_dim(qkv_weight, c * hb, hb, axis=0)
    qkv_pieces = [
        jnp.concatenate([cols(qkv_half, i * D + (s ^ m) * cw, cw) for i in range(3)], axis=1)
        for m in range(S)
    ]
    wm = swap_out(qkv_pieces)
    wo = [core_swap(w) for w in wm]

    in_half = lax.dynamic_slice_in_dim(in_weight, c * hb, hb, axis=0)
    out_half = lax.dynamic_slice_in_dim(out_weight, c * hb, hb, axis=0)
    in_pieces = [
        jnp.concatenate([cols(in_half, i * ff + (s ^ m) * fs, fs) for i in range(2)], axis=0)
        for m in range(S)
    ]
    im = swap_out(in_pieces)
    om = gather(out_half)
    io = [core_swap(w) for w in im]
    oo = [core_swap(w) for w in om]

    tails = jnp.stack([p[0, 4 * hb : 4 * hb + 2 * docs] for p in misc]).astype(jnp.int32)
    lengths = tails[:, :docs] * 64 + tails[:, docs:]
    ends = jnp.cumsum(lengths, axis=1)
    key_spots = q * T - WINDOW + jnp.arange(T + 2 * WINDOW, dtype=jnp.int32)
    passed = ends[:, :, None] <= key_spots[None, None, :]
    key_segment = jnp.sum(passed.astype(jnp.int32), axis=1)
    start = jnp.sum(jnp.where(passed, lengths[:, :, None], 0), axis=1)
    position = (key_spots[None] - start)[:, WINDOW : WINDOW + T]
    segment = key_segment[:, WINDOW : WINDOW + T]
    spots = key_spots[WINDOW : WINDOW + T]
    near = jnp.abs(spots[:, None] - key_spots[None, :]) <= WINDOW
    valid = (key_spots >= 0) & (key_spots < Q * T)
    mask = (segment[:, :, None] == key_segment[:, None, :]) & (near & valid[None, :])[None]
    mask = mask.astype(F32).reshape(S * T, T + 2 * WINDOW)
    half = HEAD // 2
    freq = jnp.power(10000.0, -(jnp.arange(half).astype(F32) * (2.0 / HEAD)))
    angle = position.reshape(S * T, 1).astype(F32) * freq[None, :]
    cos_h, sin_h = jnp.cos(angle), jnp.sin(angle)
    cos = jnp.concatenate([cos_h] * 4, axis=1)
    sin = jnp.concatenate([-sin_h, sin_h] * 2, axis=1)

    h_attn, rq, kv, lead, last, wnat, gain_a, gain_m = call(
        functools.partial(qkv_kernel, S, T, hb),
        (
            sds((S * T, D), BF),
            sds((S * T, cw), BF),
            sds((S * T, 2 * cw), BF),
            sds((S, WINDOW, 2 * cw), BF),
            sds((S, WINDOW, 2 * cw), BF),
            sds((D, 3 * cw), BF),
            sds((1, D), F32),
            sds((1, D), F32),
        ),
        *x,
        *wm,
        *wo,
        *misc,
        cos,
        sin,
        scalars=sc,
    )
    before_kv, after_kv = shift(last, 1), shift(lead, -1)
    ext = pltpu.VMEM((T + 2 * WINDOW, 2 * cw), BF)
    att_own, total = call(
        functools.partial(attend_kernel, S, T),
        (sds((S * T, cw), BF), sds((S * T, cw // HEAD), F32)),
        rq,
        kv,
        before_kv,
        after_kv,
        mask,
        scratch=[ext],
    )
    att = gather(att_own)

    g_own = after(out_grad[0], att_own)
    og = gather(g_own)
    gate_w, lin_w, outw = call(
        functools.partial(late_weights_kernel, S, hb),
        (sds((D, fs), BF), sds((D, fs), BF), sds((D, D), BF)),
        *im,
        *io,
        *om,
        *oo,
        scalars=sc,
    )
    resid_own, h_mlp, gate_in, lin = call(
        functools.partial(up_kernel, S, T),
        (sds((T, D), F32), sds((S * T, D), BF), sds((S * T, fs), F32), sds((S * T, fs), F32)),
        *x,
        *att,
        outw,
        gain_m,
        gate_w,
        lin_w,
        scratch=[pltpu.VMEM((S * T, D), BF)],
    )
    wide = pltpu.VMEM((S * T, D), BF)
    mid = call(
        functools.partial(up_back_kernel, S, T),
        (sds((S * T, fs), BF),) * 3 + (sds((T, D), BF),) * S,
        *og,
        gate_in,
        lin,
        down_weight,
        gate_w,
        lin_w,
        scratch=[wide],
    )
    act, d_gate, d_lin = mid[:3]
    d_hmlp = swap_out(mid[3:])

    down_send, down_keep = call(
        functools.partial(down_grad_kernel, S, T),
        (sds((fs, D // 2), BF),) * 2,
        act,
        *og,
        scalars=sc,
        scratch=[wide],
    )
    down_z = call(
        lane_halves_kernel,
        (sds((fs, D // 4), BF),) * 2,
        down_keep,
        core_swap(down_send),
        scalars=sc,
    )
    down_sums = both_cores(z_sum(*down_z))

    in_send, in_keep = call(
        functools.partial(in_grad_kernel, S, hb),
        (sds((2 * fs, D // 2), BF),) * 2,
        h_mlp,
        d_gate,
        d_lin,
        scalars=sc,
        scratch=[pltpu.VMEM((fs, D), F32)],
    )
    in_z = call(
        lane_halves_kernel,
        (sds((2 * fs, D // 4), BF),) * 2,
        in_keep,
        core_swap(in_send),
        scalars=sc,
    )
    in_sums = []
    for k, part in enumerate(z_sum(*in_z)):
        in_sums += slots_out(part, k)
    in_sums += [core_swap(p) for p in in_sums]

    back = call(
        functools.partial(resid_back_kernel, S),
        (sds((T, D), F32), sds((T, D), BF), sds((1, D), F32)) + (sds((T, cw), BF),) * S,
        *d_hmlp,
        resid_own,
        gain_m,
        g_own,
        outw,
    )
    d_resid, d_resid_b, gain_m_g = back[:3]
    d_mix = swap_out(back[3:])

    out_parts = call(
        functools.partial(out_parts_kernel, S, T), (sds((T, D), BF),) * S, act, down_weight
    )
    out_parts = swap_out(out_parts)
    final = resid_own
    for p in out_parts:
        final = final + p.astype(F32)
    final = final.astype(BF)

    dq, dkv, to_left, to_right = call(
        functools.partial(attend_back_kernel, S, T),
        (
            sds((S * T, cw), BF),
            sds((S * T, 2 * cw), F32),
            sds((S, WINDOW, 2 * cw), BF),
            sds((S, WINDOW, 2 * cw), BF),
        ),
        rq,
        kv,
        before_kv,
        after_kv,
        mask,
        total,
        cos,
        sin,
        *d_mix,
        scratch=[ext, pltpu.VMEM((S * T, cw), BF)],
    )
    from_right, from_left = shift(to_left, -1), shift(to_right, 1)

    drb = gather(d_resid_b)
    out_send, out_keep = call(
        functools.partial(out_grad_kernel, S, T),
        (sds((D, hb), BF),) * 2,
        att_own,
        *drb,
        scalars=sc,
        scratch=[wide, pltpu.VMEM((D, cw), F32)],
    )
    out_z = call(
        row_halves_kernel, (sds((D // 2, hb), BF),) * 2, out_keep, core_swap(out_send), scalars=sc
    )
    out_sums = both_cores(z_sum(*out_z))

    res = call(
        functools.partial(qkv_back_kernel, S, T, hb),
        (sds((3 * cw + TAIL, D // 2), BF),) * 2 + (sds((T, D), BF),) * S,
        *x,
        dq,
        dkv,
        from_left,
        from_right,
        cos,
        sin,
        h_attn,
        wnat,
        gain_m_g,
        scalars=sc,
        scratch=[
            pltpu.VMEM((S * T, 3 * cw), BF),
            pltpu.VMEM((3 * cw, D), F32),
            pltpu.VMEM((2, D), F32),
        ],
    )
    qkv_g = call(
        functools.partial(pair_sum_kernel, S, hb),
        (sds((3 * cw + TAIL, hb), BF),) * S,
        res[1],
        core_swap(res[0]),
    )
    cut = 3 * cw // 2
    qkv_z = call(
        functools.partial(slot_halves_kernel, S),
        (sds((cut, D // 4), BF),) * 2 + (sds((cut + TAIL, D // 4), BF),) * 2,
        *swap_out(qkv_g),
        scalars=sc,
    )
    qkv_sums = both_cores(z_sum(*qkv_z[:2]))
    qkv_sums += both_cores(z_sum(*qkv_z[2:]))
    d_hattn = swap_out(res[2:])

    in_rows = call(
        functools.partial(in_back_kernel, S), sds((T, D), F32), *d_hattn, x_own, gain_a, d_resid
    )

    down_grad = call(down_final_kernel, sds((fs, D), F32), *down_sums, scalars=sc)
    in_grad = call(
        functools.partial(in_final_kernel, S, hb), sds((2 * hb, 2 * ff), F32), *in_sums, scalars=sc
    )
    out_wgrad = call(
        functools.partial(out_final_kernel, hb), sds((2 * hb, D), F32), *out_sums, scalars=sc
    )
    qkv_grad, gain_a_grad, gain_m_grad = call(
        functools.partial(qkv_final_kernel, S, hb),
        (
            sds((2 * hb, 3 * D), F32),
            sds((1, 2 * hb), F32),
            sds((1, 2 * hb), F32),
        ),
        *qkv_sums,
        scalars=sc,
    )
    return (
        final[None],
        in_rows[None],
        qkv_grad,
        out_wgrad,
        in_grad,
        down_grad,
        gain_a_grad[0],
        gain_m_grad[0],
    )


def solution(mesh):
    rows = P("shard", "seq", None)
    mat = P("shard", None)
    vec = P("shard")

    return jax.shard_map(
        shards,
        mesh=mesh,
        in_specs=(rows, mat, mat, mat, mat, mat, vec, vec, rows),
        out_specs=(rows, rows, mat, mat, mat, mat, vec, vec),
        check_vma=False,
    )
```

```python
import functools
import math

import jax
import jax.numpy as jnp
from jax import lax
from jax.experimental import pallas as pl
from jax.experimental.pallas import tpu as pltpu
from jax.sharding import PartitionSpec as P


HEAD = 64
WINDOW = 64
EPSILON = 1e-05
NEGATIVE = -1e30
BF = jnp.bfloat16
F32 = jnp.float32
TAIL = 16
NT = ((1,), (1,))
TN = ((0,), (0,))


def mm(a, b, dims=((1,), (0,))):
    return lax.dot_general(a, b, (dims, ((), ())), preferred_element_type=F32)


def call(kernel, out_shape, *args, scalars=None, scratch=()):
    vmem = pl.BlockSpec(memory_space=pltpu.VMEM)
    specs = [vmem] * len(args)
    if scalars is not None:
        specs = [pl.BlockSpec(memory_space=pltpu.SMEM)] + specs
        args = (scalars,) + tuple(args)
    return pl.pallas_call(
        kernel,
        out_shape=out_shape,
        in_specs=specs,
        out_specs=jax.tree.map(lambda _: vmem, out_shape),
        scratch_shapes=list(scratch),
        compiler_params=pltpu.CompilerParams(vmem_limit_bytes=58 << 20),
    )(*args)


def sds(shape, dtype):
    return jax.ShapeDtypeStruct(shape, dtype)


def norm(values):
    centered = values - jnp.mean(values, axis=-1, keepdims=True)
    variance = jnp.mean(centered * centered, axis=-1, keepdims=True)
    inv_std = lax.rsqrt(variance + EPSILON)
    return centered * inv_std, inv_std


def norm_back(scaled, normed, inv_std):
    return inv_std * (
        scaled
        - jnp.mean(scaled, axis=-1, keepdims=True)
        - normed * jnp.mean(scaled * normed, axis=-1, keepdims=True)
    )


def swap_halves(x):
    half = HEAD // 2
    lane = lax.broadcasted_iota(jnp.int32, x.shape, 1)
    return jnp.where(lane % HEAD < half, pltpu.roll(x, 128 - half, 1), pltpu.roll(x, half, 1))


def turned(x, cos, sin):
    blocks = [x[:, i : i + 128] for i in range(0, x.shape[1], 128)]
    return jnp.concatenate([b * cos + swap_halves(b) * sin for b in blocks], axis=1)


def at(start, size):
    return pl.ds(pl.multiple_of(start, size), size)


def pick(ref, index, size):
    if size % 128 == 0:
        return ref[:, at(index * size, size)]
    two = ref[:, at(index // 2 * (2 * size), 2 * size)]
    return jnp.where(index % 2 == 0, two[:, :size], two[:, size:])


def in_order(S, hb, sc, relative, mine, other, out):
    s, c = sc[0], sc[1]
    for m in range(S):
        base = (m if relative else (s ^ m)) * (2 * hb)
        out[at(base + c * hb, hb), :] = mine[m][...]
        out[at(base + (1 - c) * hb, hb), :] = other[m][...]


def qkv_kernel(S, T, hb, sc, *refs):
    x, wm, wo, misc = (refs[i * S : (i + 1) * S] for i in range(4))
    cos, sin = refs[4 * S : 4 * S + 2]
    h, rq, kv, lead, last, wnat, gain_a, gain_m = refs[4 * S + 2 :]
    in_order(S, hb, sc, False, wm, wo, wnat)
    cw = rq.shape[1]
    for m in range(S):
        rows = misc[m][...].astype(F32)
        cols = at((sc[0] ^ m) * (2 * hb), 2 * hb)
        gain_a[:, cols] = rows[0:1, : 2 * hb]
        gain_m[:, cols] = rows[0:1, 2 * hb : 4 * hb]
    for m in range(S):
        normed, _ = norm(x[m][...].astype(F32))
        h[m * T : (m + 1) * T, :] = (normed * gain_a[...]).astype(BF)
    act = mm(h[...], wnat[...])
    rq[...] = turned(act[:, :cw], cos[...], sin[...]).astype(BF)
    kv[:, :cw] = turned(act[:, cw : 2 * cw], cos[...], sin[...]).astype(BF)
    kv[:, cw:] = act[:, 2 * cw :].astype(BF)
    for m in range(S):
        lead[m] = kv[m * T : m * T + WINDOW, :]
        last[m] = kv[(m + 1) * T - WINDOW : (m + 1) * T, :]


def two_heads(x):
    lane = lax.broadcasted_iota(jnp.int32, x.shape, 1)
    first = jnp.where(lane < HEAD, 1.0, 0.0).astype(x.dtype)
    return jnp.concatenate([x * first, x * (1 - first).astype(x.dtype)], axis=0)


def one_pair(x, T):
    lane = lax.broadcasted_iota(jnp.int32, (T, 128), 1)
    return jnp.where(lane < HEAD, x[:T], x[T:])


def extend(m, rows, T, kv, before, after, ext):
    ext[:WINDOW, :] = before[m]
    ext[WINDOW : WINDOW + T, :] = kv[rows, :]
    ext[WINDOW + T :, :] = after[m]


def attend_kernel(S, T, rq, kv, before, after, mask, out, total, ext):
    cw = rq.shape[1]

    def row(m, carry):
        rows = at(m * T, T)
        extend(m, rows, T, kv, before, after, ext)
        ok = mask[rows, :] > 0.0
        ok = jnp.concatenate([ok, ok], axis=0)
        for p in range(cw // 128):
            lanes = slice(p * 128, (p + 1) * 128)
            q = two_heads(rq[rows, lanes])
            k, v = ext[:, lanes], ext[:, cw + p * 128 : cw + (p + 1) * 128]
            scores = jnp.where(ok, mm(q, k, NT) * HEAD ** (-0.5), NEGATIVE)
            top = jnp.max(scores, axis=-1, keepdims=True)
            log_total = top + jnp.log(jnp.sum(jnp.exp(scores - top), axis=-1, keepdims=True))
            prob = jnp.exp(scores - log_total).astype(BF)
            out[rows, lanes] = one_pair(mm(prob, v), T).astype(BF)
            total[rows, 2 * p : 2 * p + 1] = log_total[:T]
            total[rows, 2 * p + 1 : 2 * p + 2] = log_total[T:]
        return carry

    lax.fori_loop(0, S, row, 0)


def attend_back_kernel(S, T, *refs):
    rq, kv, before, after, mask, total, cos, sin = refs[:8]
    d_mix = refs[8 : 8 + S]
    dq, dkv, to_left, to_right, ext, d_all = refs[8 + S :]
    cw = rq.shape[1]
    for m in range(S):
        d_all[m * T : (m + 1) * T, :] = d_mix[m][...]

    def row(m, carry):
        rows = at(m * T, T)
        extend(m, rows, T, kv, before, after, ext)
        ok = mask[rows, :] > 0.0
        ok = jnp.concatenate([ok, ok], axis=0)
        for p in range(cw // 128):
            ks = slice(p * 128, (p + 1) * 128)
            vs = slice(cw + p * 128, cw + (p + 1) * 128)
            q, d = two_heads(rq[rows, ks]), two_heads(d_all[rows, ks])
            k, v = ext[:, ks], ext[:, vs]
            log_total = jnp.concatenate(
                [total[rows, 2 * p : 2 * p + 1], total[rows, 2 * p + 1 : 2 * p + 2]], axis=0
            )
            scores = jnp.where(ok, mm(q, k, NT) * HEAD ** (-0.5), NEGATIVE)
            prob = jnp.exp(scores - log_total)
            d_prob = mm(d, v, NT)
            delta = jnp.sum(prob * d_prob, axis=-1, keepdims=True)
            d_score = (prob * (d_prob - delta)).astype(BF)
            d_val = mm(prob.astype(BF), d, TN)
            d_key = mm(d_score, q, TN) * HEAD ** (-0.5)
            g = one_pair(mm(d_score, k), T) * HEAD ** (-0.5)
            dq[rows, ks] = turned(g, cos[rows, :], -sin[rows, :]).astype(BF)
            for sl, g in ((ks, d_key), (vs, d_val)):
                to_left[m, :, sl] = g[:WINDOW].astype(BF)
                dkv[rows, sl] = g[WINDOW : WINDOW + T]
                to_right[m, :, sl] = g[WINDOW + T :].astype(BF)
        return carry

    lax.fori_loop(0, S, row, 0)


def late_weights_kernel(S, hb, sc, *refs):
    im, io = refs[:S], refs[S : 2 * S]
    gate, lin = refs[2 * S :]
    in_order(S, hb, sc, False, [r.at[:hb] for r in im], [r.at[:hb] for r in io], gate)
    in_order(S, hb, sc, False, [r.at[hb:] for r in im], [r.at[hb:] for r in io], lin)


def up_kernel(S, T, hb, sc, *refs):
    x, att, om, oo = (refs[i * S : (i + 1) * S] for i in range(4))
    gain, gate_w, lin_w = refs[4 * S : 4 * S + 3]
    resid_own, h, gate_in, lin, outw, mixed = refs[4 * S + 3 :]
    in_order(S, hb, sc, True, om, oo, outw)
    cw = att[0].shape[1]
    for m in range(S):
        for j in range(S):
            part = att[j][(m ^ j) * T : ((m ^ j) + 1) * T, :]
            mixed[m * T : (m + 1) * T, j * cw : (j + 1) * cw] = part
    summed = mm(mixed[...], outw[...])
    for m in range(S):
        resid = x[m][...].astype(F32) + summed[m * T : (m + 1) * T]
        if m == 0:
            resid_own[...] = resid
        normed, _ = norm(resid)
        h[m * T : (m + 1) * T, :] = (normed * gain[...]).astype(BF)
    gate_in[...] = mm(h[...], gate_w[...])
    lin[...] = mm(h[...], lin_w[...])


def up_back_kernel(S, T, *refs):
    og = refs[:S]
    gate_in, lin, down, gate_w, lin_w = refs[S : S + 5]
    act, d_gate, d_lin = refs[S + 5 : S + 8]
    pieces = refs[S + 8 : 2 * S + 8]
    both = refs[2 * S + 8]
    for m in range(S):
        both[m * T : (m + 1) * T, :] = og[m][...]
    d_act = mm(both[...], down[...], NT)
    gate, ln = gate_in[...], lin[...]
    cdf = 0.5 * (1.0 + lax.erf(gate * 2.0 ** (-0.5)))
    pdf = jnp.exp(-0.5 * gate * gate) * (2.0 * math.pi) ** (-0.5)
    gelu = gate * cdf
    act[...] = (gelu * ln).astype(BF)
    d_gate[...] = (d_act * ln * (cdf + gate * pdf)).astype(BF)
    d_lin[...] = (d_act * gelu).astype(BF)
    part = mm(d_gate[...], gate_w[...], NT) + mm(d_lin[...], lin_w[...], NT)
    for m in range(S):
        pieces[m][...] = part[m * T : (m + 1) * T].astype(BF)


def resid_back_kernel(S, *refs):
    parts = refs[:S]
    resid, gain, grad, outw = refs[S : S + 4]
    d_resid, d_resid_b, gain_g = refs[S + 4 : S + 7]
    pieces = refs[S + 7 :]
    d_h = parts[0][...].astype(F32)
    for m in range(1, S):
        d_h = d_h + parts[m][...].astype(F32)
    normed, inv_std = norm(resid[...])
    gain_g[...] = jnp.sum(d_h * normed, axis=0, keepdims=True)
    dr = grad[...].astype(F32) + norm_back(d_h * gain[...], normed, inv_std)
    d_resid[...] = dr
    db = dr.astype(BF)
    d_resid_b[...] = db
    cw = pieces[0].shape[1]
    d_att = mm(db, outw[...], NT)
    for m in range(S):
        pieces[m][...] = d_att[:, m * cw : (m + 1) * cw].astype(BF)


def down_grad_kernel(S, T, sc, act, *refs):
    og, (send, keep, both) = refs[:S], refs[S:]
    half = send.shape[1]
    for m in range(S):
        both[m * T : (m + 1) * T, :] = og[m][...]
    for ref, part in ((send, 1 - sc[1]), (keep, sc[1])):
        ref[...] = mm(act[...], both[:, at(part * half, half)], TN).astype(BF)


def in_grad_kernel(S, hb, sc, h, d_gate, d_lin, send, keep, grad):
    fs = d_gate.shape[1]
    for i, d in enumerate((d_gate, d_lin)):
        grad[...] = mm(d[...], h[...], TN)
        for m in range(S):
            for ref, half in ((send, 1 - sc[1]), (keep, sc[1])):
                block = pick(grad, (sc[0] ^ m) * 2 + half, hb)
                ref[i * fs : (i + 1) * fs, m * hb : (m + 1) * hb] = block.astype(BF)


def out_grad_kernel(S, T, sc, att, *refs):
    drb, (send, keep, both, grad) = refs[:S], refs[S:]
    hb = send.shape[1]
    for m in range(S):
        both[m * T : (m + 1) * T, :] = drb[m][...]
    grad[...] = mm(both[...], att[...], TN)
    send[...] = pick(grad, 1 - sc[1], hb).astype(BF)
    keep[...] = pick(grad, sc[1], hb).astype(BF)


def out_parts_kernel(S, T, act, down, *pieces):
    out = mm(act[...], down[...])
    for m in range(S):
        pieces[m][...] = out[m * T : (m + 1) * T].astype(BF)


def qkv_back_kernel(S, T, hb, sc, *refs):
    x = refs[:S]
    dq, dkv, from_left, from_right, cos, sin, h, wnat, gain_m_g = refs[S : S + 9]
    send, keep = refs[S + 9 : S + 11]
    pieces = refs[S + 11 : 2 * S + 11]
    d_qkv, grad, gain_row = refs[2 * S + 11 :]
    cw = dq.shape[1]
    d_qkv[:, :cw] = dq[...]
    for m in range(S):
        for start, edge in ((m * T, from_left), ((m + 1) * T - WINDOW, from_right)):
            rows = slice(start, start + WINDOW)
            dkv[rows, :] = dkv[rows, :] + edge[m].astype(F32)
    d_qkv[:, cw : 2 * cw] = turned(dkv[:, :cw], cos[...], -sin[...]).astype(BF)
    d_qkv[:, 2 * cw :] = dkv[:, cw:].astype(BF)
    grad[...] = mm(d_qkv[...], h[...], TN)
    d_h = mm(d_qkv[...], wnat[...], NT)
    total = None
    for m in range(S):
        part = d_h[m * T : (m + 1) * T]
        pieces[m][...] = part.astype(BF)
        normed, _ = norm(x[m][...].astype(F32))
        part = jnp.sum(part * normed, axis=0, keepdims=True)
        total = part if total is None else total + part
    gain_row[0:1, :] = total
    gain_row[1:2, :] = gain_m_g[...]
    row = lax.broadcasted_iota(jnp.int32, (TAIL, hb), 0)
    for m in range(S):
        lanes = slice(m * hb, (m + 1) * hb)
        base = (sc[0] ^ m) * 2
        tail = jnp.zeros((TAIL, hb), F32)
        for i in range(4):
            line = pick(gain_row, base + i % 2, hb)[i // 2 : i // 2 + 1]
            tail = jnp.where(row == i, jnp.broadcast_to(line, tail.shape), tail)
        for ref, half in ((send, 1 - sc[1]), (keep, sc[1])):
            ref[: 3 * cw, lanes] = pick(grad, base + half, hb).astype(BF)
            ref[3 * cw :, lanes] = tail.astype(BF)


def pair_sum_kernel(S, hb, keep, got, *pieces):
    for m in range(S):
        lanes = slice(m * hb, (m + 1) * hb)
        pieces[m][...] = keep[:, lanes] + got[:, lanes]


def lane_halves_kernel(sc, keep, got, send_z, keep_z):
    half = send_z.shape[1]
    for ref, part in ((send_z, 1 - sc[2]), (keep_z, sc[2])):
        cols = at(part * half, half)
        ref[...] = keep[:, cols] + got[:, cols]


def row_halves_kernel(sc, keep, got, send_z, keep_z):
    half = send_z.shape[0]
    for ref, part in ((send_z, 1 - sc[2]), (keep_z, sc[2])):
        rows = at(part * half, half)
        ref[...] = keep[rows, :] + got[rows, :]


def slot_halves_kernel(S, sc, *refs):
    slots, chunks = refs[:S], refs[S:]
    hb = slots[0].shape[1]
    half = S // 2
    low = (sc[2] == 0).astype(F32).astype(BF)
    high = (sc[2] == 1).astype(F32).astype(BF)
    start = 0
    for send_z, keep_z in (chunks[:2], chunks[2:]):
        stop = start + send_z.shape[0]
        for k in range(half):
            a, b = slots[k][start:stop, :], slots[half + k][start:stop, :]
            lanes = slice(k * hb, (k + 1) * hb)
            keep_z[:, lanes] = a * low + b * high
            send_z[:, lanes] = a * high + b * low
        start = stop


def in_back_kernel(S, *refs):
    parts = refs[:S]
    x, gain, d_resid, out = refs[S:]
    d_h = parts[0][...].astype(F32)
    for m in range(1, S):
        d_h = d_h + parts[m][...].astype(F32)
    normed, inv_std = norm(x[...].astype(F32))
    out[...] = d_resid[...] + norm_back(d_h * gain[...], normed, inv_std)


def down_final_kernel(sc, own, far, own_o, far_o, out):
    half = own.shape[1]
    for part, a, b in ((sc[1], own, far), (1 - sc[1], own_o, far_o)):
        out[:, at((2 * part + sc[2]) * half, half)] = a[...].astype(F32)
        out[:, at((2 * part + 1 - sc[2]) * half, half)] = b[...].astype(F32)


def unit(n):
    rows = lax.broadcasted_iota(jnp.int32, (n, n), 0)
    return jnp.where(rows == lax.broadcasted_iota(jnp.int32, (n, n), 1), 1.0, 0.0).astype(BF)


def in_final_kernel(S, hb, sc, *refs):
    out = refs[-1]
    half = S // 2
    fs = refs[0].shape[0] // 2
    eye = unit(hb)
    for j in range(S):
        m = sc[0] ^ j
        place = jnp.where(m // half == sc[2], 0, half) + m % half
        for part, parts in ((sc[1], refs[:S]), (1 - sc[1], refs[S : 2 * S])):
            block = parts[0][...] * (place == 0).astype(F32).astype(BF)
            for i in range(1, S):
                block = block + parts[i][...] * (place == i).astype(F32).astype(BF)
            block = mm(eye, block, NT)
            for i in range(2):
                start = (i * S + j) * fs
                out[at(part * hb, hb), start : start + fs] = block[:, i * fs : (i + 1) * fs]


def qkv_final_kernel(S, hb, sc, *refs):
    first, second, (out, gain_a, gain_m) = refs[:4], refs[4:8], refs[8:]
    half = S // 2
    D = out.shape[1] // 3
    cw = D // S
    eye = unit(hb)
    low = (sc[2] == 0).astype(F32).astype(BF)
    high = (sc[2] == 1).astype(F32).astype(BF)
    total = None
    for i, part in ((0, sc[1]), (2, 1 - sc[1])):
        for m in range(S):
            lanes = slice((m % half) * hb, (m % half + 1) * hb)
            p, q = (low, high) if m < half else (high, low)
            blocks = [r[i][:, lanes] * p + r[i + 1][:, lanes] * q for r in (first, second)]
            block = jnp.concatenate(blocks, axis=0)
            grad = mm(eye, block[: 3 * cw], NT)
            for k in range(3):
                cols = at(k * D + (sc[0] ^ m) * cw, cw)
                out[at(part * hb, hb), cols] = grad[:, k * cw : (k + 1) * cw]
            if i == 0:
                tail = block[3 * cw :].astype(F32)
                total = tail if total is None else total + tail
    gain_a[:, :hb], gain_a[:, hb:] = total[0:1], total[1:2]
    gain_m[:, :hb], gain_m[:, hb:] = total[2:3], total[3:4]


def out_final_kernel(hb, sc, own, far, own_o, far_o, out):
    half = own.shape[0]
    eye = unit(hb)
    for part, a, b in ((sc[1], own, far), (1 - sc[1], own_o, far_o)):
        out[at(part * hb, hb), at(sc[2] * half, half)] = mm(eye, a[...], NT)
        out[at(part * hb, hb), at((1 - sc[2]) * half, half)] = mm(eye, b[...], NT)


def after(values, *others):
    flat, tree = jax.tree.flatten(values)
    rest = jax.tree.leaves(others)
    out = lax.optimization_barrier(tuple(flat) + tuple(rest))
    return jax.tree.unflatten(tree, out[: len(flat)])


def shards(
    block_in,
    doc_lengths,
    qkv_weight,
    out_weight,
    in_weight,
    down_weight,
    attn_gain,
    mlp_gain,
    out_grad,
):
    S, Q = lax.axis_size("shard"), lax.axis_size("seq")
    Z = Q // 2
    s, q = lax.axis_index("shard"), lax.axis_index("seq")
    c, z = q % 2, q // 2
    kz = ((z + 1) // 2) % 2 if Z == 4 else 0 * z
    sc = jnp.stack([s, c, kz]).astype(jnp.int32)
    T, D = block_in.shape[1:]
    cw = D // S
    hb = D // S // 2
    ff = in_weight.shape[1] // 2
    fs = ff // S

    def permute(x, axis, pairs):
        return lax.ppermute(x, axis, pairs)

    def peer(x, m):
        return permute(x, "shard", [(i, i ^ m) for i in range(S)])

    def core_swap(x):
        return permute(x, "seq", [(i, i ^ 1) for i in range(Q)])

    def along(x, pairs):
        both = [(2 * a + e, 2 * b + e) for a, b in pairs for e in (0, 1)]
        return permute(x, "seq", both)

    def shift(x, step):
        pairs = [(i, i + step) for i in range(Q) if 0 <= i + step < Q]
        return permute(x, "seq", pairs)

    def gather(x):
        return [x] + [peer(x, m) for m in range(1, S)]

    def swap_out(pieces):
        return [pieces[0]] + [peer(pieces[m], m) for m in range(1, S)]

    def line_sum(x):
        half = Z // 2
        for k in range(half - 1):
            x = x + along(x, [(k, k + 1), (Z - 1 - k, Z - 2 - k)])
        if Z > 1:
            x = x + along(x, [(half - 1, half), (half, half - 1)])
        for k in range(half - 1, 0, -1):
            got = along(x, [(k, k - 1), (Z - 1 - k, Z - k)])
            x = jnp.where((z == k - 1) | (z == Z - k), got, x)
        return x

    def z_sum(send, keep):
        if Z == 4:
            near = [(i, i ^ 1) for i in range(Z)]
            part = keep + along(send, near)
            own = part + along(part, [(i, Z - 1 - i) for i in range(Z)])
            far = along(own, near)
        else:
            own, far = line_sum(keep), line_sum(send)
        return own, far

    def both_cores(parts):
        return [*parts, core_swap(parts[0]), core_swap(parts[1])]

    def slots_out(x, other):
        out = []
        for k in range(S // 2):
            pairs = []
            for i in range(S):
                for j in range(Q):
                    half = ((j // 2 + 1) // 2) % 2 if Z == 4 else 0
                    m = (half ^ other) * (S // 2) + k
                    pairs.append((i * Q + j, (i ^ m) * Q + j))
            out.append(permute(x[:, k * hb : (k + 1) * hb], ("shard", "seq"), pairs))
        return out

    def cols(w, start, size):
        return lax.dynamic_slice_in_dim(w, start, size, axis=1)

    x_own = block_in[0]
    row = jnp.concatenate(
        [attn_gain, mlp_gain, (doc_lengths[0] // 64).astype(BF), (doc_lengths[0] % 64).astype(BF)]
    )
    docs = doc_lengths.shape[1]
    rows = jnp.pad(row[None], ((0, TAIL - 1), (0, 640 - row.shape[0])))
    x = gather(x_own)
    misc = gather(rows)

    qkv_half = lax.dynamic_slice_in_dim(qkv_weight, c * hb, hb, axis=0)
    qkv_pieces = [
        jnp.concatenate([cols(qkv_half, i * D + (s ^ m) * cw, cw) for i in range(3)], axis=1)
        for m in range(S)
    ]
    wm = swap_out(qkv_pieces)
    wo = [core_swap(w) for w in wm]

    in_half = lax.dynamic_slice_in_dim(in_weight, c * hb, hb, axis=0)
    out_half = lax.dynamic_slice_in_dim(out_weight, c * hb, hb, axis=0)
    in_pieces = [
        jnp.concatenate([cols(in_half, i * ff + (s ^ m) * fs, fs) for i in range(2)], axis=0)
        for m in range(S)
    ]
    tails = jnp.stack([p[0, 4 * hb : 4 * hb + 2 * docs] for p in misc]).astype(jnp.int32)
    lengths = tails[:, :docs] * 64 + tails[:, docs:]
    ends = jnp.cumsum(lengths, axis=1)
    key_spots = q * T - WINDOW + jnp.arange(T + 2 * WINDOW, dtype=jnp.int32)
    passed = ends[:, :, None] <= key_spots[None, None, :]
    key_segment = jnp.sum(passed.astype(jnp.int32), axis=1)
    start = jnp.sum(jnp.where(passed, lengths[:, :, None], 0), axis=1)
    position = (key_spots[None] - start)[:, WINDOW : WINDOW + T]
    segment = key_segment[:, WINDOW : WINDOW + T]
    spots = key_spots[WINDOW : WINDOW + T]
    near = jnp.abs(spots[:, None] - key_spots[None, :]) <= WINDOW
    valid = (key_spots >= 0) & (key_spots < Q * T)
    mask = (segment[:, :, None] == key_segment[:, None, :]) & (near & valid[None, :])[None]
    mask = mask.astype(F32).reshape(S * T, T + 2 * WINDOW)
    half = HEAD // 2
    freq = jnp.power(10000.0, -(jnp.arange(half).astype(F32) * (2.0 / HEAD)))
    angle = position.reshape(S * T, 1).astype(F32) * freq[None, :]
    cos_h, sin_h = jnp.cos(angle), jnp.sin(angle)
    cos = jnp.concatenate([cos_h] * 4, axis=1)
    sin = jnp.concatenate([-sin_h, sin_h] * 2, axis=1)

    in_pieces = after(in_pieces, cos, sin, mask)
    im = swap_out(in_pieces)
    om = gather(out_half)
    io = [core_swap(w) for w in im]
    oo = [core_swap(w) for w in om]

    h_attn, rq, kv, lead, last, wnat, gain_a, gain_m = call(
        functools.partial(qkv_kernel, S, T, hb),
        (
            sds((S * T, D), BF),
            sds((S * T, cw), BF),
            sds((S * T, 2 * cw), BF),
            sds((S, WINDOW, 2 * cw), BF),
            sds((S, WINDOW, 2 * cw), BF),
            sds((D, 3 * cw), BF),
            sds((1, D), F32),
            sds((1, D), F32),
        ),
        *x,
        *wm,
        *wo,
        *misc,
        cos,
        sin,
        scalars=sc,
    )
    before_kv, after_kv = shift(last, 1), shift(lead, -1)
    ext = pltpu.VMEM((T + 2 * WINDOW, 2 * cw), BF)
    att_own, total = call(
        functools.partial(attend_kernel, S, T),
        (sds((S * T, cw), BF), sds((S * T, cw // HEAD), F32)),
        rq,
        kv,
        before_kv,
        after_kv,
        mask,
        scratch=[ext],
    )
    att = gather(att_own)

    g_own = after(out_grad[0], att_own)
    og = gather(g_own)
    gate_w, lin_w = call(
        functools.partial(late_weights_kernel, S, hb),
        (sds((D, fs), BF), sds((D, fs), BF)),
        *im,
        *io,
        scalars=sc,
    )
    resid_own, h_mlp, gate_in, lin, outw = call(
        functools.partial(up_kernel, S, T, hb),
        (
            sds((T, D), F32),
            sds((S * T, D), BF),
            sds((S * T, fs), F32),
            sds((S * T, fs), F32),
            sds((D, D), BF),
        ),
        *x,
        *att,
        *om,
        *oo,
        gain_m,
        gate_w,
        lin_w,
        scalars=sc,
        scratch=[pltpu.VMEM((S * T, D), BF)],
    )
    wide = pltpu.VMEM((S * T, D), BF)
    mid = call(
        functools.partial(up_back_kernel, S, T),
        (sds((S * T, fs), BF),) * 3 + (sds((T, D), BF),) * S,
        *og,
        gate_in,
        lin,
        down_weight,
        gate_w,
        lin_w,
        scratch=[wide],
    )
    act, d_gate, d_lin = mid[:3]
    d_hmlp = swap_out(mid[3:])

    down_send, down_keep = call(
        functools.partial(down_grad_kernel, S, T),
        (sds((fs, D // 2), BF),) * 2,
        act,
        *og,
        scalars=sc,
        scratch=[wide],
    )
    down_z = call(
        lane_halves_kernel,
        (sds((fs, D // 4), BF),) * 2,
        down_keep,
        core_swap(down_send),
        scalars=sc,
    )
    down_sums = both_cores(z_sum(*down_z))

    in_send, in_keep = call(
        functools.partial(in_grad_kernel, S, hb),
        (sds((2 * fs, D // 2), BF),) * 2,
        h_mlp,
        d_gate,
        d_lin,
        scalars=sc,
        scratch=[pltpu.VMEM((fs, D), F32)],
    )
    in_z = call(
        lane_halves_kernel,
        (sds((2 * fs, D // 4), BF),) * 2,
        in_keep,
        core_swap(in_send),
        scalars=sc,
    )
    in_sums = []
    for k, part in enumerate(z_sum(*in_z)):
        in_sums += slots_out(part, k)
    in_sums += [core_swap(p) for p in in_sums]

    back = call(
        functools.partial(resid_back_kernel, S),
        (sds((T, D), F32), sds((T, D), BF), sds((1, D), F32)) + (sds((T, cw), BF),) * S,
        *d_hmlp,
        resid_own,
        gain_m,
        g_own,
        outw,
    )
    d_resid, d_resid_b, gain_m_g = back[:3]
    d_mix = swap_out(back[3:])

    out_parts = call(
        functools.partial(out_parts_kernel, S, T), (sds((T, D), BF),) * S, act, down_weight
    )
    out_parts = swap_out(out_parts)
    final = resid_own
    for p in out_parts:
        final = final + p.astype(F32)
    final = final.astype(BF)

    dq, dkv, to_left, to_right = call(
        functools.partial(attend_back_kernel, S, T),
        (
            sds((S * T, cw), BF),
            sds((S * T, 2 * cw), F32),
            sds((S, WINDOW, 2 * cw), BF),
            sds((S, WINDOW, 2 * cw), BF),
        ),
        rq,
        kv,
        before_kv,
        after_kv,
        mask,
        total,
        cos,
        sin,
        *d_mix,
        scratch=[ext, pltpu.VMEM((S * T, cw), BF)],
    )
    from_right, from_left = shift(to_left, -1), shift(to_right, 1)

    drb = gather(d_resid_b)
    out_send, out_keep = call(
        functools.partial(out_grad_kernel, S, T),
        (sds((D, hb), BF),) * 2,
        att_own,
        *drb,
        scalars=sc,
        scratch=[wide, pltpu.VMEM((D, cw), F32)],
    )
    out_z = call(
        row_halves_kernel, (sds((D // 2, hb), BF),) * 2, out_keep, core_swap(out_send), scalars=sc
    )
    out_sums = both_cores(z_sum(*out_z))

    res = call(
        functools.partial(qkv_back_kernel, S, T, hb),
        (sds((3 * cw + TAIL, D // 2), BF),) * 2 + (sds((T, D), BF),) * S,
        *x,
        dq,
        dkv,
        from_left,
        from_right,
        cos,
        sin,
        h_attn,
        wnat,
        gain_m_g,
        scalars=sc,
        scratch=[
            pltpu.VMEM((S * T, 3 * cw), BF),
            pltpu.VMEM((3 * cw, D), F32),
            pltpu.VMEM((2, D), F32),
        ],
    )
    qkv_g = call(
        functools.partial(pair_sum_kernel, S, hb),
        (sds((3 * cw + TAIL, hb), BF),) * S,
        res[1],
        core_swap(res[0]),
    )
    cut = 3 * cw // 2
    qkv_z = call(
        functools.partial(slot_halves_kernel, S),
        (sds((cut, D // 4), BF),) * 2 + (sds((cut + TAIL, D // 4), BF),) * 2,
        *swap_out(qkv_g),
        scalars=sc,
    )
    qkv_sums = both_cores(z_sum(*qkv_z[:2]))
    qkv_sums += both_cores(z_sum(*qkv_z[2:]))
    d_hattn = swap_out(res[2:])

    in_rows = call(
        functools.partial(in_back_kernel, S), sds((T, D), F32), *d_hattn, x_own, gain_a, d_resid
    )

    down_grad = call(down_final_kernel, sds((fs, D), F32), *down_sums, scalars=sc)
    in_grad = call(
        functools.partial(in_final_kernel, S, hb), sds((2 * hb, 2 * ff), F32), *in_sums, scalars=sc
    )
    out_wgrad = call(
        functools.partial(out_final_kernel, hb), sds((2 * hb, D), F32), *out_sums, scalars=sc
    )
    qkv_grad, gain_a_grad, gain_m_grad = call(
        functools.partial(qkv_final_kernel, S, hb),
        (
            sds((2 * hb, 3 * D), F32),
            sds((1, 2 * hb), F32),
            sds((1, 2 * hb), F32),
        ),
        *qkv_sums,
        scalars=sc,
    )
    return (
        final[None],
        in_rows[None],
        qkv_grad,
        out_wgrad,
        in_grad,
        down_grad,
        gain_a_grad[0],
        gain_m_grad[0],
    )


def solution(mesh):
    rows = P("shard", "seq", None)
    mat = P("shard", None)
    vec = P("shard")

    return jax.shard_map(
        shards,
        mesh=mesh,
        in_specs=(rows, mat, mat, mat, mat, mat, vec, vec, rows),
        out_specs=(rows, rows, mat, mat, mat, mat, vec, vec),
        check_vma=False,
    )
```

```python
import functools
import math

import jax
import jax.numpy as jnp
from jax import lax
from jax.experimental import pallas as pl
from jax.experimental.pallas import tpu as pltpu
from jax.sharding import PartitionSpec as P


HEAD = 64
WINDOW = 64
EPSILON = 1e-05
NEGATIVE = -1e30
BF = jnp.bfloat16
F32 = jnp.float32
TAIL = 16
NT = ((1,), (1,))
TN = ((0,), (0,))


def mm(a, b, dims=((1,), (0,))):
    return lax.dot_general(a, b, (dims, ((), ())), preferred_element_type=F32)


def call(kernel, out_shape, *args, scalars=None, scratch=()):
    vmem = pl.BlockSpec(memory_space=pltpu.VMEM)
    specs = [vmem] * len(args)
    if scalars is not None:
        specs = [pl.BlockSpec(memory_space=pltpu.SMEM)] + specs
        args = (scalars,) + tuple(args)
    return pl.pallas_call(
        kernel,
        out_shape=out_shape,
        in_specs=specs,
        out_specs=jax.tree.map(lambda _: vmem, out_shape),
        scratch_shapes=list(scratch),
        compiler_params=pltpu.CompilerParams(vmem_limit_bytes=58 << 20),
    )(*args)


def sds(shape, dtype):
    return jax.ShapeDtypeStruct(shape, dtype)


def norm(values):
    centered = values - jnp.mean(values, axis=-1, keepdims=True)
    variance = jnp.mean(centered * centered, axis=-1, keepdims=True)
    inv_std = lax.rsqrt(variance + EPSILON)
    return centered * inv_std, inv_std


def norm_back(scaled, normed, inv_std):
    return inv_std * (
        scaled
        - jnp.mean(scaled, axis=-1, keepdims=True)
        - normed * jnp.mean(scaled * normed, axis=-1, keepdims=True)
    )


def swap_halves(x):
    half = HEAD // 2
    lane = lax.broadcasted_iota(jnp.int32, x.shape, 1)
    return jnp.where(lane % HEAD < half, pltpu.roll(x, 128 - half, 1), pltpu.roll(x, half, 1))


def turned(x, cos, sin):
    blocks = [x[:, i : i + 128] for i in range(0, x.shape[1], 128)]
    return jnp.concatenate([b * cos + swap_halves(b) * sin for b in blocks], axis=1)


def at(start, size):
    return pl.ds(pl.multiple_of(start, size), size)


def pick(ref, index, size):
    if size % 128 == 0:
        return ref[:, at(index * size, size)]
    two = ref[:, at(index // 2 * (2 * size), 2 * size)]
    return jnp.where(index % 2 == 0, two[:, :size], two[:, size:])


def in_order(S, hb, sc, relative, mine, other, out):
    s, c = sc[0], sc[1]
    for m in range(S):
        base = (m if relative else (s ^ m)) * (2 * hb)
        out[at(base + c * hb, hb), :] = mine[m][...]
        out[at(base + (1 - c) * hb, hb), :] = other[m][...]


def qkv_kernel(S, T, hb, sc, *refs):
    x, wm, wo, misc = (refs[i * S : (i + 1) * S] for i in range(4))
    cos, sin = refs[4 * S : 4 * S + 2]
    h, rq, kv, lead, last, wnat, gain_a, gain_m = refs[4 * S + 2 :]
    in_order(S, hb, sc, False, wm, wo, wnat)
    cw = rq.shape[1]
    for m in range(S):
        rows = misc[m][...].astype(F32)
        cols = at((sc[0] ^ m) * (2 * hb), 2 * hb)
        gain_a[:, cols] = rows[0:1, : 2 * hb]
        gain_m[:, cols] = rows[0:1, 2 * hb : 4 * hb]
    for m in range(S):
        normed, _ = norm(x[m][...].astype(F32))
        h[m * T : (m + 1) * T, :] = (normed * gain_a[...]).astype(BF)
    act = mm(h[...], wnat[...])
    rq[...] = turned(act[:, :cw], cos[...], sin[...]).astype(BF)
    kv[:, :cw] = turned(act[:, cw : 2 * cw], cos[...], sin[...]).astype(BF)
    kv[:, cw:] = act[:, 2 * cw :].astype(BF)
    for m in range(S):
        lead[m] = kv[m * T : m * T + WINDOW, :]
        last[m] = kv[(m + 1) * T - WINDOW : (m + 1) * T, :]


def two_heads(x):
    lane = lax.broadcasted_iota(jnp.int32, x.shape, 1)
    first = jnp.where(lane < HEAD, 1.0, 0.0).astype(x.dtype)
    return jnp.concatenate([x * first, x * (1 - first).astype(x.dtype)], axis=0)


def one_pair(x, T):
    lane = lax.broadcasted_iota(jnp.int32, (T, 128), 1)
    return jnp.where(lane < HEAD, x[:T], x[T:])


def extend(m, rows, T, kv, before, after, ext):
    ext[:WINDOW, :] = before[m]
    ext[WINDOW : WINDOW + T, :] = kv[rows, :]
    ext[WINDOW + T :, :] = after[m]


def attend_kernel(S, T, rq, kv, before, after, mask, out, total, ext):
    cw = rq.shape[1]

    def row(m, carry):
        rows = at(m * T, T)
        extend(m, rows, T, kv, before, after, ext)
        ok = mask[rows, :] > 0.0
        ok = jnp.concatenate([ok, ok], axis=0)
        for p in range(cw // 128):
            lanes = slice(p * 128, (p + 1) * 128)
            q = two_heads(rq[rows, lanes])
            k, v = ext[:, lanes], ext[:, cw + p * 128 : cw + (p + 1) * 128]
            scores = jnp.where(ok, mm(q, k, NT) * HEAD ** (-0.5), NEGATIVE)
            top = jnp.max(scores, axis=-1, keepdims=True)
            log_total = top + jnp.log(jnp.sum(jnp.exp(scores - top), axis=-1, keepdims=True))
            prob = jnp.exp(scores - log_total).astype(BF)
            out[rows, lanes] = one_pair(mm(prob, v), T).astype(BF)
            total[rows, 2 * p : 2 * p + 1] = log_total[:T]
            total[rows, 2 * p + 1 : 2 * p + 2] = log_total[T:]
        return carry

    lax.fori_loop(0, S, row, 0)


def attend_back_kernel(S, T, *refs):
    rq, kv, before, after, mask, total, cos, sin = refs[:8]
    d_mix = refs[8 : 8 + S]
    dq, dkv, to_left, to_right, ext, d_all = refs[8 + S :]
    cw = rq.shape[1]
    for m in range(S):
        d_all[m * T : (m + 1) * T, :] = d_mix[m][...]

    def row(m, carry):
        rows = at(m * T, T)
        extend(m, rows, T, kv, before, after, ext)
        ok = mask[rows, :] > 0.0
        ok = jnp.concatenate([ok, ok], axis=0)
        for p in range(cw // 128):
            ks = slice(p * 128, (p + 1) * 128)
            vs = slice(cw + p * 128, cw + (p + 1) * 128)
            q, d = two_heads(rq[rows, ks]), two_heads(d_all[rows, ks])
            k, v = ext[:, ks], ext[:, vs]
            log_total = jnp.concatenate(
                [total[rows, 2 * p : 2 * p + 1], total[rows, 2 * p + 1 : 2 * p + 2]], axis=0
            )
            scores = jnp.where(ok, mm(q, k, NT) * HEAD ** (-0.5), NEGATIVE)
            prob = jnp.exp(scores - log_total)
            d_prob = mm(d, v, NT)
            delta = jnp.sum(prob * d_prob, axis=-1, keepdims=True)
            d_score = (prob * (d_prob - delta)).astype(BF)
            d_val = mm(prob.astype(BF), d, TN)
            d_key = mm(d_score, q, TN) * HEAD ** (-0.5)
            g = one_pair(mm(d_score, k), T) * HEAD ** (-0.5)
            dq[rows, ks] = turned(g, cos[rows, :], -sin[rows, :]).astype(BF)
            for sl, g in ((ks, d_key), (vs, d_val)):
                to_left[m, :, sl] = g[:WINDOW].astype(BF)
                dkv[rows, sl] = g[WINDOW : WINDOW + T]
                to_right[m, :, sl] = g[WINDOW + T :].astype(BF)
        return carry

    lax.fori_loop(0, S, row, 0)


def late_weights_kernel(S, hb, sc, *refs):
    im, io = refs[:S], refs[S : 2 * S]
    gate, lin = refs[2 * S :]
    in_order(S, hb, sc, False, [r.at[:hb] for r in im], [r.at[:hb] for r in io], gate)
    in_order(S, hb, sc, False, [r.at[hb:] for r in im], [r.at[hb:] for r in io], lin)


def up_kernel(S, T, hb, sc, *refs):
    x, att, om, oo = (refs[i * S : (i + 1) * S] for i in range(4))
    gain, gate_w, lin_w = refs[4 * S : 4 * S + 3]
    resid_own, h, gate_in, lin, outw, mixed = refs[4 * S + 3 :]
    in_order(S, hb, sc, True, om, oo, outw)
    cw = att[0].shape[1]
    for m in range(S):
        for j in range(S):
            part = att[j][(m ^ j) * T : ((m ^ j) + 1) * T, :]
            mixed[m * T : (m + 1) * T, j * cw : (j + 1) * cw] = part
    summed = mm(mixed[...], outw[...])
    for m in range(S):
        resid = x[m][...].astype(F32) + summed[m * T : (m + 1) * T]
        if m == 0:
            resid_own[...] = resid
        normed, _ = norm(resid)
        h[m * T : (m + 1) * T, :] = (normed * gain[...]).astype(BF)
    gate_in[...] = mm(h[...], gate_w[...])
    lin[...] = mm(h[...], lin_w[...])


def up_back_kernel(S, T, *refs):
    og = refs[:S]
    gate_in, lin, down, gate_w, lin_w = refs[S : S + 5]
    act, d_gate, d_lin = refs[S + 5 : S + 8]
    pieces = refs[S + 8 : 2 * S + 8]
    both = refs[2 * S + 8]
    for m in range(S):
        both[m * T : (m + 1) * T, :] = og[m][...]
    d_act = mm(both[...], down[...], NT)
    gate, ln = gate_in[...], lin[...]
    cdf = 0.5 * (1.0 + lax.erf(gate * 2.0 ** (-0.5)))
    pdf = jnp.exp(-0.5 * gate * gate) * (2.0 * math.pi) ** (-0.5)
    gelu = gate * cdf
    act[...] = (gelu * ln).astype(BF)
    d_gate[...] = (d_act * ln * (cdf + gate * pdf)).astype(BF)
    d_lin[...] = (d_act * gelu).astype(BF)
    part = mm(d_gate[...], gate_w[...], NT) + mm(d_lin[...], lin_w[...], NT)
    for m in range(S):
        pieces[m][...] = part[m * T : (m + 1) * T].astype(BF)


def resid_back_kernel(S, *refs):
    parts = refs[:S]
    resid, gain, grad, outw = refs[S : S + 4]
    d_resid, d_resid_b, gain_g = refs[S + 4 : S + 7]
    pieces = refs[S + 7 :]
    d_h = parts[0][...].astype(F32)
    for m in range(1, S):
        d_h = d_h + parts[m][...].astype(F32)
    normed, inv_std = norm(resid[...])
    gain_g[...] = jnp.sum(d_h * normed, axis=0, keepdims=True)
    dr = grad[...].astype(F32) + norm_back(d_h * gain[...], normed, inv_std)
    d_resid[...] = dr
    db = dr.astype(BF)
    d_resid_b[...] = db
    cw = pieces[0].shape[1]
    d_att = mm(db, outw[...], NT)
    for m in range(S):
        pieces[m][...] = d_att[:, m * cw : (m + 1) * cw].astype(BF)


def down_grad_kernel(S, T, sc, act, *refs):
    og, (send, keep, both) = refs[:S], refs[S:]
    half = send.shape[1]
    for m in range(S):
        both[m * T : (m + 1) * T, :] = og[m][...]
    for ref, part in ((send, 1 - sc[1]), (keep, sc[1])):
        ref[...] = mm(act[...], both[:, at(part * half, half)], TN).astype(BF)


def in_grad_kernel(S, hb, sc, h, d_gate, d_lin, send, keep, grad):
    fs = d_gate.shape[1]
    for i, d in enumerate((d_gate, d_lin)):
        grad[...] = mm(d[...], h[...], TN)
        for m in range(S):
            for ref, half in ((send, 1 - sc[1]), (keep, sc[1])):
                block = pick(grad, (sc[0] ^ m) * 2 + half, hb)
                ref[i * fs : (i + 1) * fs, m * hb : (m + 1) * hb] = block.astype(BF)


def out_grad_kernel(S, T, sc, att, *refs):
    drb, (send, keep, both, grad) = refs[:S], refs[S:]
    hb = send.shape[1]
    for m in range(S):
        both[m * T : (m + 1) * T, :] = drb[m][...]
    grad[...] = mm(both[...], att[...], TN)
    send[...] = pick(grad, 1 - sc[1], hb).astype(BF)
    keep[...] = pick(grad, sc[1], hb).astype(BF)


def out_parts_kernel(S, T, act, down, *pieces):
    out = mm(act[...], down[...])
    for m in range(S):
        pieces[m][...] = out[m * T : (m + 1) * T].astype(BF)


def qkv_back_kernel(S, T, hb, sc, *refs):
    x = refs[:S]
    dq, dkv, from_left, from_right, cos, sin, h, wnat, gain_m_g = refs[S : S + 9]
    send, keep = refs[S + 9 : S + 11]
    pieces = refs[S + 11 : 2 * S + 11]
    d_qkv, grad, gain_row = refs[2 * S + 11 :]
    cw = dq.shape[1]
    d_qkv[:, :cw] = dq[...]
    for m in range(S):
        for start, edge in ((m * T, from_left), ((m + 1) * T - WINDOW, from_right)):
            rows = slice(start, start + WINDOW)
            dkv[rows, :] = dkv[rows, :] + edge[m].astype(F32)
    d_qkv[:, cw : 2 * cw] = turned(dkv[:, :cw], cos[...], -sin[...]).astype(BF)
    d_qkv[:, 2 * cw :] = dkv[:, cw:].astype(BF)
    grad[...] = mm(d_qkv[...], h[...], TN)
    d_h = mm(d_qkv[...], wnat[...], NT)
    total = None
    for m in range(S):
        part = d_h[m * T : (m + 1) * T]
        pieces[m][...] = part.astype(BF)
        normed, _ = norm(x[m][...].astype(F32))
        part = jnp.sum(part * normed, axis=0, keepdims=True)
        total = part if total is None else total + part
    gain_row[0:1, :] = total
    gain_row[1:2, :] = gain_m_g[...]
    row = lax.broadcasted_iota(jnp.int32, (TAIL, hb), 0)
    for m in range(S):
        lanes = slice(m * hb, (m + 1) * hb)
        base = (sc[0] ^ m) * 2
        tail = jnp.zeros((TAIL, hb), F32)
        for i in range(4):
            line = pick(gain_row, base + i % 2, hb)[i // 2 : i // 2 + 1]
            tail = jnp.where(row == i, jnp.broadcast_to(line, tail.shape), tail)
        for ref, half in ((send, 1 - sc[1]), (keep, sc[1])):
            ref[: 3 * cw, lanes] = pick(grad, base + half, hb).astype(BF)
            ref[3 * cw :, lanes] = tail.astype(BF)


def pair_sum_kernel(S, hb, keep, got, *pieces):
    for m in range(S):
        lanes = slice(m * hb, (m + 1) * hb)
        pieces[m][...] = keep[:, lanes] + got[:, lanes]


def lane_halves_kernel(sc, keep, got, send_z, keep_z):
    half = send_z.shape[1]
    for ref, part in ((send_z, 1 - sc[2]), (keep_z, sc[2])):
        cols = at(part * half, half)
        ref[...] = keep[:, cols] + got[:, cols]


def row_halves_kernel(sc, keep, got, send_z, keep_z):
    half = send_z.shape[0]
    for ref, part in ((send_z, 1 - sc[2]), (keep_z, sc[2])):
        rows = at(part * half, half)
        ref[...] = keep[rows, :] + got[rows, :]


def slot_halves_kernel(S, sc, *refs):
    slots, chunks = refs[:S], refs[S:]
    hb = slots[0].shape[1]
    half = S // 2
    low = (sc[2] == 0).astype(F32).astype(BF)
    high = (sc[2] == 1).astype(F32).astype(BF)
    start = 0
    for send_z, keep_z in (chunks[:2], chunks[2:]):
        stop = start + send_z.shape[0]
        for k in range(half):
            a, b = slots[k][start:stop, :], slots[half + k][start:stop, :]
            lanes = slice(k * hb, (k + 1) * hb)
            keep_z[:, lanes] = a * low + b * high
            send_z[:, lanes] = a * high + b * low
        start = stop


def in_back_kernel(S, *refs):
    parts = refs[:S]
    x, gain, d_resid, out = refs[S:]
    d_h = parts[0][...].astype(F32)
    for m in range(1, S):
        d_h = d_h + parts[m][...].astype(F32)
    normed, inv_std = norm(x[...].astype(F32))
    out[...] = d_resid[...] + norm_back(d_h * gain[...], normed, inv_std)


def down_final_kernel(sc, own, far, own_o, far_o, out):
    half = own.shape[1]
    for part, a, b in ((sc[1], own, far), (1 - sc[1], own_o, far_o)):
        out[:, at((2 * part + sc[2]) * half, half)] = a[...].astype(F32)
        out[:, at((2 * part + 1 - sc[2]) * half, half)] = b[...].astype(F32)


def unit(n):
    rows = lax.broadcasted_iota(jnp.int32, (n, n), 0)
    return jnp.where(rows == lax.broadcasted_iota(jnp.int32, (n, n), 1), 1.0, 0.0).astype(BF)


def in_final_kernel(S, hb, sc, *refs):
    out = refs[-1]
    half = S // 2
    fs = refs[0].shape[0] // 2
    eye = unit(hb)
    for j in range(S):
        m = sc[0] ^ j
        place = jnp.where(m // half == sc[2], 0, half) + m % half
        for part, parts in ((sc[1], refs[:S]), (1 - sc[1], refs[S : 2 * S])):
            block = parts[0][...] * (place == 0).astype(F32).astype(BF)
            for i in range(1, S):
                block = block + parts[i][...] * (place == i).astype(F32).astype(BF)
            block = mm(eye, block, NT)
            for i in range(2):
                start = (i * S + j) * fs
                out[at(part * hb, hb), start : start + fs] = block[:, i * fs : (i + 1) * fs]


def qkv_final_kernel(S, hb, sc, *refs):
    first, second, (out, gain_a, gain_m) = refs[:4], refs[4:8], refs[8:]
    half = S // 2
    D = out.shape[1] // 3
    cw = D // S
    eye = unit(hb)
    low = (sc[2] == 0).astype(F32).astype(BF)
    high = (sc[2] == 1).astype(F32).astype(BF)
    total = None
    for i, part in ((0, sc[1]), (2, 1 - sc[1])):
        for m in range(S):
            lanes = slice((m % half) * hb, (m % half + 1) * hb)
            p, q = (low, high) if m < half else (high, low)
            blocks = [r[i][:, lanes] * p + r[i + 1][:, lanes] * q for r in (first, second)]
            block = jnp.concatenate(blocks, axis=0)
            grad = mm(eye, block[: 3 * cw], NT)
            for k in range(3):
                cols = at(k * D + (sc[0] ^ m) * cw, cw)
                out[at(part * hb, hb), cols] = grad[:, k * cw : (k + 1) * cw]
            if i == 0:
                tail = block[3 * cw :].astype(F32)
                total = tail if total is None else total + tail
    gain_a[:, :hb], gain_a[:, hb:] = total[0:1], total[1:2]
    gain_m[:, :hb], gain_m[:, hb:] = total[2:3], total[3:4]


def out_final_kernel(hb, sc, own, far, own_o, far_o, out):
    half = own.shape[0]
    eye = unit(hb)
    for part, a, b in ((sc[1], own, far), (1 - sc[1], own_o, far_o)):
        out[at(part * hb, hb), at(sc[2] * half, half)] = mm(eye, a[...], NT)
        out[at(part * hb, hb), at((1 - sc[2]) * half, half)] = mm(eye, b[...], NT)


def after(values, *others):
    flat, tree = jax.tree.flatten(values)
    rest = jax.tree.leaves(others)
    out = lax.optimization_barrier(tuple(flat) + tuple(rest))
    return jax.tree.unflatten(tree, out[: len(flat)])


def shards(
    block_in,
    doc_lengths,
    qkv_weight,
    out_weight,
    in_weight,
    down_weight,
    attn_gain,
    mlp_gain,
    out_grad,
):
    S, Q = lax.axis_size("shard"), lax.axis_size("seq")
    Z = Q // 2
    s, q = lax.axis_index("shard"), lax.axis_index("seq")
    c, z = q % 2, q // 2
    kz = ((z + 1) // 2) % 2 if Z == 4 else 0 * z
    sc = jnp.stack([s, c, kz]).astype(jnp.int32)
    T, D = block_in.shape[1:]
    cw = D // S
    hb = D // S // 2
    ff = in_weight.shape[1] // 2
    fs = ff // S

    def permute(x, axis, pairs):
        return lax.ppermute(x, axis, pairs)

    def peer(x, m):
        return permute(x, "shard", [(i, i ^ m) for i in range(S)])

    def core_swap(x):
        return permute(x, "seq", [(i, i ^ 1) for i in range(Q)])

    def along(x, pairs):
        both = [(2 * a + e, 2 * b + e) for a, b in pairs for e in (0, 1)]
        return permute(x, "seq", both)

    def shift(x, step):
        pairs = [(i, i + step) for i in range(Q) if 0 <= i + step < Q]
        return permute(x, "seq", pairs)

    def gather(x):
        return [x] + [peer(x, m) for m in range(1, S)]

    def swap_out(pieces):
        return [pieces[0]] + [peer(pieces[m], m) for m in range(1, S)]

    def line_sum(x):
        half = Z // 2
        for k in range(half - 1):
            x = x + along(x, [(k, k + 1), (Z - 1 - k, Z - 2 - k)])
        if Z > 1:
            x = x + along(x, [(half - 1, half), (half, half - 1)])
        for k in range(half - 1, 0, -1):
            got = along(x, [(k, k - 1), (Z - 1 - k, Z - k)])
            x = jnp.where((z == k - 1) | (z == Z - k), got, x)
        return x

    def z_sum(send, keep):
        if Z == 4:
            near = [(i, i ^ 1) for i in range(Z)]
            part = keep + along(send, near)
            own = part + along(part, [(i, Z - 1 - i) for i in range(Z)])
            far = along(own, near)
        else:
            own, far = line_sum(keep), line_sum(send)
        return own, far

    def both_cores(parts):
        return [*parts, core_swap(parts[0]), core_swap(parts[1])]

    def slots_out(x, other):
        out = []
        for k in range(S // 2):
            pairs = []
            for i in range(S):
                for j in range(Q):
                    half = ((j // 2 + 1) // 2) % 2 if Z == 4 else 0
                    m = (half ^ other) * (S // 2) + k
                    pairs.append((i * Q + j, (i ^ m) * Q + j))
            out.append(permute(x[:, k * hb : (k + 1) * hb], ("shard", "seq"), pairs))
        return out

    def cols(w, start, size):
        return lax.dynamic_slice_in_dim(w, start, size, axis=1)

    x_own = block_in[0]
    row = jnp.concatenate(
        [attn_gain, mlp_gain, (doc_lengths[0] // 64).astype(BF), (doc_lengths[0] % 64).astype(BF)]
    )
    docs = doc_lengths.shape[1]
    rows = jnp.pad(row[None], ((0, TAIL - 1), (0, 640 - row.shape[0])))
    x = gather(x_own)
    misc = gather(rows)

    qkv_half = lax.dynamic_slice_in_dim(qkv_weight, c * hb, hb, axis=0)
    qkv_pieces = [
        jnp.concatenate([cols(qkv_half, i * D + (s ^ m) * cw, cw) for i in range(3)], axis=1)
        for m in range(S)
    ]
    wm = swap_out(qkv_pieces)
    wo = [core_swap(w) for w in wm]

    in_half = lax.dynamic_slice_in_dim(in_weight, c * hb, hb, axis=0)
    out_half = lax.dynamic_slice_in_dim(out_weight, c * hb, hb, axis=0)
    in_pieces = [
        jnp.concatenate([cols(in_half, i * ff + (s ^ m) * fs, fs) for i in range(2)], axis=0)
        for m in range(S)
    ]
    tails = jnp.stack([p[0, 4 * hb : 4 * hb + 2 * docs] for p in misc]).astype(jnp.int32)
    lengths = tails[:, :docs] * 64 + tails[:, docs:]
    ends = jnp.cumsum(lengths, axis=1)
    key_spots = q * T - WINDOW + jnp.arange(T + 2 * WINDOW, dtype=jnp.int32)
    passed = ends[:, :, None] <= key_spots[None, None, :]
    key_segment = jnp.sum(passed.astype(jnp.int32), axis=1)
    start = jnp.sum(jnp.where(passed, lengths[:, :, None], 0), axis=1)
    position = (key_spots[None] - start)[:, WINDOW : WINDOW + T]
    segment = key_segment[:, WINDOW : WINDOW + T]
    spots = key_spots[WINDOW : WINDOW + T]
    near = jnp.abs(spots[:, None] - key_spots[None, :]) <= WINDOW
    valid = (key_spots >= 0) & (key_spots < Q * T)
    mask = (segment[:, :, None] == key_segment[:, None, :]) & (near & valid[None, :])[None]
    mask = mask.astype(F32).reshape(S * T, T + 2 * WINDOW)
    half = HEAD // 2
    freq = jnp.power(10000.0, -(jnp.arange(half).astype(F32) * (2.0 / HEAD)))
    angle = position.reshape(S * T, 1).astype(F32) * freq[None, :]
    cos_h, sin_h = jnp.cos(angle), jnp.sin(angle)
    cos = jnp.concatenate([cos_h] * 4, axis=1)
    sin = jnp.concatenate([-sin_h, sin_h] * 2, axis=1)

    in_pieces = after(in_pieces, cos, sin, mask)
    im = swap_out(in_pieces)
    om = gather(out_half)
    io = [core_swap(w) for w in im]
    oo = [core_swap(w) for w in om]

    h_attn, rq, kv, lead, last, wnat, gain_a, gain_m = call(
        functools.partial(qkv_kernel, S, T, hb),
        (
            sds((S * T, D), BF),
            sds((S * T, cw), BF),
            sds((S * T, 2 * cw), BF),
            sds((S, WINDOW, 2 * cw), BF),
            sds((S, WINDOW, 2 * cw), BF),
            sds((D, 3 * cw), BF),
            sds((1, D), F32),
            sds((1, D), F32),
        ),
        *x,
        *wm,
        *wo,
        *misc,
        cos,
        sin,
        scalars=sc,
    )
    before_kv, after_kv = shift(last, 1), shift(lead, -1)
    ext = pltpu.VMEM((T + 2 * WINDOW, 2 * cw), BF)
    att_own, total = call(
        functools.partial(attend_kernel, S, T),
        (sds((S * T, cw), BF), sds((S * T, cw // HEAD), F32)),
        rq,
        kv,
        before_kv,
        after_kv,
        mask,
        scratch=[ext],
    )
    att = gather(att_own)

    g_own = after(out_grad[0], att_own)
    og = gather(g_own)
    gate_w, lin_w = call(
        functools.partial(late_weights_kernel, S, hb),
        (sds((D, fs), BF), sds((D, fs), BF)),
        *im,
        *io,
        scalars=sc,
    )
    resid_own, h_mlp, gate_in, lin, outw = call(
        functools.partial(up_kernel, S, T, hb),
        (
            sds((T, D), F32),
            sds((S * T, D), BF),
            sds((S * T, fs), F32),
            sds((S * T, fs), F32),
            sds((D, D), BF),
        ),
        *x,
        *att,
        *om,
        *oo,
        gain_m,
        gate_w,
        lin_w,
        scalars=sc,
        scratch=[pltpu.VMEM((S * T, D), BF)],
    )
    wide = pltpu.VMEM((S * T, D), BF)
    mid = call(
        functools.partial(up_back_kernel, S, T),
        (sds((S * T, fs), BF),) * 3 + (sds((T, D), BF),) * S,
        *og,
        gate_in,
        lin,
        down_weight,
        gate_w,
        lin_w,
        scratch=[wide],
    )
    act, d_gate, d_lin = mid[:3]
    d_hmlp = swap_out(mid[3:])

    down_send, down_keep = call(
        functools.partial(down_grad_kernel, S, T),
        (sds((fs, D // 2), BF),) * 2,
        act,
        *og,
        scalars=sc,
        scratch=[wide],
    )
    down_z = call(
        lane_halves_kernel,
        (sds((fs, D // 4), BF),) * 2,
        down_keep,
        core_swap(down_send),
        scalars=sc,
    )
    down_sums = both_cores(z_sum(*down_z))

    in_send, in_keep = call(
        functools.partial(in_grad_kernel, S, hb),
        (sds((2 * fs, D // 2), BF),) * 2,
        h_mlp,
        d_gate,
        d_lin,
        scalars=sc,
        scratch=[pltpu.VMEM((fs, D), F32)],
    )
    in_z = call(
        lane_halves_kernel,
        (sds((2 * fs, D // 4), BF),) * 2,
        in_keep,
        core_swap(in_send),
        scalars=sc,
    )
    own, far = z_sum(*in_z)
    own, far = slots_out(own, 0), slots_out(far, 1)
    in_sums = own + far + [core_swap(p) for p in own] + [core_swap(p) for p in far]

    back = call(
        functools.partial(resid_back_kernel, S),
        (sds((T, D), F32), sds((T, D), BF), sds((1, D), F32)) + (sds((T, cw), BF),) * S,
        *d_hmlp,
        resid_own,
        gain_m,
        g_own,
        outw,
    )
    d_resid, d_resid_b, gain_m_g = back[:3]
    d_mix = swap_out(back[3:])

    out_parts = call(
        functools.partial(out_parts_kernel, S, T), (sds((T, D), BF),) * S, act, down_weight
    )
    out_parts = swap_out(out_parts)
    final = resid_own
    for p in out_parts:
        final = final + p.astype(F32)
    final = final.astype(BF)

    dq, dkv, to_left, to_right = call(
        functools.partial(attend_back_kernel, S, T),
        (
            sds((S * T, cw), BF),
            sds((S * T, 2 * cw), F32),
            sds((S, WINDOW, 2 * cw), BF),
            sds((S, WINDOW, 2 * cw), BF),
        ),
        rq,
        kv,
        before_kv,
        after_kv,
        mask,
        total,
        cos,
        sin,
        *d_mix,
        scratch=[ext, pltpu.VMEM((S * T, cw), BF)],
    )
    from_right, from_left = shift(to_left, -1), shift(to_right, 1)

    drb = gather(d_resid_b)
    out_send, out_keep = call(
        functools.partial(out_grad_kernel, S, T),
        (sds((D, hb), BF),) * 2,
        att_own,
        *drb,
        scalars=sc,
        scratch=[wide, pltpu.VMEM((D, cw), F32)],
    )
    out_z = call(
        row_halves_kernel, (sds((D // 2, hb), BF),) * 2, out_keep, core_swap(out_send), scalars=sc
    )
    out_sums = both_cores(z_sum(*out_z))

    res = call(
        functools.partial(qkv_back_kernel, S, T, hb),
        (sds((3 * cw + TAIL, D // 2), BF),) * 2 + (sds((T, D), BF),) * S,
        *x,
        dq,
        dkv,
        from_left,
        from_right,
        cos,
        sin,
        h_attn,
        wnat,
        gain_m_g,
        scalars=sc,
        scratch=[
            pltpu.VMEM((S * T, 3 * cw), BF),
            pltpu.VMEM((3 * cw, D), F32),
            pltpu.VMEM((2, D), F32),
        ],
    )
    qkv_g = call(
        functools.partial(pair_sum_kernel, S, hb),
        (sds((3 * cw + TAIL, hb), BF),) * S,
        res[1],
        core_swap(res[0]),
    )
    cut = 3 * cw // 2
    qkv_z = call(
        functools.partial(slot_halves_kernel, S),
        (sds((cut, D // 4), BF),) * 2 + (sds((cut + TAIL, D // 4), BF),) * 2,
        *swap_out(qkv_g),
        scalars=sc,
    )
    qkv_sums = both_cores(z_sum(*qkv_z[:2]))
    qkv_sums += both_cores(z_sum(*qkv_z[2:]))
    d_hattn = swap_out(res[2:])

    in_rows = call(
        functools.partial(in_back_kernel, S), sds((T, D), F32), *d_hattn, x_own, gain_a, d_resid
    )

    down_grad = call(down_final_kernel, sds((fs, D), F32), *down_sums, scalars=sc)
    in_grad = call(
        functools.partial(in_final_kernel, S, hb), sds((2 * hb, 2 * ff), F32), *in_sums, scalars=sc
    )
    out_wgrad = call(
        functools.partial(out_final_kernel, hb), sds((2 * hb, D), F32), *out_sums, scalars=sc
    )
    qkv_grad, gain_a_grad, gain_m_grad = call(
        functools.partial(qkv_final_kernel, S, hb),
        (
            sds((2 * hb, 3 * D), F32),
            sds((1, 2 * hb), F32),
            sds((1, 2 * hb), F32),
        ),
        *qkv_sums,
        scalars=sc,
    )
    return (
        final[None],
        in_rows[None],
        qkv_grad,
        out_wgrad,
        in_grad,
        down_grad,
        gain_a_grad[0],
        gain_m_grad[0],
    )


def solution(mesh):
    rows = P("shard", "seq", None)
    mat = P("shard", None)
    vec = P("shard")

    return jax.shard_map(
        shards,
        mesh=mesh,
        in_specs=(rows, mat, mat, mat, mat, mat, vec, vec, rows),
        out_specs=(rows, rows, mat, mat, mat, mat, vec, vec),
        check_vma=False,
    )
```

```python
import functools
import math

import jax
import jax.numpy as jnp
from jax import lax
from jax.experimental import pallas as pl
from jax.experimental.pallas import tpu as pltpu
from jax.sharding import PartitionSpec as P


HEAD = 64
WINDOW = 64
EPSILON = 1e-05
NEGATIVE = -1e30
BF = jnp.bfloat16
F32 = jnp.float32
TAIL = 16
NT = ((1,), (1,))
TN = ((0,), (0,))


def mm(a, b, dims=((1,), (0,))):
    return lax.dot_general(a, b, (dims, ((), ())), preferred_element_type=F32)


def call(kernel, out_shape, *args, scalars=None, scratch=()):
    vmem = pl.BlockSpec(memory_space=pltpu.VMEM)
    specs = [vmem] * len(args)
    if scalars is not None:
        specs = [pl.BlockSpec(memory_space=pltpu.SMEM)] + specs
        args = (scalars,) + tuple(args)
    return pl.pallas_call(
        kernel,
        out_shape=out_shape,
        in_specs=specs,
        out_specs=jax.tree.map(lambda _: vmem, out_shape),
        scratch_shapes=list(scratch),
        compiler_params=pltpu.CompilerParams(vmem_limit_bytes=58 << 20),
    )(*args)


def sds(shape, dtype):
    return jax.ShapeDtypeStruct(shape, dtype)


def norm(values):
    centered = values - jnp.mean(values, axis=-1, keepdims=True)
    variance = jnp.mean(centered * centered, axis=-1, keepdims=True)
    inv_std = lax.rsqrt(variance + EPSILON)
    return centered * inv_std, inv_std


def norm_back(scaled, normed, inv_std):
    return inv_std * (
        scaled
        - jnp.mean(scaled, axis=-1, keepdims=True)
        - normed * jnp.mean(scaled * normed, axis=-1, keepdims=True)
    )


def swap_halves(x):
    half = HEAD // 2
    lane = lax.broadcasted_iota(jnp.int32, x.shape, 1)
    return jnp.where(lane % HEAD < half, pltpu.roll(x, 128 - half, 1), pltpu.roll(x, half, 1))


def turned(x, cos, sin):
    blocks = [x[:, i : i + 128] for i in range(0, x.shape[1], 128)]
    return jnp.concatenate([b * cos + swap_halves(b) * sin for b in blocks], axis=1)


def at(start, size):
    return pl.ds(pl.multiple_of(start, size), size)


def pick(ref, index, size):
    if size % 128 == 0:
        return ref[:, at(index * size, size)]
    two = ref[:, at(index // 2 * (2 * size), 2 * size)]
    return jnp.where(index % 2 == 0, two[:, :size], two[:, size:])


def in_order(S, hb, sc, relative, mine, other, out):
    s, c = sc[0], sc[1]
    for m in range(S):
        base = (m if relative else (s ^ m)) * (2 * hb)
        out[at(base + c * hb, hb), :] = mine[m][...]
        out[at(base + (1 - c) * hb, hb), :] = other[m][...]


def qkv_kernel(S, T, hb, sc, *refs):
    x, wm, wo, misc = (refs[i * S : (i + 1) * S] for i in range(4))
    cos, sin = refs[4 * S : 4 * S + 2]
    h, rq, kv, lead, last, wnat, gain_a, gain_m = refs[4 * S + 2 :]
    in_order(S, hb, sc, False, wm, wo, wnat)
    cw = rq.shape[1]
    for m in range(S):
        rows = misc[m][...].astype(F32)
        cols = at((sc[0] ^ m) * (2 * hb), 2 * hb)
        gain_a[:, cols] = rows[0:1, : 2 * hb]
        gain_m[:, cols] = rows[0:1, 2 * hb : 4 * hb]
    for m in range(S):
        normed, _ = norm(x[m][...].astype(F32))
        h[m * T : (m + 1) * T, :] = (normed * gain_a[...]).astype(BF)
    act = mm(h[...], wnat[...])
    rq[...] = turned(act[:, :cw], cos[...], sin[...]).astype(BF)
    kv[:, :cw] = turned(act[:, cw : 2 * cw], cos[...], sin[...]).astype(BF)
    kv[:, cw:] = act[:, 2 * cw :].astype(BF)
    for m in range(S):
        lead[m] = kv[m * T : m * T + WINDOW, :]
        last[m] = kv[(m + 1) * T - WINDOW : (m + 1) * T, :]


def two_heads(x):
    lane = lax.broadcasted_iota(jnp.int32, x.shape, 1)
    first = jnp.where(lane < HEAD, 1.0, 0.0).astype(x.dtype)
    return jnp.concatenate([x * first, x * (1 - first).astype(x.dtype)], axis=0)


def one_pair(x, T):
    lane = lax.broadcasted_iota(jnp.int32, (T, 128), 1)
    return jnp.where(lane < HEAD, x[:T], x[T:])


def extend(m, rows, T, kv, before, after, ext):
    ext[:WINDOW, :] = before[m]
    ext[WINDOW : WINDOW + T, :] = kv[rows, :]
    ext[WINDOW + T :, :] = after[m]


def attend_kernel(S, T, rq, kv, before, after, mask, out, total, ext):
    cw = rq.shape[1]

    def row(m, carry):
        rows = at(m * T, T)
        extend(m, rows, T, kv, before, after, ext)
        ok = mask[rows, :] > 0.0
        ok = jnp.concatenate([ok, ok], axis=0)
        for p in range(cw // 128):
            lanes = slice(p * 128, (p + 1) * 128)
            q = two_heads(rq[rows, lanes])
            k, v = ext[:, lanes], ext[:, cw + p * 128 : cw + (p + 1) * 128]
            scores = jnp.where(ok, mm(q, k, NT) * HEAD ** (-0.5), NEGATIVE)
            top = jnp.max(scores, axis=-1, keepdims=True)
            log_total = top + jnp.log(jnp.sum(jnp.exp(scores - top), axis=-1, keepdims=True))
            prob = jnp.exp(scores - log_total).astype(BF)
            out[rows, lanes] = one_pair(mm(prob, v), T).astype(BF)
            total[rows, 2 * p : 2 * p + 1] = log_total[:T]
            total[rows, 2 * p + 1 : 2 * p + 2] = log_total[T:]
        return carry

    lax.fori_loop(0, S, row, 0, unroll=2)


def attend_back_kernel(S, T, *refs):
    rq, kv, before, after, mask, total, cos, sin = refs[:8]
    d_mix = refs[8 : 8 + S]
    dq, dkv, to_left, to_right, ext, d_all = refs[8 + S :]
    cw = rq.shape[1]
    for m in range(S):
        d_all[m * T : (m + 1) * T, :] = d_mix[m][...]

    def row(m, carry):
        rows = at(m * T, T)
        extend(m, rows, T, kv, before, after, ext)
        ok = mask[rows, :] > 0.0
        ok = jnp.concatenate([ok, ok], axis=0)
        for p in range(cw // 128):
            ks = slice(p * 128, (p + 1) * 128)
            vs = slice(cw + p * 128, cw + (p + 1) * 128)
            q, d = two_heads(rq[rows, ks]), two_heads(d_all[rows, ks])
            k, v = ext[:, ks], ext[:, vs]
            log_total = jnp.concatenate(
                [total[rows, 2 * p : 2 * p + 1], total[rows, 2 * p + 1 : 2 * p + 2]], axis=0
            )
            scores = jnp.where(ok, mm(q, k, NT) * HEAD ** (-0.5), NEGATIVE)
            prob = jnp.exp(scores - log_total)
            d_prob = mm(d, v, NT)
            delta = jnp.sum(prob * d_prob, axis=-1, keepdims=True)
            d_score = (prob * (d_prob - delta)).astype(BF)
            d_val = mm(prob.astype(BF), d, TN)
            d_key = mm(d_score, q, TN) * HEAD ** (-0.5)
            g = one_pair(mm(d_score, k), T) * HEAD ** (-0.5)
            dq[rows, ks] = turned(g, cos[rows, :], -sin[rows, :]).astype(BF)
            for sl, g in ((ks, d_key), (vs, d_val)):
                to_left[m, :, sl] = g[:WINDOW].astype(BF)
                dkv[rows, sl] = g[WINDOW : WINDOW + T]
                to_right[m, :, sl] = g[WINDOW + T :].astype(BF)
        return carry

    lax.fori_loop(0, S, row, 0, unroll=2)


def late_weights_kernel(S, hb, sc, *refs):
    im, io = refs[:S], refs[S : 2 * S]
    gate, lin = refs[2 * S :]
    in_order(S, hb, sc, False, [r.at[:hb] for r in im], [r.at[:hb] for r in io], gate)
    in_order(S, hb, sc, False, [r.at[hb:] for r in im], [r.at[hb:] for r in io], lin)


def up_kernel(S, T, hb, sc, *refs):
    x, att, om, oo = (refs[i * S : (i + 1) * S] for i in range(4))
    gain, gate_w, lin_w = refs[4 * S : 4 * S + 3]
    resid_own, h, gate_in, lin, outw, mixed = refs[4 * S + 3 :]
    in_order(S, hb, sc, True, om, oo, outw)
    cw = att[0].shape[1]
    for m in range(S):
        for j in range(S):
            part = att[j][(m ^ j) * T : ((m ^ j) + 1) * T, :]
            mixed[m * T : (m + 1) * T, j * cw : (j + 1) * cw] = part
    summed = mm(mixed[...], outw[...])
    for m in range(S):
        resid = x[m][...].astype(F32) + summed[m * T : (m + 1) * T]
        if m == 0:
            resid_own[...] = resid
        normed, _ = norm(resid)
        h[m * T : (m + 1) * T, :] = (normed * gain[...]).astype(BF)
    gate_in[...] = mm(h[...], gate_w[...])
    lin[...] = mm(h[...], lin_w[...])


def up_back_kernel(S, T, *refs):
    og = refs[:S]
    gate_in, lin, down, gate_w, lin_w = refs[S : S + 5]
    act, d_gate, d_lin = refs[S + 5 : S + 8]
    pieces = refs[S + 8 : 2 * S + 8]
    both = refs[2 * S + 8]
    for m in range(S):
        both[m * T : (m + 1) * T, :] = og[m][...]
    d_act = mm(both[...], down[...], NT)
    gate, ln = gate_in[...], lin[...]
    cdf = 0.5 * (1.0 + lax.erf(gate * 2.0 ** (-0.5)))
    pdf = jnp.exp(-0.5 * gate * gate) * (2.0 * math.pi) ** (-0.5)
    gelu = gate * cdf
    act[...] = (gelu * ln).astype(BF)
    d_gate[...] = (d_act * ln * (cdf + gate * pdf)).astype(BF)
    d_lin[...] = (d_act * gelu).astype(BF)
    part = mm(d_gate[...], gate_w[...], NT) + mm(d_lin[...], lin_w[...], NT)
    for m in range(S):
        pieces[m][...] = part[m * T : (m + 1) * T].astype(BF)


def resid_back_kernel(S, *refs):
    parts = refs[:S]
    resid, gain, grad, outw = refs[S : S + 4]
    d_resid, d_resid_b, gain_g = refs[S + 4 : S + 7]
    pieces = refs[S + 7 :]
    d_h = parts[0][...].astype(F32)
    for m in range(1, S):
        d_h = d_h + parts[m][...].astype(F32)
    normed, inv_std = norm(resid[...])
    gain_g[...] = jnp.sum(d_h * normed, axis=0, keepdims=True)
    dr = grad[...].astype(F32) + norm_back(d_h * gain[...], normed, inv_std)
    d_resid[...] = dr
    db = dr.astype(BF)
    d_resid_b[...] = db
    cw = pieces[0].shape[1]
    d_att = mm(db, outw[...], NT)
    for m in range(S):
        pieces[m][...] = d_att[:, m * cw : (m + 1) * cw].astype(BF)


def down_grad_kernel(S, T, sc, act, *refs):
    og, (send, keep, both) = refs[:S], refs[S:]
    half = send.shape[1]
    for m in range(S):
        both[m * T : (m + 1) * T, :] = og[m][...]
    for ref, part in ((send, 1 - sc[1]), (keep, sc[1])):
        ref[...] = mm(act[...], both[:, at(part * half, half)], TN).astype(BF)


def in_grad_kernel(S, hb, sc, h, d_gate, d_lin, send, keep, grad):
    fs = d_gate.shape[1]
    for i, d in enumerate((d_gate, d_lin)):
        grad[...] = mm(d[...], h[...], TN)
        for m in range(S):
            for ref, half in ((send, 1 - sc[1]), (keep, sc[1])):
                block = pick(grad, (sc[0] ^ m) * 2 + half, hb)
                ref[i * fs : (i + 1) * fs, m * hb : (m + 1) * hb] = block.astype(BF)


def out_grad_kernel(S, T, sc, att, *refs):
    drb, (send, keep, both, grad) = refs[:S], refs[S:]
    hb = send.shape[1]
    for m in range(S):
        both[m * T : (m + 1) * T, :] = drb[m][...]
    grad[...] = mm(both[...], att[...], TN)
    send[...] = pick(grad, 1 - sc[1], hb).astype(BF)
    keep[...] = pick(grad, sc[1], hb).astype(BF)


def out_parts_kernel(S, T, act, down, *pieces):
    out = mm(act[...], down[...])
    for m in range(S):
        pieces[m][...] = out[m * T : (m + 1) * T].astype(BF)


def qkv_back_kernel(S, T, hb, sc, *refs):
    x = refs[:S]
    dq, dkv, from_left, from_right, cos, sin, h, wnat, gain_m_g = refs[S : S + 9]
    send, keep = refs[S + 9 : S + 11]
    pieces = refs[S + 11 : 2 * S + 11]
    d_qkv, grad, gain_row = refs[2 * S + 11 :]
    cw = dq.shape[1]
    d_qkv[:, :cw] = dq[...]
    for m in range(S):
        for start, edge in ((m * T, from_left), ((m + 1) * T - WINDOW, from_right)):
            rows = slice(start, start + WINDOW)
            dkv[rows, :] = dkv[rows, :] + edge[m].astype(F32)
    d_qkv[:, cw : 2 * cw] = turned(dkv[:, :cw], cos[...], -sin[...]).astype(BF)
    d_qkv[:, 2 * cw :] = dkv[:, cw:].astype(BF)
    grad[...] = mm(d_qkv[...], h[...], TN)
    d_h = mm(d_qkv[...], wnat[...], NT)
    total = None
    for m in range(S):
        part = d_h[m * T : (m + 1) * T]
        pieces[m][...] = part.astype(BF)
        normed, _ = norm(x[m][...].astype(F32))
        part = jnp.sum(part * normed, axis=0, keepdims=True)
        total = part if total is None else total + part
    gain_row[0:1, :] = total
    gain_row[1:2, :] = gain_m_g[...]
    row = lax.broadcasted_iota(jnp.int32, (TAIL, hb), 0)
    for m in range(S):
        lanes = slice(m * hb, (m + 1) * hb)
        base = (sc[0] ^ m) * 2
        tail = jnp.zeros((TAIL, hb), F32)
        for i in range(4):
            line = pick(gain_row, base + i % 2, hb)[i // 2 : i // 2 + 1]
            tail = jnp.where(row == i, jnp.broadcast_to(line, tail.shape), tail)
        for ref, half in ((send, 1 - sc[1]), (keep, sc[1])):
            ref[: 3 * cw, lanes] = pick(grad, base + half, hb).astype(BF)
            ref[3 * cw :, lanes] = tail.astype(BF)


def pair_sum_kernel(S, hb, keep, got, *pieces):
    for m in range(S):
        lanes = slice(m * hb, (m + 1) * hb)
        pieces[m][...] = keep[:, lanes] + got[:, lanes]


def lane_halves_kernel(sc, keep, got, send_z, keep_z):
    half = send_z.shape[1]
    for ref, part in ((send_z, 1 - sc[2]), (keep_z, sc[2])):
        cols = at(part * half, half)
        ref[...] = keep[:, cols] + got[:, cols]


def row_halves_kernel(sc, keep, got, send_z, keep_z):
    half = send_z.shape[0]
    for ref, part in ((send_z, 1 - sc[2]), (keep_z, sc[2])):
        rows = at(part * half, half)
        ref[...] = keep[rows, :] + got[rows, :]


def slot_halves_kernel(S, sc, *refs):
    slots, chunks = refs[:S], refs[S:]
    hb = slots[0].shape[1]
    half = S // 2
    low = (sc[2] == 0).astype(F32).astype(BF)
    high = (sc[2] == 1).astype(F32).astype(BF)
    start = 0
    for send_z, keep_z in (chunks[:2], chunks[2:]):
        stop = start + send_z.shape[0]
        for k in range(half):
            a, b = slots[k][start:stop, :], slots[half + k][start:stop, :]
            lanes = slice(k * hb, (k + 1) * hb)
            keep_z[:, lanes] = a * low + b * high
            send_z[:, lanes] = a * high + b * low
        start = stop


def in_back_kernel(S, *refs):
    parts = refs[:S]
    x, gain, d_resid, out = refs[S:]
    d_h = parts[0][...].astype(F32)
    for m in range(1, S):
        d_h = d_h + parts[m][...].astype(F32)
    normed, inv_std = norm(x[...].astype(F32))
    out[...] = d_resid[...] + norm_back(d_h * gain[...], normed, inv_std)


def down_final_kernel(sc, own, far, own_o, far_o, out):
    half = own.shape[1]
    for part, a, b in ((sc[1], own, far), (1 - sc[1], own_o, far_o)):
        out[:, at((2 * part + sc[2]) * half, half)] = a[...].astype(F32)
        out[:, at((2 * part + 1 - sc[2]) * half, half)] = b[...].astype(F32)


def unit(n):
    rows = lax.broadcasted_iota(jnp.int32, (n, n), 0)
    return jnp.where(rows == lax.broadcasted_iota(jnp.int32, (n, n), 1), 1.0, 0.0).astype(BF)


def in_final_kernel(S, hb, sc, *refs):
    out, all_parts = refs[-2:]
    half = S // 2
    fs = refs[0].shape[0] // 2
    eye = unit(hb)
    for i in range(2 * S):
        all_parts[i] = refs[i][...]
    for j in range(S):
        m = sc[0] ^ j
        place = jnp.where(m // half == sc[2], 0, half) + m % half
        for first, part in ((0, sc[1]), (S, 1 - sc[1])):
            block = all_parts[first + place]
            block = mm(eye, block, NT)
            for i in range(2):
                start = (i * S + j) * fs
                out[at(part * hb, hb), start : start + fs] = block[:, i * fs : (i + 1) * fs]


def qkv_final_kernel(S, hb, sc, *refs):
    first, second, (out, gain_a, gain_m) = refs[:4], refs[4:8], refs[8:]
    half = S // 2
    D = out.shape[1] // 3
    cw = D // S
    eye = unit(hb)
    low = (sc[2] == 0).astype(F32).astype(BF)
    high = (sc[2] == 1).astype(F32).astype(BF)
    total = None
    for i, part in ((0, sc[1]), (2, 1 - sc[1])):
        for m in range(S):
            lanes = slice((m % half) * hb, (m % half + 1) * hb)
            p, q = (low, high) if m < half else (high, low)
            blocks = [r[i][:, lanes] * p + r[i + 1][:, lanes] * q for r in (first, second)]
            block = jnp.concatenate(blocks, axis=0)
            grad = mm(eye, block[: 3 * cw], NT)
            for k in range(3):
                cols = at(k * D + (sc[0] ^ m) * cw, cw)
                out[at(part * hb, hb), cols] = grad[:, k * cw : (k + 1) * cw]
            if i == 0:
                tail = block[3 * cw :].astype(F32)
                total = tail if total is None else total + tail
    gain_a[:, :hb], gain_a[:, hb:] = total[0:1], total[1:2]
    gain_m[:, :hb], gain_m[:, hb:] = total[2:3], total[3:4]


def out_final_kernel(hb, sc, own, far, own_o, far_o, out):
    half = own.shape[0]
    eye = unit(hb)
    for part, a, b in ((sc[1], own, far), (1 - sc[1], own_o, far_o)):
        out[at(part * hb, hb), at(sc[2] * half, half)] = mm(eye, a[...], NT)
        out[at(part * hb, hb), at((1 - sc[2]) * half, half)] = mm(eye, b[...], NT)


def after(values, *others):
    flat, tree = jax.tree.flatten(values)
    rest = jax.tree.leaves(others)
    out = lax.optimization_barrier(tuple(flat) + tuple(rest))
    return jax.tree.unflatten(tree, out[: len(flat)])


def shards(
    block_in,
    doc_lengths,
    qkv_weight,
    out_weight,
    in_weight,
    down_weight,
    attn_gain,
    mlp_gain,
    out_grad,
):
    S, Q = lax.axis_size("shard"), lax.axis_size("seq")
    Z = Q // 2
    s, q = lax.axis_index("shard"), lax.axis_index("seq")
    c, z = q % 2, q // 2
    kz = ((z + 1) // 2) % 2 if Z == 4 else 0 * z
    sc = jnp.stack([s, c, kz]).astype(jnp.int32)
    T, D = block_in.shape[1:]
    cw = D // S
    hb = D // S // 2
    ff = in_weight.shape[1] // 2
    fs = ff // S

    def permute(x, axis, pairs):
        return lax.ppermute(x, axis, pairs)

    def peer(x, m):
        return permute(x, "shard", [(i, i ^ m) for i in range(S)])

    def core_swap(x):
        return permute(x, "seq", [(i, i ^ 1) for i in range(Q)])

    def along(x, pairs):
        both = [(2 * a + e, 2 * b + e) for a, b in pairs for e in (0, 1)]
        return permute(x, "seq", both)

    def shift(x, step):
        pairs = [(i, i + step) for i in range(Q) if 0 <= i + step < Q]
        return permute(x, "seq", pairs)

    def gather(x):
        return [x] + [peer(x, m) for m in range(1, S)]

    def swap_out(pieces):
        return [pieces[0]] + [peer(pieces[m], m) for m in range(1, S)]

    def line_sum(x):
        half = Z // 2
        for k in range(half - 1):
            x = x + along(x, [(k, k + 1), (Z - 1 - k, Z - 2 - k)])
        if Z > 1:
            x = x + along(x, [(half - 1, half), (half, half - 1)])
        for k in range(half - 1, 0, -1):
            got = along(x, [(k, k - 1), (Z - 1 - k, Z - k)])
            x = jnp.where((z == k - 1) | (z == Z - k), got, x)
        return x

    def z_sum(send, keep):
        if Z == 4:
            near = [(i, i ^ 1) for i in range(Z)]
            part = keep + along(send, near)
            own = part + along(part, [(i, Z - 1 - i) for i in range(Z)])
            far = along(own, near)
        else:
            own, far = line_sum(keep), line_sum(send)
        return own, far

    def both_cores(parts):
        return [*parts, core_swap(parts[0]), core_swap(parts[1])]

    def slots_out(x, other):
        out = []
        for k in range(S // 2):
            pairs = []
            for i in range(S):
                for j in range(Q):
                    half = ((j // 2 + 1) // 2) % 2 if Z == 4 else 0
                    m = (half ^ other) * (S // 2) + k
                    pairs.append((i * Q + j, (i ^ m) * Q + j))
            out.append(permute(x[:, k * hb : (k + 1) * hb], ("shard", "seq"), pairs))
        return out

    def cols(w, start, size):
        return lax.dynamic_slice_in_dim(w, start, size, axis=1)

    x_own = block_in[0]
    row = jnp.concatenate(
        [attn_gain, mlp_gain, (doc_lengths[0] // 64).astype(BF), (doc_lengths[0] % 64).astype(BF)]
    )
    docs = doc_lengths.shape[1]
    rows = jnp.pad(row[None], ((0, TAIL - 1), (0, 640 - row.shape[0])))
    x = gather(x_own)
    misc = gather(rows)

    qkv_half = lax.dynamic_slice_in_dim(qkv_weight, c * hb, hb, axis=0)
    qkv_pieces = [
        jnp.concatenate([cols(qkv_half, i * D + (s ^ m) * cw, cw) for i in range(3)], axis=1)
        for m in range(S)
    ]
    wm = swap_out(qkv_pieces)
    wo = [core_swap(w) for w in wm]

    in_half = lax.dynamic_slice_in_dim(in_weight, c * hb, hb, axis=0)
    out_half = lax.dynamic_slice_in_dim(out_weight, c * hb, hb, axis=0)
    in_pieces = [
        jnp.concatenate([cols(in_half, i * ff + (s ^ m) * fs, fs) for i in range(2)], axis=0)
        for m in range(S)
    ]
    tails = jnp.stack([p[0, 4 * hb : 4 * hb + 2 * docs] for p in misc]).astype(jnp.int32)
    lengths = tails[:, :docs] * 64 + tails[:, docs:]
    ends = jnp.cumsum(lengths, axis=1)
    key_spots = q * T - WINDOW + jnp.arange(T + 2 * WINDOW, dtype=jnp.int32)
    passed = ends[:, :, None] <= key_spots[None, None, :]
    key_segment = jnp.sum(passed.astype(jnp.int32), axis=1)
    start = jnp.sum(jnp.where(passed, lengths[:, :, None], 0), axis=1)
    position = (key_spots[None] - start)[:, WINDOW : WINDOW + T]
    segment = key_segment[:, WINDOW : WINDOW + T]
    spots = key_spots[WINDOW : WINDOW + T]
    near = jnp.abs(spots[:, None] - key_spots[None, :]) <= WINDOW
    valid = (key_spots >= 0) & (key_spots < Q * T)
    mask = (segment[:, :, None] == key_segment[:, None, :]) & (near & valid[None, :])[None]
    mask = mask.astype(F32).reshape(S * T, T + 2 * WINDOW)
    half = HEAD // 2
    freq = jnp.power(10000.0, -(jnp.arange(half).astype(F32) * (2.0 / HEAD)))
    angle = position.reshape(S * T, 1).astype(F32) * freq[None, :]
    cos_h, sin_h = jnp.cos(angle), jnp.sin(angle)
    cos = jnp.concatenate([cos_h] * 4, axis=1)
    sin = jnp.concatenate([-sin_h, sin_h] * 2, axis=1)

    in_pieces = after(in_pieces, cos, sin, mask)
    im = swap_out(in_pieces)
    om = gather(out_half)
    io = [core_swap(w) for w in im]
    oo = [core_swap(w) for w in om]

    h_attn, rq, kv, lead, last, wnat, gain_a, gain_m = call(
        functools.partial(qkv_kernel, S, T, hb),
        (
            sds((S * T, D), BF),
            sds((S * T, cw), BF),
            sds((S * T, 2 * cw), BF),
            sds((S, WINDOW, 2 * cw), BF),
            sds((S, WINDOW, 2 * cw), BF),
            sds((D, 3 * cw), BF),
            sds((1, D), F32),
            sds((1, D), F32),
        ),
        *x,
        *wm,
        *wo,
        *misc,
        cos,
        sin,
        scalars=sc,
    )
    before_kv, after_kv = shift(last, 1), shift(lead, -1)
    ext = pltpu.VMEM((T + 2 * WINDOW, 2 * cw), BF)
    att_own, total = call(
        functools.partial(attend_kernel, S, T),
        (sds((S * T, cw), BF), sds((S * T, cw // HEAD), F32)),
        rq,
        kv,
        before_kv,
        after_kv,
        mask,
        scratch=[ext],
    )
    att = gather(att_own)

    g_own = after(out_grad[0], att_own)
    og = gather(g_own)
    gate_w, lin_w = call(
        functools.partial(late_weights_kernel, S, hb),
        (sds((D, fs), BF), sds((D, fs), BF)),
        *im,
        *io,
        scalars=sc,
    )
    resid_own, h_mlp, gate_in, lin, outw = call(
        functools.partial(up_kernel, S, T, hb),
        (
            sds((T, D), F32),
            sds((S * T, D), BF),
            sds((S * T, fs), F32),
            sds((S * T, fs), F32),
            sds((D, D), BF),
        ),
        *x,
        *att,
        *om,
        *oo,
        gain_m,
        gate_w,
        lin_w,
        scalars=sc,
        scratch=[pltpu.VMEM((S * T, D), BF)],
    )
    wide = pltpu.VMEM((S * T, D), BF)
    mid = call(
        functools.partial(up_back_kernel, S, T),
        (sds((S * T, fs), BF),) * 3 + (sds((T, D), BF),) * S,
        *og,
        gate_in,
        lin,
        down_weight,
        gate_w,
        lin_w,
        scratch=[wide],
    )
    act, d_gate, d_lin = mid[:3]
    d_hmlp = swap_out(mid[3:])

    down_send, down_keep = call(
        functools.partial(down_grad_kernel, S, T),
        (sds((fs, D // 2), BF),) * 2,
        act,
        *og,
        scalars=sc,
        scratch=[wide],
    )
    down_z = call(
        lane_halves_kernel,
        (sds((fs, D // 4), BF),) * 2,
        down_keep,
        core_swap(down_send),
        scalars=sc,
    )
    down_sums = both_cores(z_sum(*down_z))

    in_send, in_keep = call(
        functools.partial(in_grad_kernel, S, hb),
        (sds((2 * fs, D // 2), BF),) * 2,
        h_mlp,
        d_gate,
        d_lin,
        scalars=sc,
        scratch=[pltpu.VMEM((fs, D), F32)],
    )
    in_z = call(
        lane_halves_kernel,
        (sds((2 * fs, D // 4), BF),) * 2,
        in_keep,
        core_swap(in_send),
        scalars=sc,
    )
    own, far = z_sum(*in_z)
    own, far = slots_out(own, 0), slots_out(far, 1)
    in_sums = own + far + [core_swap(p) for p in own] + [core_swap(p) for p in far]

    back = call(
        functools.partial(resid_back_kernel, S),
        (sds((T, D), F32), sds((T, D), BF), sds((1, D), F32)) + (sds((T, cw), BF),) * S,
        *d_hmlp,
        resid_own,
        gain_m,
        g_own,
        outw,
    )
    d_resid, d_resid_b, gain_m_g = back[:3]
    d_mix = swap_out(back[3:])

    out_parts = call(
        functools.partial(out_parts_kernel, S, T), (sds((T, D), BF),) * S, act, down_weight
    )
    out_parts = swap_out(out_parts)
    final = resid_own
    for p in out_parts:
        final = final + p.astype(F32)
    final = final.astype(BF)

    dq, dkv, to_left, to_right = call(
        functools.partial(attend_back_kernel, S, T),
        (
            sds((S * T, cw), BF),
            sds((S * T, 2 * cw), F32),
            sds((S, WINDOW, 2 * cw), BF),
            sds((S, WINDOW, 2 * cw), BF),
        ),
        rq,
        kv,
        before_kv,
        after_kv,
        mask,
        total,
        cos,
        sin,
        *d_mix,
        scratch=[ext, pltpu.VMEM((S * T, cw), BF)],
    )
    from_right, from_left = shift(to_left, -1), shift(to_right, 1)

    drb = gather(d_resid_b)
    out_send, out_keep = call(
        functools.partial(out_grad_kernel, S, T),
        (sds((D, hb), BF),) * 2,
        att_own,
        *drb,
        scalars=sc,
        scratch=[wide, pltpu.VMEM((D, cw), F32)],
    )
    out_z = call(
        row_halves_kernel, (sds((D // 2, hb), BF),) * 2, out_keep, core_swap(out_send), scalars=sc
    )
    out_sums = both_cores(z_sum(*out_z))

    res = call(
        functools.partial(qkv_back_kernel, S, T, hb),
        (sds((3 * cw + TAIL, D // 2), BF),) * 2 + (sds((T, D), BF),) * S,
        *x,
        dq,
        dkv,
        from_left,
        from_right,
        cos,
        sin,
        h_attn,
        wnat,
        gain_m_g,
        scalars=sc,
        scratch=[
            pltpu.VMEM((S * T, 3 * cw), BF),
            pltpu.VMEM((3 * cw, D), F32),
            pltpu.VMEM((2, D), F32),
        ],
    )
    qkv_g = call(
        functools.partial(pair_sum_kernel, S, hb),
        (sds((3 * cw + TAIL, hb), BF),) * S,
        res[1],
        core_swap(res[0]),
    )
    cut = 3 * cw // 2
    qkv_z = call(
        functools.partial(slot_halves_kernel, S),
        (sds((cut, D // 4), BF),) * 2 + (sds((cut + TAIL, D // 4), BF),) * 2,
        *swap_out(qkv_g),
        scalars=sc,
    )
    qkv_sums = both_cores(z_sum(*qkv_z[:2]))
    qkv_sums += both_cores(z_sum(*qkv_z[2:]))
    d_hattn = swap_out(res[2:])

    in_rows = call(
        functools.partial(in_back_kernel, S), sds((T, D), F32), *d_hattn, x_own, gain_a, d_resid
    )

    down_grad = call(down_final_kernel, sds((fs, D), F32), *down_sums, scalars=sc)
    in_grad = call(
        functools.partial(in_final_kernel, S, hb),
        sds((2 * hb, 2 * ff), F32),
        *in_sums,
        scalars=sc,
        scratch=[pltpu.VMEM((2 * S, 2 * fs, hb), BF)],
    )
    out_wgrad = call(
        functools.partial(out_final_kernel, hb), sds((2 * hb, D), F32), *out_sums, scalars=sc
    )
    qkv_grad, gain_a_grad, gain_m_grad = call(
        functools.partial(qkv_final_kernel, S, hb),
        (
            sds((2 * hb, 3 * D), F32),
            sds((1, 2 * hb), F32),
            sds((1, 2 * hb), F32),
        ),
        *qkv_sums,
        scalars=sc,
    )
    return (
        final[None],
        in_rows[None],
        qkv_grad,
        out_wgrad,
        in_grad,
        down_grad,
        gain_a_grad[0],
        gain_m_grad[0],
    )


def solution(mesh):
    rows = P("shard", "seq", None)
    mat = P("shard", None)
    vec = P("shard")

    return jax.shard_map(
        shards,
        mesh=mesh,
        in_specs=(rows, mat, mat, mat, mat, mat, vec, vec, rows),
        out_specs=(rows, rows, mat, mat, mat, mat, vec, vec),
        check_vma=False,
    )
```
